128 devices in a mesh: section: 8 (over x, z_hi), ctx: 16 (over z_lo, y, core).
Axes of the slice: x: 4, y: 4, z: 4 (z_hi: 2, z_lo: 2; z = z_hi * 2 + z_lo), core: 2. Of those that a mesh axis runs over, the one named last changes fastest.
Arguments:
- acts: bfloat16 [8, 2048, 12288], P('section', 'ctx'), may hold values from -6 to 6
- cots: bfloat16 [8, 2048, 4096], P('section', 'ctx'), may hold values from -1.1953125 to 1.1953125
- kern: float32 [8, 7, 12288], P('section'), may hold values from -2 to 2
- filt: bfloat16 [8, 4096, 2048], P('section', 'ctx'), may hold values from -9 to 9
- skip: float32 [8, 4096], P('section'), may hold values from 0.5 to 1.5
Outputs:
- output: bfloat16 [8, 2048, 4096], P('section', 'ctx')
- input_grad: bfloat16 [8, 2048, 12288], P('section', 'ctx')
- kern_grad: float32 [8, 7, 12288], P('section')
- filt_grad: float32 [8, 4096, 2048], P('section', 'ctx')
- skip_grad: float32 [8, 4096], P('section', 'ctx')
The draws below stay inside these ranges and needn't reach their ends.
All inputs are finite; a program needn't handle non-finite values.
Results may differ from the reference program's by a relative error of at most 0.023.
Values may be sent and summed in bfloat16 or wider, within the bound.
No kernel may reach another device: no remote copies, remote signals or barrier semaphores. Data moves between devices by JAX's collectives and lax.ppermute only.
A program may use at most 192 MiB of HBM per device.

```python
import math
import jax
import jax.numpy as jnp
from jax import lax

D = 4096
TAPS = 7
SECTIONS = 8
SEQ = 2048
FEATS = 12288


def draw_filt(key, part):
    key_rate = jax.random.fold_in(key, 11)
    key_noise = jax.random.fold_in(key, 12)
    lower, upper = (0.5, 50.0)
    rates = jnp.exp(jax.random.uniform(key_rate, (SECTIONS, D, 1), jnp.float32, math.log(lower), math.log(upper)))
    places = jnp.arange(SEQ, dtype=jnp.float32)[None, None, :] / SEQ
    envelope = jnp.sqrt(2.0 * rates / SEQ) * jnp.exp(-rates * places)
    noise = jnp.clip(jax.random.normal(key_noise, (SECTIONS, D, SEQ), jnp.float32), -4.0, 4.0)
    return (noise * envelope).astype(jnp.bfloat16)


def steps_of(stream_key, extent, pieces, smallest, largest):
    def one(position, blocks):
        heights = jax.random.uniform(jax.random.fold_in(jax.random.fold_in(stream_key, 6), position), (blocks,), jnp.float32, smallest / len(pieces), largest / len(pieces))
        return jnp.repeat(jnp.exp(heights), extent[position] // blocks).reshape((-1,) + (1,) * (len(extent) - position - 1))

    loudness = one(*pieces[0])
    for cut in pieces[1:]:
        loudness = loudness * one(*cut)
    return loudness


def bell_draw(rng, shape, width, bound, shards=(), held_as=jnp.bfloat16):
    loudness = steps_of(rng, shape, shards, -0.22, 0.18) if shards else 1.0
    array = jax.random.normal(rng, shape, jnp.float32) * width * loudness
    return jnp.minimum(jnp.maximum(array, -bound), bound).astype(held_as)


def setup_inputs(seed: int = 0) -> dict:
    arg_keys = jax.random.split(jax.random.key(seed), 6)
    return {
        "acts": bell_draw(arg_keys[0], (SECTIONS, SEQ, FEATS), 1.0, 6.0, ((0, 8), (1, 16))),
        "cots": bell_draw(arg_keys[1], (SECTIONS, SEQ, D), 0.2, 1.1953125, ((0, 8), (1, 16))),
        "kern": bell_draw(arg_keys[2], (SECTIONS, TAPS, FEATS), TAPS ** -0.5, 2.0, ((0, 8),), jnp.float32),
        "filt": draw_filt(jax.random.fold_in(arg_keys[5], 71), 0),
        "skip": jnp.clip(0.5 + 1.0 * jax.random.uniform(arg_keys[4], (SECTIONS, D), jnp.float32) ** steps_of(arg_keys[4], (SECTIONS, D), ((0, 8),), -0.2, 0.2), 0.5, 1.5),
    }


def causal_conv(signal, taps_f):
    length = signal.shape[0]
    spec = jnp.fft.rfft(signal, n=2 * length, axis=0) * jnp.fft.rfft(taps_f, n=2 * length, axis=0)
    return jnp.fft.irfft(spec, n=2 * length, axis=0)[:length]


def correlate(signal, taps_f):
    length = signal.shape[0]
    spec = jnp.fft.rfft(signal, n=2 * length, axis=0) * jnp.conj(jnp.fft.rfft(taps_f, n=2 * length, axis=0))
    return jnp.fft.irfft(spec, n=2 * length, axis=0)[:length]


def one_section(item):
    source, incoming, weights, filter_row, gain = item
    length = source.shape[0]
    margin = TAPS - 1
    padded = jnp.pad(source.astype(jnp.float32), ((margin, 0), (0, 0)))
    feature = sum(weights[offset][None, :] * padded[margin - offset:margin - offset + length] for offset in range(TAPS))
    query = feature[:, :D]
    keyed = feature[:, D:2 * D]
    value = feature[:, 2 * D:]
    gated = lax.optimization_barrier((keyed * value).astype(jnp.bfloat16)).astype(jnp.float32)
    taps_f = filter_row.astype(jnp.float32).T
    mixed = lax.optimization_barrier(causal_conv(gated, taps_f).astype(jnp.bfloat16)).astype(jnp.float32)
    inner = mixed + gain[None, :] * gated
    output = (query * inner).astype(jnp.bfloat16)
    grad_f = incoming.astype(jnp.float32)
    grad_mix = lax.optimization_barrier((grad_f * query).astype(jnp.bfloat16)).astype(jnp.float32)
    through = lax.optimization_barrier((correlate(grad_mix, taps_f) + gain[None, :] * grad_mix).astype(jnp.bfloat16)).astype(jnp.float32)
    filt_grad = correlate(grad_mix, gated).T
    skip_grad = jnp.sum(grad_mix * gated, axis=0)
    feat_grad = jnp.concatenate([grad_f * inner, through * value, through * keyed], axis=1)
    kern_grad = jnp.stack([jnp.sum(feat_grad * padded[margin - offset:margin - offset + length], axis=0) for offset in range(TAPS)])
    extended = jnp.pad(feat_grad, ((0, margin), (0, 0)))
    input_grad = sum(weights[offset][None, :] * extended[offset:offset + length] for offset in range(TAPS)).astype(jnp.bfloat16)
    return output, input_grad, kern_grad, filt_grad, skip_grad


def reference(acts, cots, kern, filt, skip):
    sources = jnp.roll(acts, 1, axis=0)
    incoming = jnp.roll(cots, -1, axis=0)
    output, input_grad, kern_grad, filt_grad, skip_grad = lax.map(one_section, (sources, incoming, kern, filt, skip))
    return (output, input_grad, kern_grad, filt_grad, skip_grad)
```

```python
import math

import jax
import jax.numpy as jnp
import ml_dtypes
import numpy as np
from jax import lax
from jax.experimental import pallas as pl
from jax.experimental.pallas import tpu as pltpu
from jax.sharding import PartitionSpec as P

TAPS = 7
HALO = 8
ROOT = math.sqrt(0.5)
F32 = jnp.float32
BF16 = jnp.bfloat16
MIB = 1 << 20


def passed_along(value, axis, steps):
    count = lax.axis_size(axis)
    pairs = [(source, (source + steps) % count) for source in range(count)]
    return lax.ppermute(value, axis, pairs)


def from_behind(block, axis, distance):
    devices = range(lax.axis_size(axis))
    route = [(i - distance, i) for i in devices if i - distance in devices]
    return lax.ppermute(block, axis, route)


def leaf_angles():
    angles = [math.pi / 2]
    for _ in range(3):
        angles = [half for angle in angles for half in (angle / 2, angle / 2 + math.pi)]
    return angles


def leaf_tables(length):
    leaf = length // 8
    order = np.arange(leaf)
    tables = []
    for angle in leaf_angles():
        phase = (angle + 2.0 * np.pi * order[:, None]) / leaf * order[None, :]
        real, imag = np.cos(phase), np.sin(phase)
        tables.append(np.block([[real, -imag], [imag, real]]))
    table = np.stack(tables)
    back = table.transpose(0, 2, 1) / length
    return table.astype(ml_dtypes.bfloat16), back.astype(ml_dtypes.bfloat16)


def turned(pair, angle):
    real, imag = pair
    cos, sin = math.cos(angle), math.sin(angle)
    return real * cos - imag * sin, real * sin + imag * cos


def split_rings(parts):
    low, high = [], []
    for lower, upper in zip(parts[:4], parts[4:]):
        scaled = upper * ROOT
        low.append((lower + scaled, scaled))
        high.append((lower - scaled, -scaled))
    rings = [(math.pi / 4, low), (math.pi / 4 + math.pi, high)]
    while len(rings[0][1]) > 1:
        finer = []
        for angle, pieces in rings:
            half = len(pieces) // 2
            plus, minus = [], []
            for lower, upper in zip(pieces[:half], pieces[half:]):
                real, imag = turned(upper, angle / 2)
                plus.append((lower[0] + real, lower[1] + imag))
                minus.append((lower[0] - real, lower[1] - imag))
            finer += [(angle / 2, plus), (angle / 2 + math.pi, minus)]
        rings = finer
    return [pieces[0] for _, pieces in rings]


def join_rings(leaves):
    angles = [math.pi / 4, math.pi / 4 + math.pi]
    angles = [half for angle in angles for half in (angle / 2, angle / 2 + math.pi)]
    groups = [[leaf] for leaf in leaves]
    while len(groups) > 2:
        merged = []
        for index in range(0, len(groups), 2):
            angle = angles[index // 2] if len(groups) == 8 else [math.pi / 4, math.pi / 4 + math.pi][index // 2]
            lower, upper = [], []
            for plus, minus in zip(groups[index], groups[index + 1]):
                lower.append((plus[0] + minus[0], plus[1] + minus[1]))
                upper.append(turned((plus[0] - minus[0], plus[1] - minus[1]), -angle / 2))
            merged.append(lower + upper)
        groups = merged
    lower, upper = [], []
    for plus, minus in zip(groups[0], groups[1]):
        lower.append(plus[0] + minus[0])
        upper.append(((plus[0] - minus[0]) + (plus[1] - minus[1])) * ROOT)
    return lower + upper


def filter_kernel(filt_ref, table_ref, spec_ref, rings):
    chans, length = filt_ref.shape
    leaf = length // 8
    step = pl.program_id(0)

    @pl.when(step == 0)
    def _():
        @pl.loop(0, chans // 16)
        def _(strip):
            rows = pl.ds(pl.multiple_of(strip * 16, 16), 16)
            for lane in range(0, leaf, 128):
                parts = [
                    filt_ref[rows, piece * leaf + lane : piece * leaf + lane + 128].astype(F32)
                    for piece in range(8)
                ]
                for index, (real, imag) in enumerate(split_rings(parts)):
                    rings[index, rows, lane : lane + 128] = real.astype(BF16)
                    rings[index, rows, leaf + lane : leaf + lane + 128] = imag.astype(BF16)

    spec_ref[0] = lax.dot_general(
        table_ref[0], rings[step], (((1,), (1,)), ((), ())), preferred_element_type=F32
    )


def filter_spectrum(filt, table):
    chans, length = filt.shape
    wide = length // 4
    return pl.pallas_call(
        filter_kernel,
        out_shape=jax.ShapeDtypeStruct((8, wide, chans), F32),
        grid=(8,),
        in_specs=[
            pl.BlockSpec((chans, length), lambda j: (0, 0)),
            pl.BlockSpec((1, wide, wide), lambda j: (j, 0, 0)),
        ],
        out_specs=pl.BlockSpec((1, wide, chans), lambda j: (j, 0, 0)),
        scratch_shapes=[pltpu.VMEM((8, chans, wide), BF16)],
        compiler_params=pltpu.CompilerParams(vmem_limit_bytes=24 * MIB),
        cost_estimate=pl.CostEstimate(
            flops=16 * wide * wide * chans, bytes_accessed=10 * MIB, transcendentals=0
        ),
        name="filter_spectrum",
    )(filt, table)


def tap_rows(kern_ref, lanes):
    return [kern_ref[tap : tap + 1, lanes] for tap in range(TAPS)]


def feature_rows(held, role, taps, start, count):
    total = taps[0] * held[role, pl.ds(start, count), :]
    for tap in range(1, TAPS):
        total = total + taps[tap] * held[role, pl.ds(start - tap, count), :]
    return total


def feature_kernel(*refs):
    sources, befores, kerns = refs[0:3], refs[3:6], refs[6:9]
    incoming_ref, moved_ref, feats_ref, held = refs[9:]
    rows, lanes_all = incoming_ref.shape
    for lane in range(0, lanes_all, 128):
        lanes = slice(lane, lane + 128)
        taps = []
        for role in range(3):
            held[role, 0:HALO, :] = befores[role][:, lanes].astype(F32)
            held[role, HALO : HALO + rows, :] = sources[role][:, lanes].astype(F32)
            taps.append(tap_rows(kerns[role], lanes))
        for row in range(0, rows, 16):
            span = slice(row, row + 16)
            query, keyed, value = [
                feature_rows(held, role, taps[role], HALO + row, 16) for role in range(3)
            ]
            feats_ref[0, span, lanes] = query
            feats_ref[1, span, lanes] = keyed
            feats_ref[2, span, lanes] = value
            moved_ref[0, 0, span, lanes] = (keyed * value).astype(BF16)
            moved_ref[0, 1, span, lanes] = (incoming_ref[span, lanes].astype(F32) * query).astype(BF16)


def featurize(source, before, incoming, weights, groups):
    rows, width = incoming.shape
    chans = width // groups

    def roles(height):
        return [
            pl.BlockSpec((height, chans), lambda d, role=role: (0, role * groups + d)) for role in range(3)
        ]

    return pl.pallas_call(
        feature_kernel,
        out_shape=(
            jax.ShapeDtypeStruct((groups, 2, rows, chans), BF16),
            jax.ShapeDtypeStruct((3, rows, width), F32),
        ),
        grid=(groups,),
        in_specs=roles(rows) + roles(HALO) + roles(TAPS) + [pl.BlockSpec((rows, chans), lambda d: (0, d))],
        out_specs=(
            pl.BlockSpec((1, 2, rows, chans), lambda d: (d, 0, 0, 0)),
            pl.BlockSpec((3, rows, chans), lambda d: (0, 0, d)),
        ),
        scratch_shapes=[pltpu.VMEM((3, HALO + rows, 128), F32)],
        compiler_params=pltpu.CompilerParams(vmem_limit_bytes=16 * MIB),
        cost_estimate=pl.CostEstimate(
            flops=45 * rows * width, bytes_accessed=24 * rows * width, transcendentals=0
        ),
        name="featurize",
    )(source, source, source, before, before, before, weights, weights, weights, incoming)


def long_kernel(
    moved_ref, spec_ref, table_ref, back_ref, gain_ref, sent_ref, filt_ref, skip_ref, rings, products, joined, turned_ref
):
    groups, _, rows, chans = moved_ref.shape
    leaf = groups * rows // 8
    per_piece = leaf // rows
    step = pl.program_id(0)

    @pl.when(step == 0)
    def _():
        @pl.loop(0, rows // 16)
        def _(strip):
            inside = pl.ds(pl.multiple_of(strip * 16, 16), 16)
            for part in range(per_piece):
                real_rows = pl.ds(pl.multiple_of(part * rows + strip * 16, 16), 16)
                imag_rows = pl.ds(pl.multiple_of(leaf + part * rows + strip * 16, 16), 16)
                for kind in range(2):
                    for lane in range(0, chans, 128):
                        lanes = slice(lane, lane + 128)
                        parts = [
                            moved_ref[piece * per_piece + part, kind, inside, lanes].astype(F32)
                            for piece in range(8)
                        ]
                        into = slice(kind * chans + lane, kind * chans + lane + 128)
                        for index, (real, imag) in enumerate(split_rings(parts)):
                            rings[index, real_rows, into] = real.astype(BF16)
                            rings[index, imag_rows, into] = imag.astype(BF16)

    both = jnp.dot(table_ref[0], rings[step], preferred_element_type=F32)
    g_real, g_imag = both[:leaf, :chans], both[leaf:, :chans]
    d_real, d_imag = both[:leaf, chans:], both[leaf:, chans:]
    f_real, f_imag = spec_ref[0, :leaf], spec_ref[0, leaf:]
    products[:leaf, 0:chans] = (g_real * f_real - g_imag * f_imag).astype(BF16)
    products[leaf:, 0:chans] = (g_real * f_imag + g_imag * f_real).astype(BF16)
    products[:leaf, chans : 2 * chans] = (d_real * f_real + d_imag * f_imag).astype(BF16)
    products[leaf:, chans : 2 * chans] = (d_imag * f_real - d_real * f_imag).astype(BF16)
    products[:leaf, 2 * chans :] = (d_real * g_real + d_imag * g_imag).astype(BF16)
    products[leaf:, 2 * chans :] = (d_imag * g_real - d_real * g_imag).astype(BF16)
    joined[step] = jnp.dot(back_ref[0], products[...], preferred_element_type=F32)

    @pl.when(step == 7)
    def _():
        skip_ref[...] = jnp.zeros_like(skip_ref)

        @pl.loop(0, rows // 16)
        def _(strip):
            inside = pl.ds(pl.multiple_of(strip * 16, 16), 16)
            for part in range(per_piece):
                real_rows = pl.ds(pl.multiple_of(part * rows + strip * 16, 16), 16)
                imag_rows = pl.ds(pl.multiple_of(leaf + part * rows + strip * 16, 16), 16)
                for lane in range(0, chans, 128):
                    lanes = slice(lane, lane + 128)
                    gain = gain_ref[0:1, lanes]
                    for kind in range(3):
                        column = slice(kind * chans + lane, kind * chans + lane + 128)
                        leaves = [
                            (joined[index, real_rows, column], joined[index, imag_rows, column])
                            for index in range(8)
                        ]
                        total = jnp.zeros((16, 128), F32)
                        for piece, result in enumerate(join_rings(leaves)):
                            owner = piece * per_piece + part
                            if kind == 0:
                                sent_ref[owner, 0, inside, lanes] = result.astype(BF16)
                            elif kind == 1:
                                grad = moved_ref[owner, 1, inside, lanes].astype(F32)
                                sent_ref[owner, 1, inside, lanes] = (result + gain * grad).astype(BF16)
                                total = total + grad * moved_ref[owner, 0, inside, lanes].astype(F32)
                            else:
                                into = pl.ds(pl.multiple_of(owner * rows + strip * 16, 16), 16)
                                turned_ref[into, lanes] = result
                        if kind == 1:
                            skip_ref[0:1, lanes] += jnp.sum(total, axis=0, keepdims=True)

        for piece in range(groups):
            span = slice(piece * rows, (piece + 1) * rows)
            filt_ref[:, span] = turned_ref[span, :].T
        for owner in range(groups - 1):
            sent_ref[owner, :, rows : rows + HALO, :] = sent_ref[owner + 1, :, 0:HALO, :]
        sent_ref[groups - 1, :, rows : rows + HALO, :] = jnp.zeros((2, HALO, chans), BF16)


def long_convolutions(moved, spectrum, table, back, gain):
    groups, _, rows, chans = moved.shape
    length = groups * rows
    wide = length // 4
    whole = pl.Buffered(1)
    return pl.pallas_call(
        long_kernel,
        out_shape=(
            jax.ShapeDtypeStruct((groups, 2, rows + HALO, chans), BF16),
            jax.ShapeDtypeStruct((chans, length), F32),
            jax.ShapeDtypeStruct((1, chans), F32),
        ),
        grid=(8,),
        in_specs=[
            pl.BlockSpec(moved.shape, lambda j: (0, 0, 0, 0), pipeline_mode=whole),
            pl.BlockSpec((1, wide, chans), lambda j: (j, 0, 0)),
            pl.BlockSpec((1, wide, wide), lambda j: (j, 0, 0)),
            pl.BlockSpec((1, wide, wide), lambda j: (j, 0, 0)),
            pl.BlockSpec((1, chans), lambda j: (0, 0)),
        ],
        out_specs=(
            pl.BlockSpec((groups, 2, rows + HALO, chans), lambda j: (0, 0, 0, 0), pipeline_mode=whole),
            pl.BlockSpec((chans, length), lambda j: (0, 0), pipeline_mode=whole),
            pl.BlockSpec((1, chans), lambda j: (0, 0)),
        ),
        scratch_shapes=[
            pltpu.VMEM((8, wide, 2 * chans), BF16),
            pltpu.VMEM((wide, 3 * chans), BF16),
            pltpu.VMEM((8, wide, 3 * chans), F32),
            pltpu.VMEM((length, chans), F32),
        ],
        compiler_params=pltpu.CompilerParams(vmem_limit_bytes=48 * MIB),
        cost_estimate=pl.CostEstimate(
            flops=80 * wide * wide * chans, bytes_accessed=20 * MIB, transcendentals=0
        ),
        name="long_convolutions",
    )(moved, spectrum, table, back, gain)


def gradient_kernel(*refs):
    sources, befores, afters, kerns = refs[0:3], refs[3:6], refs[6:9], refs[9:12]
    incoming_ref, later_ref, feats_ref, back_ref, gain_ref = refs[12:17]
    output_ref, partial_ref, grad_hbm = refs[17:20]
    held, grads, slots, sems = refs[20:]
    rows, chans = incoming_ref.shape
    width = grad_hbm.shape[1] // 3
    step = pl.program_id(0)
    slot = lax.rem(step, 2)

    def write_back(role, slot_at, step_at):
        start = pl.multiple_of(role * width + step_at * chans, 128)
        return pltpu.make_async_copy(
            slots.at[slot_at, role], grad_hbm.at[:, pl.ds(start, chans)], sems.at[slot_at, role]
        )

    @pl.when(step >= 2)
    def _():
        for role in range(3):
            write_back(role, slot, step - 2).wait()

    for lane in range(0, chans, 128):
        lanes = slice(lane, lane + 128)
        gain = gain_ref[0:1, lanes]
        taps = []
        for role in range(3):
            held[role, 0:HALO, :] = befores[role][:, lanes].astype(F32)
            held[role, HALO : HALO + rows, :] = sources[role][:, lanes].astype(F32)
            held[role, HALO + rows : HALO + rows + HALO, :] = afters[role][:, lanes].astype(F32)
            taps.append(tap_rows(kerns[role], lanes))

        def feature_grads(keyed, value, grad_in, mixed, through, span):
            gated = (keyed * value).astype(BF16).astype(F32)
            inner = mixed + gain * gated
            grads[0, span, :] = grad_in * inner
            grads[1, span, :] = through * value
            grads[2, span, :] = through * keyed
            return inner

        for row in range(0, rows, 16):
            span = slice(row, row + 16)
            inner = feature_grads(
                feats_ref[1, span, lanes],
                feats_ref[2, span, lanes],
                incoming_ref[span, lanes].astype(F32),
                back_ref[0, 0, span, lanes].astype(F32),
                back_ref[0, 1, span, lanes].astype(F32),
                span,
            )
            output_ref[span, lanes] = (feats_ref[0, span, lanes] * inner).astype(BF16)
        span = slice(rows, rows + HALO)
        feature_grads(
            feature_rows(held, 1, taps[1], HALO + rows, HALO),
            feature_rows(held, 2, taps[2], HALO + rows, HALO),
            later_ref[:, lanes].astype(F32),
            back_ref[0, 0, span, lanes].astype(F32),
            back_ref[0, 1, span, lanes].astype(F32),
            span,
        )
        for role in range(3):
            sums = [jnp.zeros((16, 128), F32) for _ in range(TAPS)]
            for row in range(0, rows, 16):
                here = grads[role, row : row + 16, :]
                total = taps[role][0] * here
                sums[0] = sums[0] + here * held[role, HALO + row : HALO + row + 16, :]
                for tap in range(1, TAPS):
                    total = total + taps[role][tap] * grads[role, row + tap : row + tap + 16, :]
                    sums[tap] = sums[tap] + here * held[role, HALO + row - tap : HALO + row - tap + 16, :]
                slots[slot, role, row : row + 16, lanes] = total.astype(BF16)
            rows_out = [jnp.sum(one, axis=0, keepdims=True) for one in sums]
            rows_out.append(jnp.zeros((1, 128), F32))
            partial_ref[0, role, :, lanes] = jnp.concatenate(rows_out, axis=0).astype(BF16)

    for role in range(3):
        write_back(role, slot, step).start()

    @pl.when(step == pl.num_programs(0) - 1)
    def _():
        for role in range(3):
            write_back(role, 1 - slot, step - 1).wait()
            write_back(role, slot, step).wait()


def gradients(source, before, after, weights, incoming, later, feats, back, gain):
    rows, width = incoming.shape
    groups = back.shape[0]
    chans = width // groups

    def roles(height):
        return [
            pl.BlockSpec((height, chans), lambda d, role=role: (0, role * groups + d)) for role in range(3)
        ]

    return pl.pallas_call(
        gradient_kernel,
        out_shape=(
            jax.ShapeDtypeStruct((rows, width), BF16),
            jax.ShapeDtypeStruct((groups, 3, HALO, chans), BF16),
            jax.ShapeDtypeStruct((rows, 3 * width), BF16),
        ),
        grid=(groups,),
        in_specs=roles(rows)
        + roles(HALO)
        + roles(HALO)
        + roles(TAPS)
        + [
            pl.BlockSpec((rows, chans), lambda d: (0, d)),
            pl.BlockSpec((HALO, chans), lambda d: (0, d)),
            pl.BlockSpec((3, rows, chans), lambda d: (0, 0, d)),
            pl.BlockSpec((1, 2, rows + HALO, chans), lambda d: (d, 0, 0, 0)),
            pl.BlockSpec((1, chans), lambda d: (0, d)),
        ],
        out_specs=(
            pl.BlockSpec((rows, chans), lambda d: (0, d)),
            pl.BlockSpec((1, 3, HALO, chans), lambda d: (d, 0, 0, 0)),
            pl.BlockSpec(memory_space=pl.ANY),
        ),
        scratch_shapes=[
            pltpu.VMEM((3, rows + 2 * HALO, 128), F32),
            pltpu.VMEM((3, rows + HALO, 128), F32),
            pltpu.VMEM((2, 3, rows, chans), BF16),
            pltpu.SemaphoreType.DMA((2, 3)),
        ],
        compiler_params=pltpu.CompilerParams(vmem_limit_bytes=16 * MIB),
        cost_estimate=pl.CostEstimate(
            flops=100 * rows * width, bytes_accessed=32 * rows * width, transcendentals=0
        ),
        name="featurizer_gradients",
    )(
        *[source] * 3,
        *[before] * 3,
        *[after] * 3,
        *[weights] * 3,
        incoming,
        later,
        feats,
        back,
        gain,
    )


def on_device(acts, cots, kern, filt, skip):
    source = passed_along(acts, "section", 1)[0]
    incoming = passed_along(cots, "section", -1)[0]
    rows, feats_all = source.shape
    groups = lax.axis_size("ctx")
    chans = filt.shape[1]
    weights = kern[0]
    before = from_behind(source[rows - HALO :], "ctx", 1)
    after = from_behind(source[:HALO], "ctx", -1)
    later = from_behind(incoming[:HALO], "ctx", -1)
    table, back = (jnp.asarray(one) for one in leaf_tables(rows * groups))
    spectrum = filter_spectrum(filt[0], table)
    gain = lax.dynamic_slice_in_dim(skip, lax.axis_index("ctx") * chans, chans, axis=1)

    moved, feats = featurize(source, before, incoming, weights, groups)
    moved = lax.all_to_all(moved, "ctx", split_axis=0, concat_axis=0, tiled=True)
    sent, filt_grad, skip_grad = long_convolutions(moved, spectrum, table, back, gain)
    sent = lax.all_to_all(sent, "ctx", split_axis=0, concat_axis=0, tiled=True)
    output, partial, input_grad = gradients(
        source, before, after, weights, incoming, later, feats, sent, skip
    )
    partial = lax.all_to_all(partial, "ctx", split_axis=0, concat_axis=0, tiled=True)
    summed = jnp.sum(partial.astype(F32), axis=0, keepdims=True).astype(BF16)
    everyone = jnp.broadcast_to(summed, partial.shape)
    everyone = lax.all_to_all(everyone, "ctx", split_axis=0, concat_axis=0, tiled=True)
    kern_grad = everyone[:, :, :TAPS].transpose(2, 1, 0, 3).reshape(TAPS, feats_all).astype(F32)
    return (output[None], input_grad[None], kern_grad[None], filt_grad[None], skip_grad)


def solution(mesh):
    return jax.shard_map(
        on_device,
        mesh=mesh,
        in_specs=(
            P("section", "ctx", None),
            P("section", "ctx", None),
            P("section", None, None),
            P("section", "ctx", None),
            P("section", None),
        ),
        out_specs=(
            P("section", "ctx", None),
            P("section", "ctx", None),
            P("section", None, None),
            P("section", "ctx", None),
            P("section", "ctx"),
        ),
        check_vma=False,
    )
```

```python
import functools
import math

import jax
import jax.numpy as jnp
import ml_dtypes
import numpy as np
from jax import lax
from jax.experimental import pallas as pl
from jax.experimental.pallas import tpu as pltpu
from jax.sharding import PartitionSpec as P

TAPS = 7
HALO = 8
ROOT = math.sqrt(0.5)
F32 = jnp.float32
BF16 = jnp.bfloat16
MIB = 1 << 20
CHUNKS = 2


def in_hbm(*arrays):
    return [pltpu.with_memory_space_constraint(array, pltpu.HBM) for array in arrays]


def passed_along(value, axis, steps):
    count = lax.axis_size(axis)
    pairs = [(source, (source + steps) % count) for source in range(count)]
    return lax.ppermute(value, axis, pairs)


def from_behind(block, axis, distance):
    devices = range(lax.axis_size(axis))
    route = [(i - distance, i) for i in devices if i - distance in devices]
    return lax.ppermute(block, axis, route)


def leaf_angles():
    angles = [math.pi / 2]
    for _ in range(3):
        angles = [half for angle in angles for half in (angle / 2, angle / 2 + math.pi)]
    return angles


def leaf_tables(length):
    leaf = length // 8
    order = np.arange(leaf)
    tables = []
    for angle in leaf_angles():
        phase = (angle + 2.0 * np.pi * order[:, None]) / leaf * order[None, :]
        real, imag = np.cos(phase), np.sin(phase)
        tables.append(np.block([[real, -imag], [imag, real]]))
    table = np.stack(tables)
    back = table.transpose(0, 2, 1) / length
    return table.astype(ml_dtypes.bfloat16), back.astype(ml_dtypes.bfloat16)


def turned(pair, angle):
    real, imag = pair
    cos, sin = math.cos(angle), math.sin(angle)
    return real * cos - imag * sin, real * sin + imag * cos


def split_rings(parts):
    low, high = [], []
    for lower, upper in zip(parts[:4], parts[4:]):
        scaled = upper * ROOT
        low.append((lower + scaled, scaled))
        high.append((lower - scaled, -scaled))
    rings = [(math.pi / 4, low), (math.pi / 4 + math.pi, high)]
    while len(rings[0][1]) > 1:
        finer = []
        for angle, pieces in rings:
            half = len(pieces) // 2
            plus, minus = [], []
            for lower, upper in zip(pieces[:half], pieces[half:]):
                real, imag = turned(upper, angle / 2)
                plus.append((lower[0] + real, lower[1] + imag))
                minus.append((lower[0] - real, lower[1] - imag))
            finer += [(angle / 2, plus), (angle / 2 + math.pi, minus)]
        rings = finer
    return [pieces[0] for _, pieces in rings]


def join_rings(leaves):
    angles = [math.pi / 4, math.pi / 4 + math.pi]
    angles = [half for angle in angles for half in (angle / 2, angle / 2 + math.pi)]
    groups = [[leaf] for leaf in leaves]
    while len(groups) > 2:
        merged = []
        for index in range(0, len(groups), 2):
            angle = angles[index // 2] if len(groups) == 8 else [math.pi / 4, math.pi / 4 + math.pi][index // 2]
            lower, upper = [], []
            for plus, minus in zip(groups[index], groups[index + 1]):
                lower.append((plus[0] + minus[0], plus[1] + minus[1]))
                upper.append(turned((plus[0] - minus[0], plus[1] - minus[1]), -angle / 2))
            merged.append(lower + upper)
        groups = merged
    lower, upper = [], []
    for plus, minus in zip(groups[0], groups[1]):
        lower.append(plus[0] + minus[0])
        upper.append(((plus[0] - minus[0]) + (plus[1] - minus[1])) * ROOT)
    return lower + upper


def filter_kernel(filt_ref, table_ref, spec_ref, rings):
    chans, length = filt_ref.shape
    leaf = length // 8
    step = pl.program_id(0)

    @pl.when(step == 0)
    def _():
        @pl.loop(0, chans // 16)
        def _(strip):
            rows = pl.ds(pl.multiple_of(strip * 16, 16), 16)
            for lane in range(0, leaf, 128):
                parts = [
                    filt_ref[rows, piece * leaf + lane : piece * leaf + lane + 128].astype(F32)
                    for piece in range(8)
                ]
                for index, (real, imag) in enumerate(split_rings(parts)):
                    rings[index, rows, lane : lane + 128] = real.astype(BF16)
                    rings[index, rows, leaf + lane : leaf + lane + 128] = imag.astype(BF16)

    spec_ref[0] = lax.dot_general(
        table_ref[0], rings[step], (((1,), (1,)), ((), ())), preferred_element_type=F32
    )


def filter_spectrum(filt, table):
    chans, length = filt.shape
    wide = length // 4
    return pl.pallas_call(
        filter_kernel,
        out_shape=pltpu.HBM((8, wide, chans), F32),
        grid=(8,),
        in_specs=[
            pl.BlockSpec((chans, length), lambda j: (0, 0)),
            pl.BlockSpec((1, wide, wide), lambda j: (j, 0, 0)),
        ],
        out_specs=pl.BlockSpec((1, wide, chans), lambda j: (j, 0, 0)),
        scratch_shapes=[pltpu.VMEM((8, chans, wide), BF16)],
        compiler_params=pltpu.CompilerParams(vmem_limit_bytes=12 * MIB),
        cost_estimate=pl.CostEstimate(
            flops=16 * wide * wide * chans, bytes_accessed=10 * MIB, transcendentals=0
        ),
        name="filter_spectrum",
    )(*in_hbm(filt, table))


def pick_kernel(chunk, wide_ref, wide_out, sems):
    lanes = wide_out.shape[1] // sems.shape[0]
    copies = [
        pltpu.make_async_copy(
            wide_ref.at[:, pl.ds((CHUNKS * piece + chunk) * lanes, lanes)],
            wide_out.at[:, pl.ds(piece * lanes, lanes)],
            sems.at[piece],
        )
        for piece in range(sems.shape[0])
    ]
    for copy in copies:
        copy.start()
    for copy in copies:
        copy.wait()


def pick_chunk(array, chunk, lanes):
    rows, width = array.shape
    pieces = width // CHUNKS // lanes
    return pl.pallas_call(
        functools.partial(pick_kernel, chunk),
        out_shape=pltpu.HBM((rows, width // CHUNKS), array.dtype),
        in_specs=[pl.BlockSpec(memory_space=pl.ANY)],
        out_specs=pl.BlockSpec(memory_space=pl.ANY),
        scratch_shapes=[pltpu.SemaphoreType.DMA((pieces,))],
        compiler_params=pltpu.CompilerParams(vmem_limit_bytes=2 * MIB),
        cost_estimate=pl.CostEstimate(
            flops=0, bytes_accessed=2 * rows * width, transcendentals=0
        ),
        name="pick_chunk",
    )(*in_hbm(array))


def tap_rows(kern_ref, lanes):
    return [kern_ref[tap : tap + 1, lanes] for tap in range(TAPS)]


def feature_rows(held, role, taps, start, count):
    total = taps[0] * held[role, pl.ds(start, count), :]
    for tap in range(1, TAPS):
        total = total + taps[tap] * held[role, pl.ds(start - tap, count), :]
    return total


def feature_kernel(*refs):
    sources, befores, kerns = refs[0:3], refs[3:6], refs[6:9]
    incoming_ref, moved_ref, feats_ref, held = refs[9:]
    rows, lanes_all = incoming_ref.shape
    for lane in range(0, lanes_all, 128):
        lanes = slice(lane, lane + 128)
        taps = []
        for role in range(3):
            held[role, 0:HALO, :] = befores[role][:, lanes].astype(F32)
            held[role, HALO : HALO + rows, :] = sources[role][:, lanes].astype(F32)
            taps.append(tap_rows(kerns[role], lanes))
        for row in range(0, rows, 16):
            span = slice(row, row + 16)
            query, keyed, value = [
                feature_rows(held, role, taps[role], HALO + row, 16) for role in range(3)
            ]
            feats_ref[0, span, lanes] = query
            feats_ref[1, span, lanes] = keyed
            feats_ref[2, span, lanes] = value
            moved_ref[0, 0, span, lanes] = (keyed * value).astype(BF16)
            moved_ref[0, 1, span, lanes] = (incoming_ref[span, lanes].astype(F32) * query).astype(BF16)


def featurize(source, before, incoming, weights, groups, chunk):
    rows, width = incoming.shape
    chans = width // groups

    def roles(height, step=1, first=0):
        return [
            pl.BlockSpec((height, chans), lambda d, role=role: (0, (role * groups + d) * step + first))
            for role in range(3)
        ]

    return pl.pallas_call(
        feature_kernel,
        out_shape=(
            pltpu.HBM((groups, 2, rows, chans), BF16),
            pltpu.HBM((3, rows, width), F32),
        ),
        grid=(groups,),
        in_specs=roles(rows) + roles(HALO) + roles(TAPS, CHUNKS, chunk) + [pl.BlockSpec((rows, chans), lambda d: (0, d))],
        out_specs=(
            pl.BlockSpec((1, 2, rows, chans), lambda d: (d, 0, 0, 0)),
            pl.BlockSpec((3, rows, chans), lambda d: (0, 0, d)),
        ),
        scratch_shapes=[pltpu.VMEM((3, HALO + rows, 128), F32)],
        compiler_params=pltpu.CompilerParams(vmem_limit_bytes=6 * MIB),
        cost_estimate=pl.CostEstimate(
            flops=45 * rows * width, bytes_accessed=24 * rows * width, transcendentals=0
        ),
        name="featurize",
    )(*[source] * 3, *[before] * 3, *in_hbm(*[weights] * 3), incoming)


def long_kernel(
    moved_ref, spec_ref, table_ref, back_ref, gain_ref, *refs
):
    sent_ref, filt_ref, skip_ref, rings, products, joined, turned_ref = refs[-7:]
    groups, _, rows, chans = moved_ref.shape
    leaf = groups * rows // 8
    per_piece = leaf // rows
    step = pl.program_id(0)

    @pl.when(step == 0)
    def _():
        @pl.loop(0, rows // 16)
        def _(strip):
            inside = pl.ds(pl.multiple_of(strip * 16, 16), 16)
            for part in range(per_piece):
                real_rows = pl.ds(pl.multiple_of(part * rows + strip * 16, 16), 16)
                imag_rows = pl.ds(pl.multiple_of(leaf + part * rows + strip * 16, 16), 16)
                for kind in range(2):
                    for lane in range(0, chans, 128):
                        lanes = slice(lane, lane + 128)
                        parts = [
                            moved_ref[piece * per_piece + part, kind, inside, lanes].astype(F32)
                            for piece in range(8)
                        ]
                        into = slice(kind * chans + lane, kind * chans + lane + 128)
                        for index, (real, imag) in enumerate(split_rings(parts)):
                            rings[index, real_rows, into] = real.astype(BF16)
                            rings[index, imag_rows, into] = imag.astype(BF16)

    both = jnp.dot(table_ref[0], rings[step], preferred_element_type=F32)
    g_real, g_imag = both[:leaf, :chans], both[leaf:, :chans]
    d_real, d_imag = both[:leaf, chans:], both[leaf:, chans:]
    f_real, f_imag = spec_ref[0, :leaf], spec_ref[0, leaf:]
    products[:leaf, 0:chans] = (g_real * f_real - g_imag * f_imag).astype(BF16)
    products[leaf:, 0:chans] = (g_real * f_imag + g_imag * f_real).astype(BF16)
    products[:leaf, chans : 2 * chans] = (d_real * f_real + d_imag * f_imag).astype(BF16)
    products[leaf:, chans : 2 * chans] = (d_imag * f_real - d_real * f_imag).astype(BF16)
    products[:leaf, 2 * chans :] = (d_real * g_real + d_imag * g_imag).astype(BF16)
    products[leaf:, 2 * chans :] = (d_imag * g_real - d_real * g_imag).astype(BF16)
    joined[step] = jnp.dot(back_ref[0], products[...], preferred_element_type=F32)

    @pl.when(step == 7)
    def _():
        skip_ref[...] = jnp.zeros_like(skip_ref)

        @pl.loop(0, rows // 16)
        def _(strip):
            inside = pl.ds(pl.multiple_of(strip * 16, 16), 16)
            for part in range(per_piece):
                real_rows = pl.ds(pl.multiple_of(part * rows + strip * 16, 16), 16)
                imag_rows = pl.ds(pl.multiple_of(leaf + part * rows + strip * 16, 16), 16)
                for lane in range(0, chans, 128):
                    lanes = slice(lane, lane + 128)
                    gain = gain_ref[0:1, lanes]
                    for kind in range(3):
                        column = slice(kind * chans + lane, kind * chans + lane + 128)
                        leaves = [
                            (joined[index, real_rows, column], joined[index, imag_rows, column])
                            for index in range(8)
                        ]
                        total = jnp.zeros((16, 128), F32)
                        for piece, result in enumerate(join_rings(leaves)):
                            owner = piece * per_piece + part
                            if kind == 0:
                                sent_ref[owner, 0, inside, lanes] = result.astype(BF16)
                            elif kind == 1:
                                grad = moved_ref[owner, 1, inside, lanes].astype(F32)
                                sent_ref[owner, 1, inside, lanes] = (result + gain * grad).astype(BF16)
                                total = total + grad * moved_ref[owner, 0, inside, lanes].astype(F32)
                            else:
                                into = pl.ds(pl.multiple_of(owner * rows + strip * 16, 16), 16)
                                turned_ref[into, lanes] = result
                        if kind == 1:
                            skip_ref[0:1, lanes] += jnp.sum(total, axis=0, keepdims=True)

        for piece in range(groups):
            span = slice(piece * rows, (piece + 1) * rows)
            filt_ref[:, span] = turned_ref[span, :].T
        for owner in range(groups - 1):
            sent_ref[owner, :, rows : rows + HALO, :] = sent_ref[owner + 1, :, 0:HALO, :]
        sent_ref[groups - 1, :, rows : rows + HALO, :] = jnp.zeros((2, HALO, chans), BF16)


def long_convolutions(moved, spectrum, table, back, gain, chunk, earlier):
    groups, _, rows, chans = moved.shape
    length = groups * rows
    wide = length // 4
    whole = pl.Buffered(1)
    return pl.pallas_call(
        long_kernel,
        input_output_aliases={5: 1} if earlier else {},
        out_shape=(
            pltpu.HBM((groups, 2, rows + HALO, chans), BF16),
            pltpu.HBM((CHUNKS * chans, length), F32),
            pltpu.HBM((1, chans), F32),
        ),
        grid=(8,),
        in_specs=[
            pl.BlockSpec(moved.shape, lambda j: (0, 0, 0, 0), pipeline_mode=whole),
            pl.BlockSpec((1, wide, chans), lambda j: (j, 0, chunk)),
            pl.BlockSpec((1, wide, wide), lambda j: (j, 0, 0)),
            pl.BlockSpec((1, wide, wide), lambda j: (j, 0, 0)),
            pl.BlockSpec((1, chans), lambda j: (0, chunk)),
        ]
        + [pl.BlockSpec(memory_space=pl.ANY)] * len(earlier),
        out_specs=(
            pl.BlockSpec((groups, 2, rows + HALO, chans), lambda j: (0, 0, 0, 0), pipeline_mode=whole),
            pl.BlockSpec((chans, length), lambda j: (chunk, 0), pipeline_mode=whole),
            pl.BlockSpec((1, chans), lambda j: (0, 0)),
        ),
        scratch_shapes=[
            pltpu.VMEM((8, wide, 2 * chans), BF16),
            pltpu.VMEM((wide, 3 * chans), BF16),
            pltpu.VMEM((8, wide, 3 * chans), F32),
            pltpu.VMEM((length, chans), F32),
        ],
        compiler_params=pltpu.CompilerParams(vmem_limit_bytes=20 * MIB),
        cost_estimate=pl.CostEstimate(
            flops=80 * wide * wide * chans, bytes_accessed=20 * MIB, transcendentals=0
        ),
        name="long_convolutions",
    )(moved, *in_hbm(spectrum, table, back, gain, *earlier))


def gradient_kernel(chunk, *refs):
    sources, befores, afters, kerns = refs[0:3], refs[3:6], refs[6:9], refs[9:12]
    incoming_ref, later_ref, feats_ref, back_ref, gain_ref = refs[12:17]
    output_ref, partial_ref, grad_hbm, held, grads, slots, sems = refs[-7:]
    rows, chans = incoming_ref.shape
    width = grad_hbm.shape[1] // 3
    step = pl.program_id(0)
    slot = lax.rem(step, 2)

    def write_back(role, slot_at, step_at):
        start = pl.multiple_of(role * width + (step_at * CHUNKS + chunk) * chans, 128)
        return pltpu.make_async_copy(
            slots.at[slot_at, role], grad_hbm.at[:, pl.ds(start, chans)], sems.at[slot_at, role]
        )

    @pl.when(step >= 2)
    def _():
        for role in range(3):
            write_back(role, slot, step - 2).wait()

    for lane in range(0, chans, 128):
        lanes = slice(lane, lane + 128)
        gain = gain_ref[0:1, lanes]
        taps = []
        for role in range(3):
            held[role, 0:HALO, :] = befores[role][:, lanes].astype(F32)
            held[role, HALO : HALO + rows, :] = sources[role][:, lanes].astype(F32)
            held[role, HALO + rows : HALO + rows + HALO, :] = afters[role][:, lanes].astype(F32)
            taps.append(tap_rows(kerns[role], lanes))

        def feature_grads(keyed, value, grad_in, mixed, through, span):
            gated = (keyed * value).astype(BF16).astype(F32)
            inner = mixed + gain * gated
            grads[0, span, :] = grad_in * inner
            grads[1, span, :] = through * value
            grads[2, span, :] = through * keyed
            return inner

        for row in range(0, rows, 16):
            span = slice(row, row + 16)
            inner = feature_grads(
                feats_ref[1, span, lanes],
                feats_ref[2, span, lanes],
                incoming_ref[span, lanes].astype(F32),
                back_ref[0, 0, span, lanes].astype(F32),
                back_ref[0, 1, span, lanes].astype(F32),
                span,
            )
            output_ref[span, lanes] = (feats_ref[0, span, lanes] * inner).astype(BF16)
        span = slice(rows, rows + HALO)
        feature_grads(
            feature_rows(held, 1, taps[1], HALO + rows, HALO),
            feature_rows(held, 2, taps[2], HALO + rows, HALO),
            later_ref[:, lanes].astype(F32),
            back_ref[0, 0, span, lanes].astype(F32),
            back_ref[0, 1, span, lanes].astype(F32),
            span,
        )
        for role in range(3):
            sums = [jnp.zeros((16, 128), F32) for _ in range(TAPS)]
            for row in range(0, rows, 16):
                here = grads[role, row : row + 16, :]
                total = taps[role][0] * here
                sums[0] = sums[0] + here * held[role, HALO + row : HALO + row + 16, :]
                for tap in range(1, TAPS):
                    total = total + taps[role][tap] * grads[role, row + tap : row + tap + 16, :]
                    sums[tap] = sums[tap] + here * held[role, HALO + row - tap : HALO + row - tap + 16, :]
                slots[slot, role, row : row + 16, lanes] = total.astype(BF16)
            rows_out = [jnp.sum(one, axis=0, keepdims=True) for one in sums]
            rows_out.append(jnp.zeros((1, 128), F32))
            partial_ref[0, role, :, lanes] = jnp.concatenate(rows_out, axis=0).astype(BF16)

    for role in range(3):
        write_back(role, slot, step).start()

    @pl.when(step == pl.num_programs(0) - 1)
    def _():
        for role in range(3):
            write_back(role, 1 - slot, step - 1).wait()
            write_back(role, slot, step).wait()


def gradients(source, before, after, weights, incoming, later, feats, back, gain, chunk, earlier):
    rows, width = incoming.shape
    groups = back.shape[0]
    chans = width // groups

    def roles(height, step=1, first=0):
        return [
            pl.BlockSpec((height, chans), lambda d, role=role: (0, (role * groups + d) * step + first))
            for role in range(3)
        ]

    return pl.pallas_call(
        functools.partial(gradient_kernel, chunk),
        input_output_aliases={17: 0, 18: 2} if earlier else {},
        out_shape=(
            pltpu.HBM((rows, CHUNKS * width), BF16),
            pltpu.HBM((groups, 3, HALO, chans), BF16),
            pltpu.HBM((rows, 3 * CHUNKS * width), BF16),
        ),
        grid=(groups,),
        in_specs=roles(rows)
        + roles(HALO)
        + roles(HALO)
        + roles(TAPS, CHUNKS, chunk)
        + [
            pl.BlockSpec((rows, chans), lambda d: (0, d)),
            pl.BlockSpec((HALO, chans), lambda d: (0, d)),
            pl.BlockSpec((3, rows, chans), lambda d: (0, 0, d)),
            pl.BlockSpec((1, 2, rows + HALO, chans), lambda d: (d, 0, 0, 0)),
            pl.BlockSpec((1, chans), lambda d: (0, d * CHUNKS + chunk)),
        ]
        + [pl.BlockSpec(memory_space=pl.ANY)] * len(earlier),
        out_specs=(
            pl.BlockSpec((rows, chans), lambda d: (0, d * CHUNKS + chunk)),
            pl.BlockSpec((1, 3, HALO, chans), lambda d: (d, 0, 0, 0)),
            pl.BlockSpec(memory_space=pl.ANY),
        ),
        scratch_shapes=[
            pltpu.VMEM((3, rows + 2 * HALO, 128), F32),
            pltpu.VMEM((3, rows + HALO, 128), F32),
            pltpu.VMEM((2, 3, rows, chans), BF16),
            pltpu.SemaphoreType.DMA((2, 3)),
        ],
        compiler_params=pltpu.CompilerParams(vmem_limit_bytes=8 * MIB),
        cost_estimate=pl.CostEstimate(
            flops=100 * rows * width, bytes_accessed=32 * rows * width, transcendentals=0
        ),
        name="featurizer_gradients",
    )(
        *[source] * 3,
        *[before] * 3,
        *[after] * 3,
        *in_hbm(*[weights] * 3),
        incoming,
        later,
        *in_hbm(feats),
        back,
        *in_hbm(gain, *earlier),
    )


def on_device(acts, cots, kern, filt, skip):
    rows, feats_all = acts.shape[1:]
    groups = lax.axis_size("ctx")
    chans = filt.shape[1]
    part = chans // CHUNKS
    weights = kern[0]
    table, back = (jnp.asarray(one) for one in leaf_tables(rows * groups))
    spectrum = filter_spectrum(filt[0], table)
    gain = lax.dynamic_slice_in_dim(skip, lax.axis_index("ctx") * chans, chans, axis=1)

    arrived = []
    for chunk in range(CHUNKS):
        leaving = pick_chunk(acts[0], chunk, part), pick_chunk(cots[0], chunk, part)
        if arrived:
            leaving, arrived[-1] = lax.optimization_barrier((leaving, arrived[-1]))
        arrived.append((passed_along(leaving[0], "section", 1), passed_along(leaving[1], "section", -1)))

    partials, skips, filters, results = [], [], (), ()
    for chunk, (source, incoming) in enumerate(arrived):
        before = from_behind(source[rows - HALO :], "ctx", 1)
        after = from_behind(source[:HALO], "ctx", -1)
        later = from_behind(incoming[:HALO], "ctx", -1)
        moved, feats = featurize(source, before, incoming, weights, groups, chunk)
        moved = lax.all_to_all(moved, "ctx", split_axis=0, concat_axis=0, tiled=True)
        sent, *filters, skip_grad = long_convolutions(moved, spectrum, table, back, gain, chunk, filters)
        sent = lax.all_to_all(sent, "ctx", split_axis=0, concat_axis=0, tiled=True)
        output, partial, input_grad = gradients(
            source, before, after, weights, incoming, later, feats, sent, skip, chunk, results
        )
        results = (output, input_grad)
        skips.append(skip_grad)
        partial = lax.all_to_all(partial, "ctx", split_axis=0, concat_axis=0, tiled=True)
        summed = jnp.sum(partial.astype(F32), axis=0, keepdims=True).astype(BF16)
        everyone = jnp.broadcast_to(summed, partial.shape)
        everyone = lax.all_to_all(everyone, "ctx", split_axis=0, concat_axis=0, tiled=True)
        partials.append(everyone[:, :, :TAPS].transpose(2, 1, 0, 3).astype(F32))
    kern_grad = jnp.stack(partials, axis=3).reshape(TAPS, feats_all)
    skip_grad = jnp.concatenate(skips, axis=1)
    return (results[0][None], results[1][None], kern_grad[None], filters[0][None], skip_grad)


def solution(mesh):
    return jax.shard_map(
        on_device,
        mesh=mesh,
        in_specs=(
            P("section", "ctx", None),
            P("section", "ctx", None),
            P("section", None, None),
            P("section", "ctx", None),
            P("section", None),
        ),
        out_specs=(
            P("section", "ctx", None),
            P("section", "ctx", None),
            P("section", None, None),
            P("section", "ctx", None),
            P("section", "ctx"),
        ),
        check_vma=False,
    )
```

```python
import math

import jax
import jax.numpy as jnp
import ml_dtypes
import numpy as np
from jax import lax
from jax.experimental import pallas as pl
from jax.experimental.pallas import tpu as pltpu
from jax.sharding import PartitionSpec as P

TAPS = 7
HALO = 8
EXTRA = 32
ROOT = math.sqrt(0.5)
F32 = jnp.float32
BF16 = jnp.bfloat16
MIB = 1 << 20


def in_hbm(*arrays):
    return [pltpu.with_memory_space_constraint(array, pltpu.HBM) for array in arrays]


def passed_along(value, axis, steps):
    count = lax.axis_size(axis)
    pairs = [(source, (source + steps) % count) for source in range(count)]
    return lax.ppermute(value, axis, pairs)


def handed_over(value, steps, partner):
    sections, groups = lax.axis_size("section"), lax.axis_size("ctx")
    pairs = [
        (section * groups + place, (section + steps) % sections * groups + (place ^ partner))
        for section in range(sections)
        for place in range(groups)
    ]
    return lax.ppermute(value, ("section", "ctx"), pairs)


def leaf_angles():
    angles = [math.pi / 2]
    for _ in range(3):
        angles = [half for angle in angles for half in (angle / 2, angle / 2 + math.pi)]
    return angles


def leaf_tables(length):
    leaf = length // 8
    order = np.arange(leaf)
    tables = []
    for angle in leaf_angles():
        phase = (angle + 2.0 * np.pi * order[:, None]) / leaf * order[None, :]
        real, imag = np.cos(phase), np.sin(phase)
        tables.append(np.block([[real, -imag], [imag, real]]))
    table = np.stack(tables)
    back = table.transpose(0, 2, 1) / length
    return table.astype(ml_dtypes.bfloat16), back.astype(ml_dtypes.bfloat16)


def turned(pair, angle):
    real, imag = pair
    cos, sin = math.cos(angle), math.sin(angle)
    return real * cos - imag * sin, real * sin + imag * cos


def split_rings(parts):
    low, high = [], []
    for lower, upper in zip(parts[:4], parts[4:]):
        scaled = upper * ROOT
        low.append((lower + scaled, scaled))
        high.append((lower - scaled, -scaled))
    rings = [(math.pi / 4, low), (math.pi / 4 + math.pi, high)]
    while len(rings[0][1]) > 1:
        finer = []
        for angle, pieces in rings:
            half = len(pieces) // 2
            plus, minus = [], []
            for lower, upper in zip(pieces[:half], pieces[half:]):
                real, imag = turned(upper, angle / 2)
                plus.append((lower[0] + real, lower[1] + imag))
                minus.append((lower[0] - real, lower[1] - imag))
            finer += [(angle / 2, plus), (angle / 2 + math.pi, minus)]
        rings = finer
    return [pieces[0] for _, pieces in rings]


def join_rings(leaves):
    angles = [math.pi / 4, math.pi / 4 + math.pi]
    angles = [half for angle in angles for half in (angle / 2, angle / 2 + math.pi)]
    groups = [[leaf] for leaf in leaves]
    while len(groups) > 2:
        merged = []
        for index in range(0, len(groups), 2):
            angle = angles[index // 2] if len(groups) == 8 else [math.pi / 4, math.pi / 4 + math.pi][index // 2]
            lower, upper = [], []
            for plus, minus in zip(groups[index], groups[index + 1]):
                lower.append((plus[0] + minus[0], plus[1] + minus[1]))
                upper.append(turned((plus[0] - minus[0], plus[1] - minus[1]), -angle / 2))
            merged.append(lower + upper)
        groups = merged
    lower, upper = [], []
    for plus, minus in zip(groups[0], groups[1]):
        lower.append(plus[0] + minus[0])
        upper.append(((plus[0] - minus[0]) + (plus[1] - minus[1])) * ROOT)
    return lower + upper


def filter_kernel(filt_ref, table_ref, spec_ref, rings):
    chans, length = filt_ref.shape
    leaf = length // 8
    step = pl.program_id(0)

    @pl.when(step == 0)
    def _():
        @pl.loop(0, chans // 16)
        def _(strip):
            rows = pl.ds(pl.multiple_of(strip * 16, 16), 16)
            for lane in range(0, leaf, 128):
                parts = [
                    filt_ref[rows, piece * leaf + lane : piece * leaf + lane + 128].astype(F32)
                    for piece in range(8)
                ]
                for index, (real, imag) in enumerate(split_rings(parts)):
                    rings[index, rows, lane : lane + 128] = real.astype(BF16)
                    rings[index, rows, leaf + lane : leaf + lane + 128] = imag.astype(BF16)

    spec_ref[0] = lax.dot_general(
        table_ref[0], rings[step], (((1,), (1,)), ((), ())), preferred_element_type=F32
    )


def filter_spectrum(filt, table):
    chans, length = filt.shape
    wide = length // 4
    return pl.pallas_call(
        filter_kernel,
        out_shape=pltpu.HBM((8, wide, chans), F32),
        grid=(8,),
        in_specs=[
            pl.BlockSpec((chans, length), lambda j: (0, 0)),
            pl.BlockSpec((1, wide, wide), lambda j: (j, 0, 0)),
        ],
        out_specs=pl.BlockSpec((1, wide, chans), lambda j: (j, 0, 0)),
        scratch_shapes=[pltpu.VMEM((8, chans, wide), BF16)],
        compiler_params=pltpu.CompilerParams(vmem_limit_bytes=12 * MIB),
        cost_estimate=pl.CostEstimate(
            flops=16 * wide * wide * chans, bytes_accessed=10 * MIB, transcendentals=0
        ),
        name="filter_spectrum",
    )(*in_hbm(filt, table))


def piece_kernel(me_ref, *refs):
    groups = len(refs) - 3
    step = pl.program_id(0)
    for partner in range(groups):

        @pl.when(step == partner)
        def _(partner=partner):
            for role in range(3):
                refs[3 + partner][role] = refs[role][...]


def pieces_for_owners(me, acts, groups):
    rows, feats_all = acts.shape
    chans = feats_all // 3 // groups
    return pl.pallas_call(
        piece_kernel,
        out_shape=[pltpu.HBM((3, rows, chans), BF16)] * groups,
        grid_spec=pltpu.PrefetchScalarGridSpec(
            num_scalar_prefetch=1,
            grid=(groups,),
            in_specs=[
                pl.BlockSpec((rows, chans), lambda k, me, role=role: (0, role * groups + (me[0] ^ k)))
                for role in range(3)
            ],
            out_specs=[pl.BlockSpec((3, rows, chans), lambda k, me: (0, 0, 0), pipeline_mode=pl.Buffered(1))] * groups,
        ),
        compiler_params=pltpu.CompilerParams(vmem_limit_bytes=8 * MIB),
        cost_estimate=pl.CostEstimate(
            flops=0, bytes_accessed=4 * rows * feats_all, transcendentals=0
        ),
        name="pieces_for_owners",
    )(me, *in_hbm(acts, acts, acts))


def split_kernel(wide_ref, pieces_ref):
    pieces_ref[0] = wide_ref[...]


def split_columns(array, groups):
    rows, width = array.shape
    return pl.pallas_call(
        split_kernel,
        out_shape=pltpu.HBM((groups, rows, width // groups), array.dtype),
        grid=(groups,),
        in_specs=[pl.BlockSpec((rows, width // groups), lambda d: (0, d))],
        out_specs=pl.BlockSpec((1, rows, width // groups), lambda d: (d, 0, 0)),
        compiler_params=pltpu.CompilerParams(vmem_limit_bytes=4 * MIB),
        cost_estimate=pl.CostEstimate(flops=0, bytes_accessed=4 * rows * width, transcendentals=0),
        name="split_columns",
    )(*in_hbm(array))


def fetch_pieces(me_ref, pieces, source, sems):
    for partner, piece in enumerate(pieces):
        block = me_ref[0] ^ partner
        pltpu.make_async_copy(piece, source.at[block], sems.at[block]).start()


def feature_kernel(me_ref, *refs):
    groups = len(refs) - 7
    pieces = refs[:groups]
    taps_ref, incoming_ref, moved_ref, feats_ref, source, held, sems = refs[groups:]
    _, rows, chans = incoming_ref.shape
    step = pl.program_id(0)

    @pl.when(step == 0)
    def _():
        fetch_pieces(me_ref, pieces, source, sems)
        held[:, :, rows:, :] = jnp.zeros((3, chans // 128, HALO, 128), F32)

    pltpu.make_async_copy(pieces[0], source.at[step], sems.at[step]).wait()
    for part in range(chans // 128):
        lanes = slice(part * 128, part * 128 + 128)
        taps = []
        for role in range(3):
            held[role, part, 0:HALO, :] = held[role, part, rows : rows + HALO, :]
            held[role, part, HALO:, :] = source[step, role, :, lanes].astype(F32)
            taps.append([taps_ref[role, tap : tap + 1, lanes] for tap in range(TAPS)])
        for row in range(0, rows, 16):
            span = slice(row, row + 16)
            features = []
            for role in range(3):
                total = taps[role][0] * held[role, part, HALO + row : HALO + row + 16, :]
                for tap in range(1, TAPS):
                    total = total + taps[role][tap] * held[role, part, HALO + row - tap : HALO + row - tap + 16, :]
                feats_ref[0, role, span, lanes] = total
                features.append(total)
            query, keyed, value = features
            moved_ref[0, 0, span, lanes] = (keyed * value).astype(BF16)
            moved_ref[0, 1, span, lanes] = (incoming_ref[0, span, lanes].astype(F32) * query).astype(BF16)


def featurize(me, pieces, taps, incoming):
    groups, rows, chans = incoming.shape
    return pl.pallas_call(
        feature_kernel,
        out_shape=(
            pltpu.HBM((groups, 2, rows, chans), BF16),
            pltpu.HBM((groups, 3, rows, chans), F32),
        ),
        grid=(groups,),
        in_specs=[pl.BlockSpec(memory_space=pltpu.SMEM)]
        + [pl.BlockSpec(memory_space=pl.ANY)] * groups
        + [
            pl.BlockSpec((3, HALO, chans), lambda p: (0, 0, 0)),
            pl.BlockSpec((1, rows, chans), lambda p: (p, 0, 0)),
        ],
        out_specs=(
            pl.BlockSpec((1, 2, rows, chans), lambda p: (p, 0, 0, 0)),
            pl.BlockSpec((1, 3, rows, chans), lambda p: (p, 0, 0, 0)),
        ),
        scratch_shapes=[
            pltpu.VMEM((groups, 3, rows, chans), BF16),
            pltpu.VMEM((3, chans // 128, HALO + rows, 128), F32),
            pltpu.SemaphoreType.DMA((groups,)),
        ],
        compiler_params=pltpu.CompilerParams(vmem_limit_bytes=12 * MIB),
        cost_estimate=pl.CostEstimate(
            flops=45 * groups * rows * chans, bytes_accessed=24 * groups * rows * chans, transcendentals=0
        ),
        name="featurize",
    )(me, *pieces, taps, incoming)


def long_kernel(
    moved_ref, spec_ref, table_ref, back_ref, gain_ref, sent_ref, filt_ref, skip_ref, rings, products, joined, turned_ref
):
    groups, _, rows, chans = moved_ref.shape
    leaf = groups * rows // 8
    per_piece = leaf // rows
    step = pl.program_id(0)

    @pl.when(step == 0)
    def _():
        @pl.loop(0, rows // 16)
        def _(strip):
            inside = pl.ds(pl.multiple_of(strip * 16, 16), 16)
            for part in range(per_piece):
                real_rows = pl.ds(pl.multiple_of(part * rows + strip * 16, 16), 16)
                imag_rows = pl.ds(pl.multiple_of(leaf + part * rows + strip * 16, 16), 16)
                for kind in range(2):
                    for lane in range(0, chans, 128):
                        lanes = slice(lane, lane + 128)
                        parts = [
                            moved_ref[piece * per_piece + part, kind, inside, lanes].astype(F32)
                            for piece in range(8)
                        ]
                        into = slice(kind * chans + lane, kind * chans + lane + 128)
                        for index, (real, imag) in enumerate(split_rings(parts)):
                            rings[index, real_rows, into] = real.astype(BF16)
                            rings[index, imag_rows, into] = imag.astype(BF16)

    both = jnp.dot(table_ref[0], rings[step], preferred_element_type=F32)
    g_real, g_imag = both[:leaf, :chans], both[leaf:, :chans]
    d_real, d_imag = both[:leaf, chans:], both[leaf:, chans:]
    f_real, f_imag = spec_ref[0, :leaf], spec_ref[0, leaf:]
    products[:leaf, 0:chans] = (g_real * f_real - g_imag * f_imag).astype(BF16)
    products[leaf:, 0:chans] = (g_real * f_imag + g_imag * f_real).astype(BF16)
    products[:leaf, chans : 2 * chans] = (d_real * f_real + d_imag * f_imag).astype(BF16)
    products[leaf:, chans : 2 * chans] = (d_imag * f_real - d_real * f_imag).astype(BF16)
    products[:leaf, 2 * chans :] = (d_real * g_real + d_imag * g_imag).astype(BF16)
    products[leaf:, 2 * chans :] = (d_imag * g_real - d_real * g_imag).astype(BF16)
    joined[step] = jnp.dot(back_ref[0], products[...], preferred_element_type=F32)

    @pl.when(step == 7)
    def _():
        skip_ref[...] = jnp.zeros_like(skip_ref)

        @pl.loop(0, rows // 16)
        def _(strip):
            inside = pl.ds(pl.multiple_of(strip * 16, 16), 16)
            for part in range(per_piece):
                real_rows = pl.ds(pl.multiple_of(part * rows + strip * 16, 16), 16)
                imag_rows = pl.ds(pl.multiple_of(leaf + part * rows + strip * 16, 16), 16)
                for lane in range(0, chans, 128):
                    lanes = slice(lane, lane + 128)
                    gain = gain_ref[0:1, lanes]
                    for kind in range(3):
                        column = slice(kind * chans + lane, kind * chans + lane + 128)
                        leaves = [
                            (joined[index, real_rows, column], joined[index, imag_rows, column])
                            for index in range(8)
                        ]
                        total = jnp.zeros((16, 128), F32)
                        for piece, result in enumerate(join_rings(leaves)):
                            owner = piece * per_piece + part
                            if kind == 0:
                                sent_ref[owner, 0, inside, lanes] = result.astype(BF16)
                            elif kind == 1:
                                grad = moved_ref[owner, 1, inside, lanes].astype(F32)
                                sent_ref[owner, 1, inside, lanes] = (result + gain * grad).astype(BF16)
                                total = total + grad * moved_ref[owner, 0, inside, lanes].astype(F32)
                            else:
                                into = pl.ds(pl.multiple_of(owner * rows + strip * 16, 16), 16)
                                turned_ref[into, lanes] = result
                        if kind == 1:
                            skip_ref[0:1, lanes] += jnp.sum(total, axis=0, keepdims=True)

        for piece in range(groups):
            span = slice(piece * rows, (piece + 1) * rows)
            filt_ref[:, span] = turned_ref[span, :].T


def long_convolutions(moved, spectrum, table, back, gain):
    groups, _, rows, chans = moved.shape
    length = groups * rows
    wide = length // 4
    whole = pl.Buffered(1)
    return pl.pallas_call(
        long_kernel,
        out_shape=(
            pltpu.HBM((groups, 2, rows, chans), BF16),
            pltpu.HBM((chans, length), F32),
            pltpu.HBM((1, chans), F32),
        ),
        grid=(8,),
        in_specs=[
            pl.BlockSpec(moved.shape, lambda j: (0, 0, 0, 0), pipeline_mode=whole),
            pl.BlockSpec((1, wide, chans), lambda j: (j, 0, 0)),
            pl.BlockSpec((1, wide, wide), lambda j: (j, 0, 0)),
            pl.BlockSpec((1, wide, wide), lambda j: (j, 0, 0)),
            pl.BlockSpec((1, chans), lambda j: (0, 0)),
        ],
        out_specs=(
            pl.BlockSpec((groups, 2, rows, chans), lambda j: (0, 0, 0, 0), pipeline_mode=whole),
            pl.BlockSpec((chans, length), lambda j: (0, 0), pipeline_mode=whole),
            pl.BlockSpec((1, chans), lambda j: (0, 0)),
        ),
        scratch_shapes=[
            pltpu.VMEM((8, wide, 2 * chans), BF16),
            pltpu.VMEM((wide, 3 * chans), BF16),
            pltpu.VMEM((8, wide, 3 * chans), F32),
            pltpu.VMEM((length, chans), F32),
        ],
        compiler_params=pltpu.CompilerParams(vmem_limit_bytes=38 * MIB),
        cost_estimate=pl.CostEstimate(
            flops=80 * wide * wide * chans, bytes_accessed=20 * MIB, transcendentals=0
        ),
        name="long_convolutions",
    )(*in_hbm(moved, spectrum, table, back, gain))


def gradient_kernel(me_ref, *refs):
    groups = len(refs) - 14
    pieces = refs[:groups]
    taps_ref, incoming_ref, feats_ref, back_ref, gain_ref, ready_hbm = refs[groups : groups + 6]
    source, grads, sums, slots, last, sems, slot_sems, last_sems = refs[groups + 6 :]
    _, rows, chans = incoming_ref.shape
    step = pl.program_id(0)
    block = groups - 1 - step
    slot = lax.rem(step, 2)

    def write_back(slot_at, block_at):
        return pltpu.make_async_copy(
            slots.at[slot_at], ready_hbm.at[block_at, pl.ds(0, 4 * rows)], slot_sems.at[slot_at]
        )

    @pl.when(step == 0)
    def _():
        fetch_pieces(me_ref, pieces, source, sems)
        grads[:, :, 0:HALO, :] = jnp.zeros((3, chans // 128, HALO, 128), F32)
        sums[...] = jnp.zeros_like(sums)

    @pl.when(step >= 2)
    def _():
        write_back(slot, block + 2).wait()

    pltpu.make_async_copy(pieces[0], source.at[block], sems.at[block]).wait()
    for part in range(chans // 128):
        lanes = slice(part * 128, part * 128 + 128)
        gain = gain_ref[0:1, lanes]
        for role in range(3):
            grads[role, part, rows : rows + HALO, :] = grads[role, part, 0:HALO, :]
        for row in range(0, rows, 16):
            span = slice(row, row + 16)
            query, keyed, value = [feats_ref[0, role, span, lanes] for role in range(3)]
            gated = (keyed * value).astype(BF16).astype(F32)
            inner = back_ref[0, 0, span, lanes].astype(F32) + gain * gated
            through = back_ref[0, 1, span, lanes].astype(F32)
            grads[0, part, span, :] = incoming_ref[0, span, lanes].astype(F32) * inner
            grads[1, part, span, :] = through * value
            grads[2, part, span, :] = through * keyed
            slots[slot, span, lanes] = (query * inner).astype(BF16)
        for role in range(3):
            taps = [taps_ref[role, tap : tap + 1, lanes] for tap in range(TAPS)]
            parts = [jnp.zeros((16, 128), F32) for _ in range(TAPS)]
            for row in range(0, rows, 16):
                here = source[block, role, row : row + 16, lanes].astype(F32)
                total = jnp.zeros((16, 128), F32)
                for tap in range(TAPS):
                    ahead = grads[role, part, row + tap : row + tap + 16, :]
                    total = total + taps[tap] * ahead
                    parts[tap] = parts[tap] + here * ahead
                start = (1 + role) * rows + row
                slots[slot, start : start + 16, lanes] = total.astype(BF16)
            for tap in range(TAPS):
                sums[role, tap, :, lanes] += parts[tap][0:8] + parts[tap][8:16]

    write_back(slot, block).start()

    @pl.when(step == groups - 1)
    def _():
        rows_out = []
        for role in range(3):
            for tap in range(TAPS):
                rows_out.append(jnp.sum(sums[role, tap], axis=0, keepdims=True))
            rows_out.append(jnp.zeros((HALO - TAPS, chans), F32))
        rows_out.append(jnp.zeros((EXTRA - 3 * HALO, chans), F32))
        last[...] = jnp.concatenate(rows_out, axis=0).astype(BF16)
        copies = [
            pltpu.make_async_copy(last, ready_hbm.at[owner, pl.ds(4 * rows, EXTRA)], last_sems.at[owner])
            for owner in range(groups)
        ]
        for copy in copies:
            copy.start()
        write_back(1 - slot, block + 1).wait()
        write_back(slot, block).wait()
        for copy in copies:
            copy.wait()


def gradients(me, pieces, taps, incoming, feats, back, gain):
    groups, rows, chans = incoming.shape
    last = groups - 1
    return pl.pallas_call(
        gradient_kernel,
        out_shape=pltpu.HBM((groups, 4 * rows + EXTRA, chans), BF16),
        grid=(groups,),
        in_specs=[pl.BlockSpec(memory_space=pltpu.SMEM)]
        + [pl.BlockSpec(memory_space=pl.ANY)] * groups
        + [
            pl.BlockSpec((3, HALO, chans), lambda p: (0, 0, 0)),
            pl.BlockSpec((1, rows, chans), lambda p: (last - p, 0, 0)),
            pl.BlockSpec((1, 3, rows, chans), lambda p: (last - p, 0, 0, 0)),
            pl.BlockSpec((1, 2, rows, chans), lambda p: (last - p, 0, 0, 0)),
            pl.BlockSpec((1, chans), lambda p: (0, 0)),
        ],
        out_specs=pl.BlockSpec(memory_space=pl.ANY),
        scratch_shapes=[
            pltpu.VMEM((groups, 3, rows, chans), BF16),
            pltpu.VMEM((3, chans // 128, rows + HALO, 128), F32),
            pltpu.VMEM((3, TAPS, 8, chans), F32),
            pltpu.VMEM((2, 4 * rows, chans), BF16),
            pltpu.VMEM((EXTRA, chans), BF16),
            pltpu.SemaphoreType.DMA((groups,)),
            pltpu.SemaphoreType.DMA((2,)),
            pltpu.SemaphoreType.DMA((groups,)),
        ],
        compiler_params=pltpu.CompilerParams(vmem_limit_bytes=12 * MIB),
        cost_estimate=pl.CostEstimate(
            flops=100 * groups * rows * chans, bytes_accessed=32 * groups * rows * chans, transcendentals=0
        ),
        name="featurizer_gradients",
    )(me, *pieces, taps, incoming, *in_hbm(feats, back, gain))


def place_kernel(held_ref, output_ref, grad_ref):
    step = pl.program_id(0)
    chans = held_ref.shape[2]

    def place(into):
        for owner in range(held_ref.shape[0]):
            into[:, owner * chans : (owner + 1) * chans] = held_ref[owner]

    @pl.when(step < 4)
    def _():
        place(output_ref)

    @pl.when(step >= 4)
    def _():
        place(grad_ref)


def place_columns(held, rows):
    groups, _, chans = held.shape
    some = groups // 4
    return pl.pallas_call(
        place_kernel,
        out_shape=(
            pltpu.HBM((rows, groups * chans), BF16),
            pltpu.HBM((rows, 3 * groups * chans), BF16),
        ),
        grid=(16,),
        in_specs=[pl.BlockSpec((some, rows, chans), lambda i: (lax.rem(i, 4), lax.div(i, 4), 0))],
        out_specs=(
            pl.BlockSpec((rows, some * chans), lambda i: (0, jnp.minimum(i, 3))),
            pl.BlockSpec((rows, some * chans), lambda i: (0, jnp.maximum(i - 4, 0))),
        ),
        compiler_params=pltpu.CompilerParams(vmem_limit_bytes=4 * MIB),
        cost_estimate=pl.CostEstimate(
            flops=0, bytes_accessed=16 * groups * rows * chans, transcendentals=0
        ),
        name="place_columns",
    )(*in_hbm(held))


def on_device(acts, cots, kern, filt, skip):
    rows, feats_all = acts.shape[1:]
    groups = lax.axis_size("ctx")
    chans = filt.shape[1]
    place = lax.axis_index("ctx").astype(jnp.int32)
    me = place[None]

    pieces = pieces_for_owners(me, acts[0], groups)
    incoming, pieces = lax.optimization_barrier((split_columns(cots[0], groups), pieces))
    incoming = passed_along(incoming, "section", -1)
    pieces = [handed_over(piece, 1, partner) for partner, piece in enumerate(pieces)]
    half = groups // 2
    incoming, pieces[:half] = lax.optimization_barrier((incoming, pieces[:half]))
    incoming = lax.all_to_all(incoming, "ctx", split_axis=0, concat_axis=0, tiled=True)

    table, back = (jnp.asarray(one) for one in leaf_tables(rows * groups))
    spectrum = filter_spectrum(filt[0], table)
    gain = lax.dynamic_slice_in_dim(skip, place * chans, chans, axis=1)
    taps = kern[0].reshape(TAPS, 3, groups, chans)
    taps = lax.dynamic_index_in_dim(taps, place, axis=2, keepdims=False).transpose(1, 0, 2)
    taps = jnp.pad(taps, ((0, 0), (0, HALO - TAPS), (0, 0)))

    moved, feats = featurize(me, pieces, taps, incoming)
    sent, filt_grad, skip_grad = long_convolutions(moved, spectrum, table, back, gain)
    ready = gradients(me, pieces, taps, incoming, feats, sent, gain)
    ready = lax.all_to_all(ready, "ctx", split_axis=0, concat_axis=0, tiled=True)
    output, input_grad = place_columns(ready, rows)
    sums = ready[:, 4 * rows : 4 * rows + 3 * HALO].reshape(groups, 3, HALO, chans)[:, :, :TAPS]
    kern_grad = sums.transpose(2, 1, 0, 3).reshape(TAPS, feats_all).astype(F32)
    return (output[None], input_grad[None], kern_grad[None], filt_grad[None], skip_grad)


def solution(mesh):
    return jax.shard_map(
        on_device,
        mesh=mesh,
        in_specs=(
            P("section", "ctx", None),
            P("section", "ctx", None),
            P("section", None, None),
            P("section", "ctx", None),
            P("section", None),
        ),
        out_specs=(
            P("section", "ctx", None),
            P("section", "ctx", None),
            P("section", None, None),
            P("section", "ctx", None),
            P("section", "ctx"),
        ),
        check_vma=False,
    )
```

```python
import functools
import math

import jax
import jax.numpy as jnp
import ml_dtypes
import numpy as np
from jax import lax
from jax.experimental import pallas as pl
from jax.experimental.pallas import tpu as pltpu
from jax.sharding import PartitionSpec as P

TAPS = 7
HALO = 8
EXTRA = 32
CHUNKS = 2
OWNER_MIB = 34
GATE = 4
ROOT = math.sqrt(0.5)
F32 = jnp.float32
BF16 = jnp.bfloat16
MIB = 1 << 20


def in_hbm(*arrays):
    return [pltpu.with_memory_space_constraint(array, pltpu.HBM) for array in arrays]


def passed_along(value, axis, steps):
    count = lax.axis_size(axis)
    pairs = [(source, (source + steps) % count) for source in range(count)]
    return lax.ppermute(value, axis, pairs)


def handed_over(value, steps, partner):
    sections, groups = lax.axis_size("section"), lax.axis_size("ctx")
    pairs = [
        (section * groups + place, (section + steps) % sections * groups + (place ^ partner))
        for section in range(sections)
        for place in range(groups)
    ]
    return lax.ppermute(value, ("section", "ctx"), pairs)


def leaf_angles():
    angles = [math.pi / 2]
    for _ in range(3):
        angles = [half for angle in angles for half in (angle / 2, angle / 2 + math.pi)]
    return angles


def leaf_tables(length):
    leaf = length // 8
    order = np.arange(leaf)
    tables = []
    for angle in leaf_angles():
        phase = (angle + 2.0 * np.pi * order[:, None]) / leaf * order[None, :]
        real, imag = np.cos(phase), np.sin(phase)
        tables.append(np.block([[real, -imag], [imag, real]]))
    table = np.stack(tables)
    back = table.transpose(0, 2, 1) / length
    return table.astype(ml_dtypes.bfloat16), back.astype(ml_dtypes.bfloat16)


def turned(pair, angle):
    real, imag = pair
    cos, sin = math.cos(angle), math.sin(angle)
    return real * cos - imag * sin, real * sin + imag * cos


def split_rings(parts):
    low, high = [], []
    for lower, upper in zip(parts[:4], parts[4:]):
        scaled = upper * ROOT
        low.append((lower + scaled, scaled))
        high.append((lower - scaled, -scaled))
    rings = [(math.pi / 4, low), (math.pi / 4 + math.pi, high)]
    while len(rings[0][1]) > 1:
        finer = []
        for angle, pieces in rings:
            half = len(pieces) // 2
            plus, minus = [], []
            for lower, upper in zip(pieces[:half], pieces[half:]):
                real, imag = turned(upper, angle / 2)
                plus.append((lower[0] + real, lower[1] + imag))
                minus.append((lower[0] - real, lower[1] - imag))
            finer += [(angle / 2, plus), (angle / 2 + math.pi, minus)]
        rings = finer
    return [pieces[0] for _, pieces in rings]


def join_rings(leaves):
    angles = [math.pi / 4, math.pi / 4 + math.pi]
    angles = [half for angle in angles for half in (angle / 2, angle / 2 + math.pi)]
    groups = [[leaf] for leaf in leaves]
    while len(groups) > 2:
        merged = []
        for index in range(0, len(groups), 2):
            angle = angles[index // 2] if len(groups) == 8 else [math.pi / 4, math.pi / 4 + math.pi][index // 2]
            lower, upper = [], []
            for plus, minus in zip(groups[index], groups[index + 1]):
                lower.append((plus[0] + minus[0], plus[1] + minus[1]))
                upper.append(turned((plus[0] - minus[0], plus[1] - minus[1]), -angle / 2))
            merged.append(lower + upper)
        groups = merged
    lower, upper = [], []
    for plus, minus in zip(groups[0], groups[1]):
        lower.append(plus[0] + minus[0])
        upper.append(((plus[0] - minus[0]) + (plus[1] - minus[1])) * ROOT)
    return lower + upper


def filter_kernel(filt_ref, table_ref, spec_ref, rings):
    chans, length = filt_ref.shape
    leaf = length // 8
    step = pl.program_id(0)

    @pl.when(step == 0)
    def _():
        @pl.loop(0, chans // 16)
        def _(strip):
            rows = pl.ds(pl.multiple_of(strip * 16, 16), 16)
            for lane in range(0, leaf, 128):
                parts = [
                    filt_ref[rows, piece * leaf + lane : piece * leaf + lane + 128].astype(F32)
                    for piece in range(8)
                ]
                for index, (real, imag) in enumerate(split_rings(parts)):
                    rings[index, rows, lane : lane + 128] = real.astype(BF16)
                    rings[index, rows, leaf + lane : leaf + lane + 128] = imag.astype(BF16)

    spec_ref[0] = lax.dot_general(
        table_ref[0], rings[step], (((1,), (1,)), ((), ())), preferred_element_type=F32
    )


def filter_spectrum(filt, table):
    chans, length = filt.shape
    wide = length // 4
    return pl.pallas_call(
        filter_kernel,
        out_shape=pltpu.HBM((8, wide, chans), F32),
        grid=(8,),
        in_specs=[
            pl.BlockSpec((chans, length), lambda j: (0, 0)),
            pl.BlockSpec((1, wide, wide), lambda j: (j, 0, 0)),
        ],
        out_specs=pl.BlockSpec((1, wide, chans), lambda j: (j, 0, 0)),
        scratch_shapes=[pltpu.VMEM((8, chans, wide), BF16)],
        compiler_params=pltpu.CompilerParams(vmem_limit_bytes=12 * MIB),
        cost_estimate=pl.CostEstimate(
            flops=16 * wide * wide * chans, bytes_accessed=10 * MIB, transcendentals=0
        ),
        name="filter_spectrum",
    )(*in_hbm(filt, table))


def wait_all(copies):
    for copy in copies:
        copy.start()
    for copy in copies:
        copy.wait()


def leave_kernel(me_ref, wide_ref, leaving_ref, sems):
    chips, roles, _, chans = leaving_ref.shape
    width = wide_ref.shape[1] // roles
    copies = []
    for chip in range(chips):
        start = (me_ref[0] ^ (2 * chip + 1)) * chans
        for role in range(roles):
            columns = pl.ds(pl.multiple_of(role * width + start, 128), chans)
            copies.append(
                pltpu.make_async_copy(wide_ref.at[:, columns], leaving_ref.at[chip, role], sems.at[chip, role])
            )
    wait_all(copies)


def piece_kernel(me_ref, wide_ref, came_ref, *refs):
    *pieces, sems = refs
    _, roles, _, chans = pieces[0].shape
    width = wide_ref.shape[1] // roles
    copies = []
    for chip, piece in enumerate(pieces):
        start = (me_ref[0] ^ (2 * chip)) * chans
        for role in range(roles):
            columns = pl.ds(pl.multiple_of(role * width + start, 128), chans)
            copies.append(pltpu.make_async_copy(wide_ref.at[:, columns], piece.at[0, role], sems.at[chip, role]))
        copies.append(pltpu.make_async_copy(came_ref.at[chip], piece.at[1], sems.at[chip, roles]))
    wait_all(copies)


def leaving_pieces(me, wide, groups, roles):
    rows, width = wide.shape
    chans = width // roles // groups
    return pl.pallas_call(
        leave_kernel,
        out_shape=jax.ShapeDtypeStruct((groups // 2, roles, rows, chans), BF16),
        in_specs=[pl.BlockSpec(memory_space=pltpu.SMEM), pl.BlockSpec(memory_space=pl.ANY)],
        out_specs=pl.BlockSpec(memory_space=pltpu.VMEM),
        scratch_shapes=[pltpu.SemaphoreType.DMA((groups // 2, roles))],
        compiler_params=pltpu.CompilerParams(vmem_limit_bytes=4 * MIB),
        cost_estimate=pl.CostEstimate(flops=0, bytes_accessed=2 * rows * width, transcendentals=0),
        name="leaving_pieces",
    )(me, *in_hbm(wide))


def pieces_for_owners(me, wide, came, groups):
    chips, roles, rows, chans = came.shape
    return pl.pallas_call(
        piece_kernel,
        out_shape=[jax.ShapeDtypeStruct((2, roles, rows, chans), BF16)] * chips,
        in_specs=[pl.BlockSpec(memory_space=pltpu.SMEM), pl.BlockSpec(memory_space=pl.ANY), pl.BlockSpec(memory_space=pltpu.VMEM)],
        out_specs=[pl.BlockSpec(memory_space=pltpu.VMEM)] * chips,
        scratch_shapes=[pltpu.SemaphoreType.DMA((chips, roles + 1))],
        compiler_params=pltpu.CompilerParams(vmem_limit_bytes=8 * MIB),
        cost_estimate=pl.CostEstimate(flops=0, bytes_accessed=8 * chips * roles * rows * chans, transcendentals=0),
        name="pieces_for_owners",
    )(me, *in_hbm(wide), came)


def split_kernel(wide_ref, pieces_ref, sems):
    groups, _, part = pieces_ref.shape
    wait_all(
        [
            pltpu.make_async_copy(
                wide_ref.at[:, pl.ds(owner * part, part)], pieces_ref.at[owner], sems.at[owner]
            )
            for owner in range(groups)
        ]
    )


def split_columns(wide, groups):
    rows, width = wide.shape
    return pl.pallas_call(
        split_kernel,
        out_shape=jax.ShapeDtypeStruct((groups, rows, width // groups), BF16),
        in_specs=[pl.BlockSpec(memory_space=pl.ANY)],
        out_specs=pl.BlockSpec(memory_space=pltpu.VMEM),
        scratch_shapes=[pltpu.SemaphoreType.DMA((groups,))],
        compiler_params=pltpu.CompilerParams(vmem_limit_bytes=4 * MIB),
        cost_estimate=pl.CostEstimate(flops=0, bytes_accessed=4 * rows * width, transcendentals=0),
        name="split_columns",
    )(*in_hbm(wide))


def featurize(step, source, incoming, taps_ref, held, feats, moved):
    _, rows, chans = incoming.shape
    for part in range(chans // 128):
        lanes = slice(part * 128, part * 128 + 128)
        taps = []
        for role in range(3):
            held[role, part, 0:HALO, :] = held[role, part, rows : rows + HALO, :]
            held[role, part, HALO:, :] = source[step, role, :, lanes].astype(F32)
            taps.append([taps_ref[role, tap : tap + 1, lanes] for tap in range(TAPS)])
        for row in range(0, rows, 16):
            span = slice(row, row + 16)
            features = []
            for role in range(3):
                total = taps[role][0] * held[role, part, HALO + row : HALO + row + 16, :]
                for tap in range(1, TAPS):
                    total = total + taps[role][tap] * held[role, part, HALO + row - tap : HALO + row - tap + 16, :]
                feats[step, role, span, lanes] = total
                features.append(total)
            query, keyed, value = features
            moved[step, 0, span, lanes] = (keyed * value).astype(BF16)
            moved[step, 1, span, lanes] = (incoming[step, span, lanes].astype(F32) * query).astype(BF16)


def split_all(moved, rings):
    groups, _, rows, chans = moved.shape
    leaf = groups * rows // 8
    per_piece = leaf // rows

    @pl.loop(0, rows // 16)
    def _(strip):
        inside = pl.ds(pl.multiple_of(strip * 16, 16), 16)
        for part in range(per_piece):
            real_rows = pl.ds(pl.multiple_of(part * rows + strip * 16, 16), 16)
            imag_rows = pl.ds(pl.multiple_of(leaf + part * rows + strip * 16, 16), 16)
            for kind in range(2):
                for lane in range(0, chans, 128):
                    lanes = slice(lane, lane + 128)
                    parts = [
                        moved[piece * per_piece + part, kind, inside, lanes].astype(F32) for piece in range(8)
                    ]
                    into = slice(kind * chans + lane, kind * chans + lane + 128)
                    for index, (real, imag) in enumerate(split_rings(parts)):
                        rings[index, real_rows, into] = real.astype(BF16)
                        rings[index, imag_rows, into] = imag.astype(BF16)


def multiply_ring(step, rings, table, back, spec, products, joined):
    chans = spec.shape[2]
    leaf = spec.shape[1] // 2
    both = jnp.dot(table[step], rings[step], preferred_element_type=F32)
    g_real, g_imag = both[:leaf, :chans], both[leaf:, :chans]
    d_real, d_imag = both[:leaf, chans:], both[leaf:, chans:]
    f_real, f_imag = spec[step, :leaf], spec[step, leaf:]
    products[:leaf, 0:chans] = (g_real * f_real - g_imag * f_imag).astype(BF16)
    products[leaf:, 0:chans] = (g_real * f_imag + g_imag * f_real).astype(BF16)
    products[:leaf, chans : 2 * chans] = (d_real * f_real + d_imag * f_imag).astype(BF16)
    products[leaf:, chans : 2 * chans] = (d_imag * f_real - d_real * f_imag).astype(BF16)
    products[:leaf, 2 * chans :] = (d_real * g_real + d_imag * g_imag).astype(BF16)
    products[leaf:, 2 * chans :] = (d_imag * g_real - d_real * g_imag).astype(BF16)
    joined[step] = jnp.dot(back[step], products[...], preferred_element_type=F32)


def join_all(joined, moved, gain_ref, sent, flat, skip_ref):
    groups, _, rows, chans = moved.shape
    leaf = groups * rows // 8
    per_piece = leaf // rows
    skip_ref[...] = jnp.zeros_like(skip_ref)

    @pl.loop(0, rows // 16)
    def _(strip):
        inside = pl.ds(pl.multiple_of(strip * 16, 16), 16)
        for part in range(per_piece):
            real_rows = pl.ds(pl.multiple_of(part * rows + strip * 16, 16), 16)
            imag_rows = pl.ds(pl.multiple_of(leaf + part * rows + strip * 16, 16), 16)
            for lane in range(0, chans, 128):
                lanes = slice(lane, lane + 128)
                gain = gain_ref[0:1, lanes]
                for kind in range(3):
                    column = slice(kind * chans + lane, kind * chans + lane + 128)
                    leaves = [
                        (joined[index, real_rows, column], joined[index, imag_rows, column]) for index in range(8)
                    ]
                    total = jnp.zeros((16, 128), F32)
                    for piece, result in enumerate(join_rings(leaves)):
                        owner = piece * per_piece + part
                        if kind == 0:
                            sent[owner, 0, inside, lanes] = result.astype(BF16)
                        elif kind == 1:
                            grad = moved[owner, 1, inside, lanes].astype(F32)
                            sent[owner, 1, inside, lanes] = (result + gain * grad).astype(BF16)
                            total = total + grad * moved[owner, 0, inside, lanes].astype(F32)
                        else:
                            into = pl.ds(pl.multiple_of(owner * rows + strip * 16, 16), 16)
                            flat[into, lanes] = result
                    if kind == 1:
                        skip_ref[0:1, lanes] += jnp.sum(total, axis=0, keepdims=True)


def gradients(block, slot, source, incoming, feats, sent, taps_ref, gain_ref, grads, sums, slots):
    _, rows, chans = incoming.shape
    for part in range(chans // 128):
        lanes = slice(part * 128, part * 128 + 128)
        gain = gain_ref[0:1, lanes]
        for role in range(3):
            grads[role, part, rows : rows + HALO, :] = grads[role, part, 0:HALO, :]
        for row in range(0, rows, 16):
            span = slice(row, row + 16)
            query, keyed, value = [feats[block, role, span, lanes] for role in range(3)]
            gated = (keyed * value).astype(BF16).astype(F32)
            inner = sent[block, 0, span, lanes].astype(F32) + gain * gated
            through = sent[block, 1, span, lanes].astype(F32)
            grads[0, part, span, :] = incoming[block, span, lanes].astype(F32) * inner
            grads[1, part, span, :] = through * value
            grads[2, part, span, :] = through * keyed
            slots[slot, span, lanes] = (query * inner).astype(BF16)
        for role in range(3):
            taps = [taps_ref[role, tap : tap + 1, lanes] for tap in range(TAPS)]
            parts = [jnp.zeros((16, 128), F32) for _ in range(TAPS)]
            for row in range(0, rows, 16):
                here = source[block, role, row : row + 16, lanes].astype(F32)
                total = jnp.zeros((16, 128), F32)
                for tap in range(TAPS):
                    ahead = grads[role, part, row + tap : row + tap + 16, :]
                    total = total + taps[tap] * ahead
                    parts[tap] = parts[tap] + here * ahead
                start = (1 + role) * rows + row
                slots[slot, start : start + 16, lanes] = total.astype(BF16)
            for tap in range(TAPS):
                sums[role, tap, :, lanes] += parts[tap][0:8] + parts[tap][8:16]


def owner_kernel(chunk, groups, me_ref, *refs):
    pieces = refs[: groups // 2]
    incoming_hbm, spec_hbm, table_hbm, back_hbm, taps_ref, gain_ref = refs[groups // 2 : groups // 2 + 6]
    (
        ready_hbm, filt_hbm, skip_ref,
        source, incoming, spec, table, back, held, feats, moved, rings, products, joined, sent, flat, turned_flat,
        grads, sums, slots, last,
        piece_sems, incoming_sem, spec_sems, table_sems, back_sems, filt_sem, slot_sems, last_sems,
    ) = refs[-29:]
    _, rows, chans = incoming.shape

    lanes = pl.ds(chunk * chans, chans)
    incoming_copy = pltpu.make_async_copy(incoming_hbm.at[:, :, lanes], incoming, incoming_sem.at[0])
    incoming_copy.start()
    for partner in range(groups):
        block = me_ref[0] ^ partner
        piece = pieces[partner // 2].at[partner % 2, :, :, lanes]
        pltpu.make_async_copy(piece, source.at[block], piece_sems.at[block]).start()
    loads = []
    for ring in range(8):
        loads.append(
            [
                pltpu.make_async_copy(table_hbm.at[ring], table.at[ring], table_sems.at[ring]),
                pltpu.make_async_copy(spec_hbm.at[ring, :, lanes], spec.at[ring], spec_sems.at[ring]),
                pltpu.make_async_copy(back_hbm.at[ring], back.at[ring], back_sems.at[ring]),
            ]
        )
        for copy in loads[-1]:
            copy.start()
    held[:, :, rows:, :] = jnp.zeros((3, chans // 128, HALO, 128), F32)
    grads[:, :, 0:HALO, :] = jnp.zeros((3, chans // 128, HALO, 128), F32)
    sums[...] = jnp.zeros_like(sums)
    incoming_copy.wait()

    @pl.loop(0, groups)
    def _(step):
        pltpu.make_async_copy(pieces[0].at[0, :, :, lanes], source.at[step], piece_sems.at[step]).wait()
        featurize(step, source, incoming, taps_ref, held, feats, moved)

    split_all(moved, rings)

    @pl.loop(0, 8)
    def _(step):
        pltpu.make_async_copy(table_hbm.at[step], table.at[step], table_sems.at[step]).wait()
        pltpu.make_async_copy(spec_hbm.at[step, :, lanes], spec.at[step], spec_sems.at[step]).wait()
        pltpu.make_async_copy(back_hbm.at[step], back.at[step], back_sems.at[step]).wait()
        multiply_ring(step, rings, table, back, spec, products, joined)

    join_all(joined, moved, gain_ref, sent, flat, skip_ref)
    for block in range(groups):
        span = slice(block * rows, (block + 1) * rows)
        turned_flat[:, span] = flat[span, :].T
    filt_copy = pltpu.make_async_copy(turned_flat, filt_hbm.at[pl.ds(chunk * chans, chans)], filt_sem.at[0])
    filt_copy.start()

    def write_back(slot_at, block_at):
        return pltpu.make_async_copy(
            slots.at[slot_at], ready_hbm.at[block_at, pl.ds(0, 4 * rows)], slot_sems.at[slot_at]
        )

    @pl.loop(0, groups)
    def _(step):
        block = groups - 1 - step
        slot = lax.rem(step, 2)

        @pl.when(step >= 2)
        def _():
            write_back(slot, block + 2).wait()

        gradients(block, slot, source, incoming, feats, sent, taps_ref, gain_ref, grads, sums, slots)
        write_back(slot, block).start()

    rows_out = []
    for role in range(3):
        for tap in range(TAPS):
            rows_out.append(jnp.sum(sums[role, tap], axis=0, keepdims=True))
        rows_out.append(jnp.zeros((HALO - TAPS, chans), F32))
    rows_out.append(jnp.zeros((EXTRA - 3 * HALO, chans), F32))
    last[...] = jnp.concatenate(rows_out, axis=0).astype(BF16)
    wait_all(
        [
            pltpu.make_async_copy(last, ready_hbm.at[owner, pl.ds(4 * rows, EXTRA)], last_sems.at[owner])
            for owner in range(groups)
        ]
    )
    write_back(groups % 2, 1).wait()
    write_back((groups + 1) % 2, 0).wait()
    filt_copy.wait()


def owner_work(me, pieces, incoming, spectrum, table, back, taps, gain, chunk, earlier):
    groups, rows, chans = incoming.shape
    chans = chans // CHUNKS
    length = groups * rows
    wide = length // 4
    parts = chans // 128
    flops = 80 * wide * wide * chans + 200 * length * chans
    return pl.pallas_call(
        functools.partial(owner_kernel, chunk, groups),
        input_output_aliases={groups // 2 + 7: 1} if earlier else {},
        out_shape=(
            pltpu.HBM((groups, 4 * rows + EXTRA, chans), BF16),
            pltpu.HBM((CHUNKS * chans, length), F32),
            jax.ShapeDtypeStruct((1, chans), F32),
        ),
        in_specs=[pl.BlockSpec(memory_space=pltpu.SMEM)]
        + [pl.BlockSpec(memory_space=pl.ANY)] * (groups // 2 + 4)
        + [pl.BlockSpec(memory_space=pltpu.VMEM)] * 2
        + [pl.BlockSpec(memory_space=pl.ANY)] * len(earlier),
        out_specs=(
            pl.BlockSpec(memory_space=pl.ANY),
            pl.BlockSpec(memory_space=pl.ANY),
            pl.BlockSpec(memory_space=pltpu.VMEM),
        ),
        scratch_shapes=[
            pltpu.VMEM((groups, 3, rows, chans), BF16),
            pltpu.VMEM((groups, rows, chans), BF16),
            pltpu.VMEM((8, wide, chans), F32),
            pltpu.VMEM((8, wide, wide), BF16),
            pltpu.VMEM((8, wide, wide), BF16),
            pltpu.VMEM((3, parts, HALO + rows, 128), F32),
            pltpu.VMEM((groups, 3, rows, chans), F32),
            pltpu.VMEM((groups, 2, rows, chans), BF16),
            pltpu.VMEM((8, wide, 2 * chans), BF16),
            pltpu.VMEM((wide, 3 * chans), BF16),
            pltpu.VMEM((8, wide, 3 * chans), F32),
            pltpu.VMEM((groups, 2, rows, chans), BF16),
            pltpu.VMEM((length, chans), F32),
            pltpu.VMEM((chans, length), F32),
            pltpu.VMEM((3, parts, rows + HALO, 128), F32),
            pltpu.VMEM((3, TAPS, 8, chans), F32),
            pltpu.VMEM((2, 4 * rows, chans), BF16),
            pltpu.VMEM((EXTRA, chans), BF16),
            pltpu.SemaphoreType.DMA((groups,)),
            pltpu.SemaphoreType.DMA((1,)),
            pltpu.SemaphoreType.DMA((8,)),
            pltpu.SemaphoreType.DMA((8,)),
            pltpu.SemaphoreType.DMA((8,)),
            pltpu.SemaphoreType.DMA((1,)),
            pltpu.SemaphoreType.DMA((2,)),
            pltpu.SemaphoreType.DMA((groups,)),
        ],
        compiler_params=pltpu.CompilerParams(vmem_limit_bytes=OWNER_MIB * MIB),
        cost_estimate=pl.CostEstimate(flops=flops, bytes_accessed=24 * MIB, transcendentals=0),
        name="owner_work",
    )(me, *in_hbm(*pieces, incoming, spectrum, table, back), taps, gain, *in_hbm(*earlier))


def place_kernel(chunk, held_ref, *refs):
    output_ref, grad_ref, sems = refs[-3:]
    groups, _, part = held_ref.shape
    rows, width = output_ref.shape
    copies = []
    for owner in range(groups):
        start = owner * (width // groups) + chunk * part
        for kind in range(4):
            into, at = (output_ref, start) if kind == 0 else (grad_ref, (kind - 1) * width + start)
            copies.append(
                pltpu.make_async_copy(
                    held_ref.at[owner, pl.ds(kind * rows, rows)], into.at[:, pl.ds(at, part)], sems.at[owner, kind]
                )
            )
    wait_all(copies)


def place_columns(held, rows, chunk, earlier):
    groups, _, part = held.shape
    width = groups * part * CHUNKS
    return pl.pallas_call(
        functools.partial(place_kernel, chunk),
        input_output_aliases={1: 0, 2: 1} if earlier else {},
        out_shape=(pltpu.HBM((rows, width), BF16), pltpu.HBM((rows, 3 * width), BF16)),
        in_specs=[pl.BlockSpec(memory_space=pltpu.VMEM)] + [pl.BlockSpec(memory_space=pl.ANY)] * len(earlier),
        out_specs=(pl.BlockSpec(memory_space=pl.ANY),) * 2,
        scratch_shapes=[pltpu.SemaphoreType.DMA((groups, 4))],
        compiler_params=pltpu.CompilerParams(vmem_limit_bytes=12 * MIB),
        cost_estimate=pl.CostEstimate(flops=0, bytes_accessed=16 * rows * width, transcendentals=0),
        name="place_columns",
    )(held, *in_hbm(*earlier))


def on_device(acts, cots, kern, filt, skip):
    rows, feats_all = acts.shape[1:]
    groups = lax.axis_size("ctx")
    chans = filt.shape[1]
    part = chans // CHUNKS
    place = lax.axis_index("ctx").astype(jnp.int32)
    me = place[None]

    table, back = (jnp.asarray(one) for one in leaf_tables(rows * groups))
    spectrum = filter_spectrum(filt[0], table)
    gain = lax.dynamic_slice_in_dim(skip, place * chans, chans, axis=1)
    taps = kern[0].reshape(TAPS, 3, groups, chans)
    taps = lax.dynamic_index_in_dim(taps, place, axis=2, keepdims=False).transpose(1, 0, 2)
    taps = jnp.pad(taps, ((0, 0), (0, HALO - TAPS), (0, 0)))

    incoming = passed_along(split_columns(cots[0], groups), "section", -1)
    came = handed_over(leaving_pieces(me, acts[0], groups, 3), 0, 1)
    pieces = pieces_for_owners(me, acts[0], came, groups)
    pieces = [handed_over(piece, 1, 2 * chip) for chip, piece in enumerate(pieces)]
    incoming, pieces[:GATE] = lax.optimization_barrier((incoming, pieces[:GATE]))
    incoming = lax.all_to_all(incoming, "ctx", split_axis=0, concat_axis=0, tiled=True)

    filters, skips, results, tap_sums = [], [], (), []
    for chunk in range(CHUNKS):
        span = slice(chunk * part, chunk * part + part)
        ready, *filters, skip_grad = owner_work(
            me, pieces, incoming, spectrum, table, back, taps[:, :, span], gain[:, span], chunk, filters
        )
        ready = lax.all_to_all(ready, "ctx", split_axis=0, concat_axis=0, tiled=True)
        results = place_columns(ready, rows, chunk, results)
        skips.append(skip_grad)
        sums = ready[:, 4 * rows : 4 * rows + 3 * HALO].reshape(groups, 3, HALO, part)[:, :, :TAPS]
        tap_sums.append(sums.transpose(2, 1, 0, 3).astype(F32))
    kern_grad = jnp.stack(tap_sums, axis=3).reshape(TAPS, feats_all)
    skip_grad = jnp.concatenate(skips, axis=1)
    output, input_grad = results
    return (output[None], input_grad[None], kern_grad[None], filters[0][None], skip_grad)


def solution(mesh):
    return jax.shard_map(
        on_device,
        mesh=mesh,
        in_specs=(
            P("section", "ctx", None),
            P("section", "ctx", None),
            P("section", None, None),
            P("section", "ctx", None),
            P("section", None),
        ),
        out_specs=(
            P("section", "ctx", None),
            P("section", "ctx", None),
            P("section", None, None),
            P("section", "ctx", None),
            P("section", "ctx"),
        ),
        check_vma=False,
    )
```

```python
import functools
import math

import jax
import jax.numpy as jnp
import ml_dtypes
import numpy as np
from jax import lax
from jax.experimental import pallas as pl
from jax.experimental.pallas import tpu as pltpu
from jax.sharding import PartitionSpec as P

TAPS = 7
HALO = 8
EXTRA = 32
LATE = 4
ROOT = math.sqrt(0.5)
F32 = jnp.float32
BF16 = jnp.bfloat16
MIB = 1 << 20


def in_hbm(*arrays):
    return [pltpu.with_memory_space_constraint(array, pltpu.HBM) for array in arrays]


def passed_along(value, axis, steps):
    count = lax.axis_size(axis)
    pairs = [(source, (source + steps) % count) for source in range(count)]
    return lax.ppermute(value, axis, pairs)


def handed_over(value, steps, partner):
    sections, groups = lax.axis_size("section"), lax.axis_size("ctx")
    pairs = [
        (section * groups + place, (section + steps) % sections * groups + (place ^ partner))
        for section in range(sections)
        for place in range(groups)
    ]
    return lax.ppermute(value, ("section", "ctx"), pairs)


def leaf_angles():
    angles = [math.pi / 2]
    for _ in range(3):
        angles = [half for angle in angles for half in (angle / 2, angle / 2 + math.pi)]
    return angles


def leaf_tables(length):
    leaf = length // 8
    order = np.arange(leaf)
    tables = []
    for angle in leaf_angles():
        phase = (angle + 2.0 * np.pi * order[:, None]) / leaf * order[None, :]
        real, imag = np.cos(phase), np.sin(phase)
        tables.append(np.block([[real, -imag], [imag, real]]))
    table = np.stack(tables)
    back = table.transpose(0, 2, 1) / length
    return table.astype(ml_dtypes.bfloat16), back.astype(ml_dtypes.bfloat16)


def turned(pair, angle):
    real, imag = pair
    cos, sin = math.cos(angle), math.sin(angle)
    return real * cos - imag * sin, real * sin + imag * cos


def split_rings(parts):
    low, high = [], []
    for lower, upper in zip(parts[:4], parts[4:]):
        scaled = upper * ROOT
        low.append((lower + scaled, scaled))
        high.append((lower - scaled, -scaled))
    rings = [(math.pi / 4, low), (math.pi / 4 + math.pi, high)]
    while len(rings[0][1]) > 1:
        finer = []
        for angle, pieces in rings:
            half = len(pieces) // 2
            plus, minus = [], []
            for lower, upper in zip(pieces[:half], pieces[half:]):
                real, imag = turned(upper, angle / 2)
                plus.append((lower[0] + real, lower[1] + imag))
                minus.append((lower[0] - real, lower[1] - imag))
            finer += [(angle / 2, plus), (angle / 2 + math.pi, minus)]
        rings = finer
    return [pieces[0] for _, pieces in rings]


def join_rings(leaves):
    angles = [math.pi / 4, math.pi / 4 + math.pi]
    angles = [half for angle in angles for half in (angle / 2, angle / 2 + math.pi)]
    groups = [[leaf] for leaf in leaves]
    while len(groups) > 2:
        merged = []
        for index in range(0, len(groups), 2):
            angle = angles[index // 2] if len(groups) == 8 else [math.pi / 4, math.pi / 4 + math.pi][index // 2]
            lower, upper = [], []
            for plus, minus in zip(groups[index], groups[index + 1]):
                lower.append((plus[0] + minus[0], plus[1] + minus[1]))
                upper.append(turned((plus[0] - minus[0], plus[1] - minus[1]), -angle / 2))
            merged.append(lower + upper)
        groups = merged
    lower, upper = [], []
    for plus, minus in zip(groups[0], groups[1]):
        lower.append(plus[0] + minus[0])
        upper.append(((plus[0] - minus[0]) + (plus[1] - minus[1])) * ROOT)
    return lower + upper


def filter_kernel(filt_ref, table_ref, spec_ref, rings):
    chans, length = filt_ref.shape
    leaf = length // 8
    step = pl.program_id(0)

    @pl.when(step == 0)
    def _():
        @pl.loop(0, chans // 16)
        def _(strip):
            rows = pl.ds(pl.multiple_of(strip * 16, 16), 16)
            for lane in range(0, leaf, 128):
                parts = [
                    filt_ref[rows, piece * leaf + lane : piece * leaf + lane + 128].astype(F32)
                    for piece in range(8)
                ]
                for index, (real, imag) in enumerate(split_rings(parts)):
                    rings[index, rows, lane : lane + 128] = real.astype(BF16)
                    rings[index, rows, leaf + lane : leaf + lane + 128] = imag.astype(BF16)

    spec_ref[0] = lax.dot_general(
        table_ref[0], rings[step], (((1,), (1,)), ((), ())), preferred_element_type=F32
    )


def filter_spectrum(filt, table):
    chans, length = filt.shape
    wide = length // 4
    return pl.pallas_call(
        filter_kernel,
        out_shape=pltpu.HBM((8, wide, chans), F32),
        grid=(8,),
        in_specs=[
            pl.BlockSpec((chans, length), lambda j: (0, 0)),
            pl.BlockSpec((1, wide, wide), lambda j: (j, 0, 0)),
        ],
        out_specs=pl.BlockSpec((1, wide, chans), lambda j: (j, 0, 0)),
        scratch_shapes=[pltpu.VMEM((8, chans, wide), BF16)],
        compiler_params=pltpu.CompilerParams(vmem_limit_bytes=12 * MIB),
        cost_estimate=pl.CostEstimate(
            flops=16 * wide * wide * chans, bytes_accessed=10 * MIB, transcendentals=0
        ),
        name="filter_spectrum",
    )(*in_hbm(filt, table))


def wait_all(copies):
    for copy in copies:
        copy.start()
    for copy in copies:
        copy.wait()


def leave_kernel(me_ref, wide_ref, leaving_ref, sems):
    chips, roles, _, chans = leaving_ref.shape
    width = wide_ref.shape[1] // 3
    copies = []
    for chip in range(chips):
        start = (me_ref[0] ^ (2 * chip + 1)) * chans
        for role in range(roles):
            columns = pl.ds(pl.multiple_of((role + 1) * width + start, 128), chans)
            copies.append(
                pltpu.make_async_copy(wide_ref.at[:, columns], leaving_ref.at[chip, role], sems.at[chip, role])
            )
    wait_all(copies)


def piece_kernel(me_ref, wide_ref, came_ref, *refs):
    *pieces, sems = refs
    _, roles, _, chans = pieces[0].shape
    width = wide_ref.shape[1] // 3
    copies = []
    for chip, piece in enumerate(pieces):
        start = (me_ref[0] ^ (2 * chip)) * chans
        for role in range(roles):
            columns = pl.ds(pl.multiple_of((role + 1) * width + start, 128), chans)
            copies.append(pltpu.make_async_copy(wide_ref.at[:, columns], piece.at[0, role], sems.at[chip, role]))
        copies.append(pltpu.make_async_copy(came_ref.at[chip], piece.at[1], sems.at[chip, roles]))
    wait_all(copies)


def leaving_pieces(me, wide, groups, roles):
    rows, width = wide.shape
    chans = width // 3 // groups
    return pl.pallas_call(
        leave_kernel,
        out_shape=jax.ShapeDtypeStruct((groups // 2, roles, rows, chans), BF16),
        in_specs=[pl.BlockSpec(memory_space=pltpu.SMEM), pl.BlockSpec(memory_space=pl.ANY)],
        out_specs=pl.BlockSpec(memory_space=pltpu.VMEM),
        scratch_shapes=[pltpu.SemaphoreType.DMA((groups // 2, roles))],
        compiler_params=pltpu.CompilerParams(vmem_limit_bytes=4 * MIB),
        cost_estimate=pl.CostEstimate(flops=0, bytes_accessed=2 * rows * width, transcendentals=0),
        name="leaving_pieces",
    )(me, *in_hbm(wide))


def pieces_for_owners(me, wide, came, groups):
    chips, roles, rows, chans = came.shape
    return pl.pallas_call(
        piece_kernel,
        out_shape=[jax.ShapeDtypeStruct((2, roles, rows, chans), BF16)] * chips,
        in_specs=[pl.BlockSpec(memory_space=pltpu.SMEM), pl.BlockSpec(memory_space=pl.ANY), pl.BlockSpec(memory_space=pltpu.VMEM)],
        out_specs=[pl.BlockSpec(memory_space=pltpu.VMEM)] * chips,
        scratch_shapes=[pltpu.SemaphoreType.DMA((chips, roles + 1))],
        compiler_params=pltpu.CompilerParams(vmem_limit_bytes=8 * MIB),
        cost_estimate=pl.CostEstimate(flops=0, bytes_accessed=8 * chips * roles * rows * chans, transcendentals=0),
        name="pieces_for_owners",
    )(me, *in_hbm(wide), came)


def tap_sum(held, part, taps, row):
    total = taps[0] * held[part, HALO + row : HALO + row + 16, :]
    for tap in range(1, TAPS):
        total = total + taps[tap] * held[part, HALO + row - tap : HALO + row - tap + 16, :]
    return total


def hold(held, part, block):
    rows = block.shape[0]
    held[part, 0:HALO, :] = held[part, rows : rows + HALO, :]
    held[part, HALO:, :] = block.astype(F32)


def tap_rows(taps_ref, role, lanes):
    return [taps_ref[role, tap : tap + 1, lanes] for tap in range(TAPS)]


def split_signal(signal, rings):
    groups, rows, chans = signal.shape
    leaf = groups * rows // 8
    per_piece = leaf // rows

    @pl.loop(0, rows // 16)
    def _(strip):
        inside = pl.ds(pl.multiple_of(strip * 16, 16), 16)
        for part in range(per_piece):
            real_rows = pl.ds(pl.multiple_of(part * rows + strip * 16, 16), 16)
            imag_rows = pl.ds(pl.multiple_of(leaf + part * rows + strip * 16, 16), 16)
            for lane in range(0, chans, 128):
                lanes = slice(lane, lane + 128)
                parts = [signal[piece * per_piece + part, inside, lanes].astype(F32) for piece in range(8)]
                for index, (real, imag) in enumerate(split_rings(parts)):
                    rings[index, real_rows, lanes] = real.astype(BF16)
                    rings[index, imag_rows, lanes] = imag.astype(BF16)


def join_signal(joined, first, rows, place):
    leaf = joined.shape[1] // 2
    per_piece = leaf // rows
    chans = 256 if joined.shape[2] % 256 == 0 else 128

    @pl.loop(0, rows // 16)
    def _(strip):
        inside = pl.ds(pl.multiple_of(strip * 16, 16), 16)
        for part in range(per_piece):
            real_rows = pl.ds(pl.multiple_of(part * rows + strip * 16, 16), 16)
            imag_rows = pl.ds(pl.multiple_of(leaf + part * rows + strip * 16, 16), 16)
            for lane in range(0, chans, 128):
                column = slice(first + lane, first + lane + 128)
                leaves = [
                    (joined[index, real_rows, column], joined[index, imag_rows, column]) for index in range(8)
                ]
                for piece, result in enumerate(join_rings(leaves)):
                    place(piece * per_piece + part, strip, inside, slice(lane, lane + 128), result)


def back_taps(grads, source_block, part, taps, place, sums, role, lanes):
    rows = grads.shape[1] - HALO
    parts = [jnp.zeros((16, 128), F32) for _ in range(TAPS)]
    for row in range(0, rows, 16):
        here = source_block(row).astype(F32)
        total = jnp.zeros((16, 128), F32)
        for tap in range(TAPS):
            ahead = grads[part, row + tap : row + tap + 16, :]
            total = total + taps[tap] * ahead
            parts[tap] = parts[tap] + here * ahead
        place(row, total.astype(BF16))
    for tap in range(TAPS):
        sums[role, tap, :, lanes] += parts[tap][0:8] + parts[tap][8:16]


def sum_rows(sums, roles):
    rows_out = []
    chans = sums.shape[3]
    for role in range(roles):
        for tap in range(TAPS):
            rows_out.append(jnp.sum(sums[role, tap], axis=0, keepdims=True))
        rows_out.append(jnp.zeros((HALO - TAPS, chans), F32))
    return rows_out


def mixed_kernel(groups, me_ref, *refs):
    pieces = refs[: groups // 2]
    spec_hbm, table_hbm, back_hbm, taps_ref, gain_ref = refs[groups // 2 : groups // 2 + 5]
    (
        feats_hbm, gated_hbm, inner_ref, ring_hbm,
        source, spec, table, back, held, feats, gated, rings, products, joined, ring,
        piece_sems, load_sems, feats_sems, gated_sem, ring_sems,
    ) = refs[groups // 2 + 5 :]
    _, _, rows, chans = source.shape
    for partner in range(groups):
        block = me_ref[0] ^ partner
        piece = pieces[partner // 2].at[partner % 2]
        pltpu.make_async_copy(piece, source.at[block], piece_sems.at[block]).start()
    loads = []
    for index in range(8):
        for kind, (from_ref, into) in enumerate(((table_hbm, table), (spec_hbm, spec), (back_hbm, back))):
            loads.append(pltpu.make_async_copy(from_ref.at[index], into.at[index], load_sems.at[kind, index]))
            loads[-1].start()
    held[:, :, rows:, :] = jnp.zeros((2, chans // 128, HALO, 128), F32)

    def feats_copy(block):
        return pltpu.make_async_copy(feats.at[block], feats_hbm.at[block], feats_sems.at[block])

    @pl.loop(0, groups)
    def _(step):
        pltpu.make_async_copy(pieces[0].at[0], source.at[step], piece_sems.at[step]).wait()
        for part in range(chans // 128):
            lanes = slice(part * 128, part * 128 + 128)
            for role in range(2):
                hold(held.at[role], part, source[step, role, :, lanes])
            taps = [tap_rows(taps_ref, role + 1, lanes) for role in range(2)]
            for row in range(0, rows, 16):
                span = slice(row, row + 16)
                keyed, value = [tap_sum(held.at[role], part, taps[role], row) for role in range(2)]
                feats[step, 0, span, lanes] = keyed
                feats[step, 1, span, lanes] = value
                gated[step, span, lanes] = (keyed * value).astype(BF16)
        feats_copy(step).start()

    gated_copy = pltpu.make_async_copy(gated, gated_hbm, gated_sem.at[0])
    gated_copy.start()
    split_signal(gated, rings)
    leaf = spec.shape[1] // 2

    def ring_copy(index):
        return pltpu.make_async_copy(ring.at[index], ring_hbm.at[index], ring_sems.at[index])

    @pl.loop(0, 8)
    def _(index):
        for kind, (from_ref, into) in enumerate(((table_hbm, table), (spec_hbm, spec), (back_hbm, back))):
            pltpu.make_async_copy(from_ref.at[index], into.at[index], load_sems.at[kind, index]).wait()
        ring[index] = jnp.dot(table[index], rings[index], preferred_element_type=F32)
        g_real, g_imag = ring[index, :leaf], ring[index, leaf:]
        f_real, f_imag = spec[index, :leaf], spec[index, leaf:]
        products[:leaf] = (g_real * f_real - g_imag * f_imag).astype(BF16)
        products[leaf:] = (g_real * f_imag + g_imag * f_real).astype(BF16)
        joined[index] = jnp.dot(back[index], products[...], preferred_element_type=F32)
        ring_copy(index).start()

    def place(owner, strip, inside, lanes, result):
        total = result + gain_ref[0:1, lanes] * gated[owner, inside, lanes].astype(F32)
        inner_ref[owner, inside, lanes] = total.astype(BF16)

    join_signal(joined, 0, rows, place)
    for owner in range(groups - 1):
        inner_ref[owner, rows:, :] = inner_ref[owner + 1, 0:HALO, :]
    inner_ref[groups - 1, rows:, :] = jnp.zeros((HALO, chans), BF16)

    @pl.loop(0, groups)
    def _(step):
        feats_copy(step).wait()

    gated_copy.wait()

    @pl.loop(0, 8)
    def _(index):
        ring_copy(index).wait()


def inner_work(me, pieces, spectrum, table, back, taps, gain):
    groups = 2 * len(pieces)
    _, _, rows, chans = pieces[0].shape
    length = groups * rows
    wide = length // 4
    parts = chans // 128
    return pl.pallas_call(
        functools.partial(mixed_kernel, groups),
        out_shape=(
            pltpu.HBM((groups, 2, rows, chans), F32),
            pltpu.HBM((groups, rows, chans), BF16),
            jax.ShapeDtypeStruct((groups, rows + HALO, chans), BF16),
            pltpu.HBM((8, wide, chans), F32),
        ),
        in_specs=[pl.BlockSpec(memory_space=pltpu.SMEM)]
        + [pl.BlockSpec(memory_space=pl.ANY)] * (groups // 2 + 3)
        + [pl.BlockSpec(memory_space=pltpu.VMEM)] * 2,
        out_specs=(
            pl.BlockSpec(memory_space=pl.ANY),
            pl.BlockSpec(memory_space=pl.ANY),
            pl.BlockSpec(memory_space=pltpu.VMEM),
            pl.BlockSpec(memory_space=pl.ANY),
        ),
        scratch_shapes=[
            pltpu.VMEM((groups, 2, rows, chans), BF16),
            pltpu.VMEM((8, wide, chans), F32),
            pltpu.VMEM((8, wide, wide), BF16),
            pltpu.VMEM((8, wide, wide), BF16),
            pltpu.VMEM((2, parts, HALO + rows, 128), F32),
            pltpu.VMEM((groups, 2, rows, chans), F32),
            pltpu.VMEM((groups, rows, chans), BF16),
            pltpu.VMEM((8, wide, chans), BF16),
            pltpu.VMEM((wide, chans), BF16),
            pltpu.VMEM((8, wide, chans), F32),
            pltpu.VMEM((8, wide, chans), F32),
            pltpu.SemaphoreType.DMA((groups,)),
            pltpu.SemaphoreType.DMA((3, 8)),
            pltpu.SemaphoreType.DMA((groups,)),
            pltpu.SemaphoreType.DMA((1,)),
            pltpu.SemaphoreType.DMA((8,)),
        ],
        compiler_params=pltpu.CompilerParams(vmem_limit_bytes=40 * MIB),
        cost_estimate=pl.CostEstimate(
            flops=32 * wide * wide * chans + 60 * length * chans, bytes_accessed=24 * MIB, transcendentals=0
        ),
        name="inner_values",
    )(me, *in_hbm(*pieces, spectrum, table, back), taps, gain)


def query_kernel(source, before, incoming, taps_ref, mix_grad, features, held):
    groups, rows, chans = mix_grad.shape

    @pl.loop(0, groups)
    def _(owner):
        for part in range(chans // 128):
            columns = pl.ds(pl.multiple_of(owner * chans + part * 128, 128), 128)
            lanes = slice(part * 128, part * 128 + 128)
            held[part, 0:HALO, :] = before[:, columns].astype(F32)
            held[part, HALO:, :] = source[:, columns].astype(F32)
            taps = [taps_ref[tap : tap + 1, columns] for tap in range(TAPS)]
            for row in range(0, rows, 16):
                span = slice(row, row + 16)
                total = tap_sum(held, part, taps, row)
                features[span, columns] = total
                mix_grad[owner, span, lanes] = (incoming[span, columns].astype(F32) * total).astype(BF16)


def query_features(source, before, incoming, taps, groups):
    rows, width = source.shape
    chans = width // groups
    return pl.pallas_call(
        query_kernel,
        out_shape=(
            jax.ShapeDtypeStruct((groups, rows, chans), BF16),
            jax.ShapeDtypeStruct((rows, width), F32),
        ),
        in_specs=[pl.BlockSpec(memory_space=pltpu.VMEM)] * 4,
        out_specs=(pl.BlockSpec(memory_space=pltpu.VMEM),) * 2,
        scratch_shapes=[pltpu.VMEM((chans // 128, HALO + rows, 128), F32)],
        compiler_params=pltpu.CompilerParams(vmem_limit_bytes=10 * MIB),
        cost_estimate=pl.CostEstimate(flops=15 * rows * width, bytes_accessed=10 * rows * width, transcendentals=0),
        name="query_features",
    )(source, before, incoming, taps)


def output_kernel(
    source, incoming, later, features, inner, taps_ref, output_hbm, grad_hbm, sums_ref, grads, sums, slots, slot_sems
):
    groups, _, chans = inner.shape
    rows = source.shape[0]

    def write_back(owner, slot):
        columns = pl.ds(pl.multiple_of(owner * chans, 128), chans)
        return [
            pltpu.make_async_copy(slots.at[slot, kind], into.at[:, columns], slot_sems.at[slot, kind])
            for kind, into in enumerate((output_hbm, grad_hbm))
        ]

    @pl.loop(0, groups)
    def _(owner):
        slot = lax.rem(owner, 2)

        @pl.when(owner >= 2)
        def _():
            for copy in write_back(owner - 2, slot):
                copy.wait()

        sums[...] = jnp.zeros_like(sums)
        for part in range(chans // 128):
            columns = pl.ds(pl.multiple_of(owner * chans + part * 128, 128), 128)
            lanes = slice(part * 128, part * 128 + 128)
            for row in range(0, rows, 16):
                span = slice(row, row + 16)
                values = inner[owner, span, lanes].astype(F32)
                grads[part, span, :] = incoming[span, columns].astype(F32) * values
                slots[slot, 0, span, lanes] = (features[span, columns] * values).astype(BF16)
            ahead = inner[owner, rows : rows + HALO, lanes].astype(F32)
            grads[part, rows:, :] = later[:, columns].astype(F32) * ahead

            def place(row, values, lanes=lanes):
                slots[slot, 1, row : row + 16, lanes] = values

            def source_block(row, columns=columns):
                return source[row : row + 16, columns]

            taps = [taps_ref[tap : tap + 1, columns] for tap in range(TAPS)]
            back_taps(grads, source_block, part, taps, place, sums, 0, lanes)
        sums_ref[owner] = jnp.concatenate(sum_rows(sums, 1), axis=0).astype(BF16)
        for copy in write_back(owner, slot):
            copy.start()

    for owner in (groups - 2, groups - 1):
        for copy in write_back(owner, owner % 2):
            copy.wait()


def query_outputs(source, incoming, later, features, inner, taps):
    rows, width = source.shape
    groups, _, chans = inner.shape
    return pl.pallas_call(
        output_kernel,
        out_shape=(
            pltpu.HBM((rows, width), BF16),
            pltpu.HBM((rows, 3 * width), BF16),
            jax.ShapeDtypeStruct((groups, HALO, chans), BF16),
        ),
        in_specs=[pl.BlockSpec(memory_space=pltpu.VMEM)] * 6,
        out_specs=(
            pl.BlockSpec(memory_space=pl.ANY),
            pl.BlockSpec(memory_space=pl.ANY),
            pl.BlockSpec(memory_space=pltpu.VMEM),
        ),
        scratch_shapes=[
            pltpu.VMEM((chans // 128, rows + HALO, 128), F32),
            pltpu.VMEM((1, TAPS, 8, chans), F32),
            pltpu.VMEM((2, 2, rows, chans), BF16),
            pltpu.SemaphoreType.DMA((2, 2)),
        ],
        compiler_params=pltpu.CompilerParams(vmem_limit_bytes=12 * MIB),
        cost_estimate=pl.CostEstimate(flops=35 * rows * width, bytes_accessed=14 * rows * width, transcendentals=0),
        name="query_outputs",
    )(source, incoming, later, features, inner, taps)


def through_kernel(groups, me_ref, *refs):
    pieces = refs[: groups // 2]
    (
        grad_hbm, feats_hbm, spec_hbm, table_hbm, back_hbm, taps_ref, gain_ref,
        ready_hbm, ring_hbm,
        source, mix_grad, feats, spec, ring, table, back, rings, products, joined, through,
        grads, sums, slots, last,
        piece_sems, signal_sem, feats_sems, load_sems, ring_sems, slot_sems, last_sems,
    ) = refs[groups // 2 :]
    _, rows, chans = through.shape
    signal = pltpu.make_async_copy(grad_hbm, mix_grad, signal_sem.at[0])
    signal.start()
    kinds = ((table_hbm, table), (spec_hbm, spec), (back_hbm, back))
    for index in range(8):
        for kind, (from_ref, into) in enumerate(kinds):
            pltpu.make_async_copy(from_ref.at[index], into.at[index], load_sems.at[kind, index]).start()
    for partner in range(groups):
        block = me_ref[0] ^ partner
        piece = pieces[partner // 2].at[partner % 2]
        pltpu.make_async_copy(piece, source.at[block], piece_sems.at[block]).start()

    def feats_copy(block):
        return pltpu.make_async_copy(feats_hbm.at[block], feats.at[block], feats_sems.at[block])

    for block in range(groups):
        feats_copy(block).start()
    grads[:, :, 0:HALO, :] = jnp.zeros((2, chans // 128, HALO, 128), F32)
    sums[...] = jnp.zeros_like(sums)
    signal.wait()
    split_signal(mix_grad, rings)
    leaf = spec.shape[1] // 2

    def ring_copy(index):
        return pltpu.make_async_copy(ring.at[index], ring_hbm.at[index], ring_sems.at[index])

    @pl.loop(0, 8)
    def _(index):
        for kind, (from_ref, into) in enumerate(kinds):
            pltpu.make_async_copy(from_ref.at[index], into.at[index], load_sems.at[kind, index]).wait()
        ring[index] = jnp.dot(table[index], rings[index], preferred_element_type=F32)
        d_real, d_imag = ring[index, :leaf], ring[index, leaf:]
        f_real, f_imag = spec[index, :leaf], spec[index, leaf:]
        products[:leaf] = (d_real * f_real + d_imag * f_imag).astype(BF16)
        products[leaf:] = (d_imag * f_real - d_real * f_imag).astype(BF16)
        joined[index] = jnp.dot(back[index], products[...], preferred_element_type=F32)
        ring_copy(index).start()

    def place_through(owner, strip, inside, lanes, result):
        grad = mix_grad[owner, inside, lanes].astype(F32)
        through[owner, inside, lanes] = (result + gain_ref[0:1, lanes] * grad).astype(BF16)

    join_signal(joined, 0, rows, place_through)

    @pl.loop(0, groups)
    def _(block):
        pltpu.make_async_copy(pieces[0].at[0], source.at[block], piece_sems.at[block]).wait()
        feats_copy(block).wait()

    def write_back(slot_at, block_at):
        return pltpu.make_async_copy(
            slots.at[slot_at], ready_hbm.at[block_at, pl.ds(0, 2 * rows)], slot_sems.at[slot_at]
        )

    @pl.loop(0, groups)
    def _(step):
        block = groups - 1 - step
        slot = lax.rem(step, 2)

        @pl.when(step >= 2)
        def _():
            write_back(slot, block + 2).wait()

        for part in range(chans // 128):
            lanes = slice(part * 128, part * 128 + 128)
            for role in range(2):
                grads[role, part, rows : rows + HALO, :] = grads[role, part, 0:HALO, :]
            for row in range(0, rows, 16):
                span = slice(row, row + 16)
                values = through[block, span, lanes].astype(F32)
                grads[0, part, span, :] = values * feats[block, 1, span, lanes]
                grads[1, part, span, :] = values * feats[block, 0, span, lanes]
            for role in range(2):

                def place(row, values, role=role, lanes=lanes):
                    slots[slot, role * rows + row : role * rows + row + 16, lanes] = values

                def source_block(row, role=role, lanes=lanes):
                    return source[block, role, row : row + 16, lanes]

                taps = tap_rows(taps_ref, role + 1, lanes)
                back_taps(grads.at[role], source_block, part, taps, place, sums, role, lanes)
        write_back(slot, block).start()

    rows_out = [jnp.zeros((HALO, chans), F32)] + sum_rows(sums, 2)
    rows_out.append(jnp.zeros((EXTRA - 3 * HALO, chans), F32))
    last[...] = jnp.concatenate(rows_out, axis=0).astype(BF16)
    wait_all(
        [
            pltpu.make_async_copy(last, ready_hbm.at[owner, pl.ds(2 * rows, EXTRA)], last_sems.at[owner])
            for owner in range(groups)
        ]
    )
    write_back(groups % 2, 1).wait()
    write_back((groups + 1) % 2, 0).wait()

    @pl.loop(0, 8)
    def _(index):
        ring_copy(index).wait()


def through_work(me, pieces, mix_grad, feats, spectrum, table, back, taps, gain):
    groups, rows, chans = mix_grad.shape
    length = groups * rows
    wide = length // 4
    parts = chans // 128
    return pl.pallas_call(
        functools.partial(through_kernel, groups),
        out_shape=(
            pltpu.HBM((groups, 2 * rows + EXTRA, chans), BF16),
            pltpu.HBM((8, wide, chans), F32),
        ),
        in_specs=[pl.BlockSpec(memory_space=pltpu.SMEM)]
        + [pl.BlockSpec(memory_space=pl.ANY)] * (groups // 2 + 5)
        + [pl.BlockSpec(memory_space=pltpu.VMEM)] * 2,
        out_specs=(pl.BlockSpec(memory_space=pl.ANY),) * 2,
        scratch_shapes=[
            pltpu.VMEM((groups, 2, rows, chans), BF16),
            pltpu.VMEM((groups, rows, chans), BF16),
            pltpu.VMEM((groups, 2, rows, chans), F32),
            pltpu.VMEM((8, wide, chans), F32),
            pltpu.VMEM((8, wide, chans), F32),
            pltpu.VMEM((8, wide, wide), BF16),
            pltpu.VMEM((8, wide, wide), BF16),
            pltpu.VMEM((8, wide, chans), BF16),
            pltpu.VMEM((wide, chans), BF16),
            pltpu.VMEM((8, wide, chans), F32),
            pltpu.VMEM((groups, rows, chans), BF16),
            pltpu.VMEM((2, parts, rows + HALO, 128), F32),
            pltpu.VMEM((2, TAPS, 8, chans), F32),
            pltpu.VMEM((2, 2 * rows, chans), BF16),
            pltpu.VMEM((EXTRA, chans), BF16),
            pltpu.SemaphoreType.DMA((groups,)),
            pltpu.SemaphoreType.DMA((1,)),
            pltpu.SemaphoreType.DMA((groups,)),
            pltpu.SemaphoreType.DMA((3, 8)),
            pltpu.SemaphoreType.DMA((8,)),
            pltpu.SemaphoreType.DMA((2,)),
            pltpu.SemaphoreType.DMA((groups,)),
        ],
        compiler_params=pltpu.CompilerParams(vmem_limit_bytes=40 * MIB),
        cost_estimate=pl.CostEstimate(
            flops=32 * wide * wide * chans + 100 * length * chans, bytes_accessed=28 * MIB, transcendentals=0
        ),
        name="through_values",
    )(me, *in_hbm(*pieces), mix_grad, *in_hbm(feats, spectrum, table, back), taps, gain)


def filter_grad_kernel(
    grad_hbm, gated_hbm, d_hbm, g_hbm, back_hbm, filt_hbm, skip_ref,
    mix_grad, gated, d_ring, g_ring, back, products, joined, flat, turned_flat, signal_sems, load_sems, filt_sem,
):
    groups, rows, chans = mix_grad.shape
    signals = [
        pltpu.make_async_copy(grad_hbm, mix_grad, signal_sems.at[0]),
        pltpu.make_async_copy(gated_hbm, gated, signal_sems.at[1]),
    ]
    kinds = ((d_hbm, d_ring), (g_hbm, g_ring), (back_hbm, back))
    for index in range(8):
        for kind, (from_ref, into) in enumerate(kinds):
            pltpu.make_async_copy(from_ref.at[index], into.at[index], load_sems.at[kind, index]).start()
    for copy in signals:
        copy.start()
    leaf = d_ring.shape[1] // 2

    @pl.loop(0, 8)
    def _(index):
        for kind, (from_ref, into) in enumerate(kinds):
            pltpu.make_async_copy(from_ref.at[index], into.at[index], load_sems.at[kind, index]).wait()
        d_real, d_imag = d_ring[index, :leaf], d_ring[index, leaf:]
        g_real, g_imag = g_ring[index, :leaf], g_ring[index, leaf:]
        products[:leaf] = (d_real * g_real + d_imag * g_imag).astype(BF16)
        products[leaf:] = (d_imag * g_real - d_real * g_imag).astype(BF16)
        joined[index] = jnp.dot(back[index], products[...], preferred_element_type=F32)

    for copy in signals:
        copy.wait()
    skip_ref[...] = jnp.zeros_like(skip_ref)

    @pl.loop(0, groups)
    def _(block):
        for lane in range(0, chans, 128):
            lanes = slice(lane, lane + 128)
            total = jnp.zeros((16, 128), F32)
            for row in range(0, rows, 16):
                span = slice(row, row + 16)
                total = total + mix_grad[block, span, lanes].astype(F32) * gated[block, span, lanes].astype(F32)
            skip_ref[0:1, lanes] += jnp.sum(total, axis=0, keepdims=True)

    def place_filter(owner, strip, inside, lanes, result):
        flat[pl.ds(pl.multiple_of(owner * rows + strip * 16, 16), 16), lanes] = result

    join_signal(joined, 0, rows, place_filter)
    for block in range(groups):
        span = slice(block * rows, (block + 1) * rows)
        turned_flat[:, span] = flat[span, :].T
    wait_all([pltpu.make_async_copy(turned_flat, filt_hbm, filt_sem.at[0])])


def filter_gradient(mix_grad, gated, d_ring, g_ring, back):
    groups, rows, chans = mix_grad.shape
    length = groups * rows
    wide = length // 4
    return pl.pallas_call(
        filter_grad_kernel,
        out_shape=(pltpu.HBM((chans, length), F32), jax.ShapeDtypeStruct((1, chans), F32)),
        in_specs=[pl.BlockSpec(memory_space=pl.ANY)] * 5,
        out_specs=(pl.BlockSpec(memory_space=pl.ANY), pl.BlockSpec(memory_space=pltpu.VMEM)),
        scratch_shapes=[
            pltpu.VMEM((groups, rows, chans), BF16),
            pltpu.VMEM((groups, rows, chans), BF16),
            pltpu.VMEM((8, wide, chans), F32),
            pltpu.VMEM((8, wide, chans), F32),
            pltpu.VMEM((8, wide, wide), BF16),
            pltpu.VMEM((wide, chans), BF16),
            pltpu.VMEM((8, wide, chans), F32),
            pltpu.VMEM((length, chans), F32),
            pltpu.VMEM((chans, length), F32),
            pltpu.SemaphoreType.DMA((2,)),
            pltpu.SemaphoreType.DMA((3, 8)),
            pltpu.SemaphoreType.DMA((1,)),
        ],
        compiler_params=pltpu.CompilerParams(vmem_limit_bytes=28 * MIB),
        cost_estimate=pl.CostEstimate(
            flops=16 * wide * wide * chans + 40 * length * chans, bytes_accessed=16 * MIB, transcendentals=0
        ),
        name="filter_gradient",
    )(mix_grad, *in_hbm(gated, d_ring, g_ring, back))


def place_kernel(columns, held_ref, *refs):
    *wide_refs, sems = refs
    groups, _, chans = held_ref.shape
    rows = wide_refs[-1].shape[0]
    wide_refs = wide_refs[-1 - max(index for index, _ in columns) :]
    copies = []
    for owner in range(groups):
        for kind, (index, first) in enumerate(columns):
            copies.append(
                pltpu.make_async_copy(
                    held_ref.at[owner, pl.ds(kind * rows, rows)],
                    wide_refs[index].at[:, pl.ds(first * groups * chans + owner * chans, chans)],
                    sems.at[owner, kind],
                )
            )
    wait_all(copies)


def place_columns(held, rows, columns, earlier):
    groups, _, chans = held.shape
    width = groups * chans
    shapes = [(rows, 3 * width)]
    return pl.pallas_call(
        functools.partial(place_kernel, columns),
        input_output_aliases={1: 0} if earlier else {},
        out_shape=[pltpu.HBM(shape, BF16) for shape in shapes],
        in_specs=[pl.BlockSpec(memory_space=pltpu.VMEM)] + [pl.BlockSpec(memory_space=pl.ANY)] * len(earlier),
        out_specs=[pl.BlockSpec(memory_space=pl.ANY)] * len(shapes),
        scratch_shapes=[pltpu.SemaphoreType.DMA((groups, 2))],
        compiler_params=pltpu.CompilerParams(vmem_limit_bytes=6 * MIB),
        cost_estimate=pl.CostEstimate(flops=0, bytes_accessed=8 * rows * width, transcendentals=0),
        name="place_columns",
    )(held, *in_hbm(*earlier))


def from_behind(block, axis, distance):
    devices = range(lax.axis_size(axis))
    route = [(i - distance, i) for i in devices if i - distance in devices]
    return lax.ppermute(block, axis, route)


def on_device(acts, cots, kern, filt, skip):
    rows, feats_all = acts.shape[1:]
    groups = lax.axis_size("ctx")
    chans = filt.shape[1]
    width = groups * chans
    place = lax.axis_index("ctx").astype(jnp.int32)
    me = place[None]

    table, back = (jnp.asarray(one) for one in leaf_tables(rows * groups))
    spectrum = filter_spectrum(filt[0], table)
    gain = lax.dynamic_slice_in_dim(skip, place * chans, chans, axis=1)
    taps = kern[0].reshape(TAPS, 3, groups, chans)
    taps = lax.dynamic_index_in_dim(taps, place, axis=2, keepdims=False).transpose(1, 0, 2)
    taps = jnp.pad(taps, ((0, 0), (0, HALO - TAPS), (0, 0)))
    query_taps = jnp.pad(kern[0, :, :width], ((0, HALO - TAPS), (0, 0)))

    came = handed_over(leaving_pieces(me, acts[0], groups, 2), 0, 1)
    pieces = pieces_for_owners(me, acts[0], came, groups)
    pieces = [handed_over(piece, 1, 2 * chip) for chip, piece in enumerate(pieces)]
    query, incoming = acts[0, :, :width], cots[0]
    query, incoming, pieces[:LATE] = lax.optimization_barrier((query, incoming, pieces[:LATE]))
    query = passed_along(query, "section", 1)
    incoming = passed_along(incoming, "section", -1)

    feats, gated, inner, g_ring = inner_work(me, pieces, spectrum, table, back, taps, gain)
    inner = lax.all_to_all(inner, "ctx", split_axis=0, concat_axis=0, tiled=True)

    before = from_behind(query[rows - HALO :], "ctx", 1)
    later = from_behind(incoming[:HALO], "ctx", -1)
    mix_grad, features = query_features(query, before, incoming, query_taps, groups)
    mix_grad = lax.all_to_all(mix_grad, "ctx", split_axis=0, concat_axis=0, tiled=True)
    output, input_grad, partial = query_outputs(query, incoming, later, features, inner, query_taps)
    partial, mix_grad = lax.optimization_barrier((partial, mix_grad))
    partial = lax.all_to_all(partial, "ctx", split_axis=0, concat_axis=0, tiled=True)
    query_sums = jnp.sum(partial.astype(F32), axis=0)

    ready, d_ring = through_work(me, pieces, mix_grad, feats, spectrum, table, back, taps, gain)
    query_rows = jnp.broadcast_to(query_sums.astype(BF16), (groups, HALO, chans))
    ready = lax.dynamic_update_slice(ready, query_rows, (0, 2 * rows, 0))
    ready = lax.all_to_all(ready, "ctx", split_axis=0, concat_axis=0, tiled=True)
    filt_grad, skip_grad = filter_gradient(mix_grad, gated, d_ring, g_ring, back)
    (input_grad,) = place_columns(ready, rows, ((0, 1), (0, 2)), (input_grad,))
    sums = ready[:, 2 * rows : 2 * rows + 3 * HALO].reshape(groups, 3, HALO, chans)[:, :, :TAPS]
    kern_grad = sums.transpose(2, 1, 0, 3).reshape(TAPS, feats_all).astype(F32)
    return (output[None], input_grad[None], kern_grad[None], filt_grad[None], skip_grad)


def solution(mesh):
    return jax.shard_map(
        on_device,
        mesh=mesh,
        in_specs=(
            P("section", "ctx", None),
            P("section", "ctx", None),
            P("section", None, None),
            P("section", "ctx", None),
            P("section", None),
        ),
        out_specs=(
            P("section", "ctx", None),
            P("section", "ctx", None),
            P("section", None, None),
            P("section", "ctx", None),
            P("section", "ctx"),
        ),
        check_vma=False,
    )
```

```python
import functools
import math

import jax
import jax.numpy as jnp
import ml_dtypes
import numpy as np
from jax import lax
from jax.experimental import pallas as pl
from jax.experimental.pallas import tpu as pltpu
from jax.sharding import PartitionSpec as P

TAPS = 7
HALO = 8
EXTRA = 24
LATE = 6
ROOT = math.sqrt(0.5)
F32 = jnp.float32
BF16 = jnp.bfloat16
MIB = 1 << 20


def in_hbm(*arrays):
    return [pltpu.with_memory_space_constraint(array, pltpu.HBM) for array in arrays]


def passed_along(value, axis, steps):
    count = lax.axis_size(axis)
    pairs = [(source, (source + steps) % count) for source in range(count)]
    return lax.ppermute(value, axis, pairs)


def handed_over(value, steps, partner):
    sections, groups = lax.axis_size("section"), lax.axis_size("ctx")
    pairs = [
        (section * groups + place, (section + steps) % sections * groups + (place ^ partner))
        for section in range(sections)
        for place in range(groups)
    ]
    return lax.ppermute(value, ("section", "ctx"), pairs)


def leaf_angles():
    angles = [math.pi / 2]
    for _ in range(3):
        angles = [half for angle in angles for half in (angle / 2, angle / 2 + math.pi)]
    return angles


def leaf_tables(length):
    leaf = length // 8
    order = np.arange(leaf)
    tables = []
    for angle in leaf_angles():
        phase = (angle + 2.0 * np.pi * order[:, None]) / leaf * order[None, :]
        real, imag = np.cos(phase), np.sin(phase)
        tables.append(np.block([[real, -imag], [imag, real]]))
    table = np.stack(tables)
    back = table.transpose(0, 2, 1) / length
    return table.astype(ml_dtypes.bfloat16), back.astype(ml_dtypes.bfloat16)


def turned(pair, angle):
    real, imag = pair
    cos, sin = math.cos(angle), math.sin(angle)
    return real * cos - imag * sin, real * sin + imag * cos


def split_rings(parts):
    low, high = [], []
    for lower, upper in zip(parts[:4], parts[4:]):
        scaled = upper * ROOT
        low.append((lower + scaled, scaled))
        high.append((lower - scaled, -scaled))
    rings = [(math.pi / 4, low), (math.pi / 4 + math.pi, high)]
    while len(rings[0][1]) > 1:
        finer = []
        for angle, pieces in rings:
            half = len(pieces) // 2
            plus, minus = [], []
            for lower, upper in zip(pieces[:half], pieces[half:]):
                real, imag = turned(upper, angle / 2)
                plus.append((lower[0] + real, lower[1] + imag))
                minus.append((lower[0] - real, lower[1] - imag))
            finer += [(angle / 2, plus), (angle / 2 + math.pi, minus)]
        rings = finer
    return [pieces[0] for _, pieces in rings]


def join_rings(leaves):
    angles = [math.pi / 4, math.pi / 4 + math.pi]
    angles = [half for angle in angles for half in (angle / 2, angle / 2 + math.pi)]
    groups = [[leaf] for leaf in leaves]
    while len(groups) > 2:
        merged = []
        for index in range(0, len(groups), 2):
            angle = angles[index // 2] if len(groups) == 8 else [math.pi / 4, math.pi / 4 + math.pi][index // 2]
            lower, upper = [], []
            for plus, minus in zip(groups[index], groups[index + 1]):
                lower.append((plus[0] + minus[0], plus[1] + minus[1]))
                upper.append(turned((plus[0] - minus[0], plus[1] - minus[1]), -angle / 2))
            merged.append(lower + upper)
        groups = merged
    lower, upper = [], []
    for plus, minus in zip(groups[0], groups[1]):
        lower.append(plus[0] + minus[0])
        upper.append(((plus[0] - minus[0]) + (plus[1] - minus[1])) * ROOT)
    return lower + upper


def filter_kernel(filt_ref, table_ref, spec_ref, rings):
    chans, length = filt_ref.shape
    leaf = length // 8
    step = pl.program_id(0)

    @pl.when(step == 0)
    def _():
        @pl.loop(0, chans // 16)
        def _(strip):
            rows = pl.ds(pl.multiple_of(strip * 16, 16), 16)
            for lane in range(0, leaf, 128):
                parts = [
                    filt_ref[rows, piece * leaf + lane : piece * leaf + lane + 128].astype(F32)
                    for piece in range(8)
                ]
                for index, (real, imag) in enumerate(split_rings(parts)):
                    rings[index, rows, lane : lane + 128] = real.astype(BF16)
                    rings[index, rows, leaf + lane : leaf + lane + 128] = imag.astype(BF16)

    spec_ref[0] = lax.dot_general(
        table_ref[0], rings[step], (((1,), (1,)), ((), ())), preferred_element_type=F32
    )


def filter_spectrum(filt, table):
    chans, length = filt.shape
    wide = length // 4
    return pl.pallas_call(
        filter_kernel,
        out_shape=pltpu.HBM((8, wide, chans), F32),
        grid=(8,),
        in_specs=[
            pl.BlockSpec((chans, length), lambda j: (0, 0)),
            pl.BlockSpec((1, wide, wide), lambda j: (j, 0, 0)),
        ],
        out_specs=pl.BlockSpec((1, wide, chans), lambda j: (j, 0, 0)),
        scratch_shapes=[pltpu.VMEM((8, chans, wide), BF16)],
        compiler_params=pltpu.CompilerParams(vmem_limit_bytes=12 * MIB),
        cost_estimate=pl.CostEstimate(
            flops=16 * wide * wide * chans, bytes_accessed=10 * MIB, transcendentals=0
        ),
        name="filter_spectrum",
    )(*in_hbm(filt, table))


def wait_all(copies):
    for copy in copies:
        copy.start()
    for copy in copies:
        copy.wait()


def leave_kernel(me_ref, wide_ref, leaving_ref, sems):
    chips, roles, _, chans = leaving_ref.shape
    width = wide_ref.shape[1] // 3
    copies = []
    for chip in range(chips):
        start = (me_ref[0] ^ (2 * chip + 1)) * chans
        for role in range(roles):
            columns = pl.ds(pl.multiple_of((role + 1) * width + start, 128), chans)
            copies.append(
                pltpu.make_async_copy(wide_ref.at[:, columns], leaving_ref.at[chip, role], sems.at[chip, role])
            )
    wait_all(copies)


def piece_kernel(me_ref, wide_ref, came_ref, *refs):
    *pieces, sems = refs
    _, roles, _, chans = pieces[0].shape
    width = wide_ref.shape[1] // 3
    copies = []
    for chip, piece in enumerate(pieces):
        start = (me_ref[0] ^ (2 * chip)) * chans
        for role in range(roles):
            columns = pl.ds(pl.multiple_of((role + 1) * width + start, 128), chans)
            copies.append(pltpu.make_async_copy(wide_ref.at[:, columns], piece.at[0, role], sems.at[chip, role]))
        copies.append(pltpu.make_async_copy(came_ref.at[chip], piece.at[1], sems.at[chip, roles]))
    wait_all(copies)


def leaving_pieces(me, wide, groups, roles):
    rows, width = wide.shape
    chans = width // 3 // groups
    return pl.pallas_call(
        leave_kernel,
        out_shape=jax.ShapeDtypeStruct((groups // 2, roles, rows, chans), BF16),
        in_specs=[pl.BlockSpec(memory_space=pltpu.SMEM), pl.BlockSpec(memory_space=pl.ANY)],
        out_specs=pl.BlockSpec(memory_space=pltpu.VMEM),
        scratch_shapes=[pltpu.SemaphoreType.DMA((groups // 2, roles))],
        compiler_params=pltpu.CompilerParams(vmem_limit_bytes=4 * MIB),
        cost_estimate=pl.CostEstimate(flops=0, bytes_accessed=2 * rows * width, transcendentals=0),
        name="leaving_pieces",
    )(me, *in_hbm(wide))


def pieces_for_owners(me, wide, came, groups):
    chips, roles, rows, chans = came.shape
    return pl.pallas_call(
        piece_kernel,
        out_shape=[jax.ShapeDtypeStruct((2, roles, rows, chans), BF16)] * chips,
        in_specs=[pl.BlockSpec(memory_space=pltpu.SMEM), pl.BlockSpec(memory_space=pl.ANY), pl.BlockSpec(memory_space=pltpu.VMEM)],
        out_specs=[pl.BlockSpec(memory_space=pltpu.VMEM)] * chips,
        scratch_shapes=[pltpu.SemaphoreType.DMA((chips, roles + 1))],
        compiler_params=pltpu.CompilerParams(vmem_limit_bytes=8 * MIB),
        cost_estimate=pl.CostEstimate(flops=0, bytes_accessed=8 * chips * roles * rows * chans, transcendentals=0),
        name="pieces_for_owners",
    )(me, *in_hbm(wide), came)


def tap_sum(held, part, taps, row):
    total = taps[0] * held[part, HALO + row : HALO + row + 16, :]
    for tap in range(1, TAPS):
        total = total + taps[tap] * held[part, HALO + row - tap : HALO + row - tap + 16, :]
    return total


def hold(held, part, block):
    rows = block.shape[0]
    held[part, 0:HALO, :] = held[part, rows : rows + HALO, :]
    held[part, HALO:, :] = block.astype(F32)


def tap_rows(taps_ref, role, lanes):
    return [taps_ref[role, tap : tap + 1, lanes] for tap in range(TAPS)]


def split_signal(signal, rings):
    groups, rows, chans = signal.shape
    leaf = groups * rows // 8
    per_piece = leaf // rows

    @pl.loop(0, rows // 16)
    def _(strip):
        inside = pl.ds(pl.multiple_of(strip * 16, 16), 16)
        for part in range(per_piece):
            real_rows = pl.ds(pl.multiple_of(part * rows + strip * 16, 16), 16)
            imag_rows = pl.ds(pl.multiple_of(leaf + part * rows + strip * 16, 16), 16)
            for lane in range(0, chans, 128):
                lanes = slice(lane, lane + 128)
                parts = [signal[piece * per_piece + part, inside, lanes].astype(F32) for piece in range(8)]
                for index, (real, imag) in enumerate(split_rings(parts)):
                    rings[index, real_rows, lanes] = real.astype(BF16)
                    rings[index, imag_rows, lanes] = imag.astype(BF16)


def join_signal(joined, first, rows, place):
    leaf = joined.shape[1] // 2
    per_piece = leaf // rows
    chans = 256 if joined.shape[2] % 256 == 0 else 128

    @pl.loop(0, rows // 16)
    def _(strip):
        inside = pl.ds(pl.multiple_of(strip * 16, 16), 16)
        for part in range(per_piece):
            real_rows = pl.ds(pl.multiple_of(part * rows + strip * 16, 16), 16)
            imag_rows = pl.ds(pl.multiple_of(leaf + part * rows + strip * 16, 16), 16)
            for lane in range(0, chans, 128):
                column = slice(first + lane, first + lane + 128)
                leaves = [
                    (joined[index, real_rows, column], joined[index, imag_rows, column]) for index in range(8)
                ]
                for piece, result in enumerate(join_rings(leaves)):
                    place(piece * per_piece + part, strip, inside, slice(lane, lane + 128), result)


def back_taps(grads, source_block, part, taps, place, sums, role, lanes):
    rows = grads.shape[1] - HALO
    parts = [jnp.zeros((16, 128), F32) for _ in range(TAPS)]
    for row in range(0, rows, 16):
        here = source_block(row).astype(F32)
        total = jnp.zeros((16, 128), F32)
        for tap in range(TAPS):
            ahead = grads[part, row + tap : row + tap + 16, :]
            total = total + taps[tap] * ahead
            parts[tap] = parts[tap] + here * ahead
        place(row, total.astype(BF16))
    for tap in range(TAPS):
        sums[role, tap, :, lanes] += parts[tap][0:8] + parts[tap][8:16]


def sum_rows(sums, roles):
    rows_out = []
    chans = sums.shape[3]
    for role in range(roles):
        for tap in range(TAPS):
            rows_out.append(jnp.sum(sums[role, tap], axis=0, keepdims=True))
        rows_out.append(jnp.zeros((HALO - TAPS, chans), F32))
    return rows_out


def mixed_kernel(groups, me_ref, *refs):
    pieces = refs[: groups // 2]
    spec_hbm, table_hbm, back_hbm, taps_ref, gain_ref = refs[groups // 2 : groups // 2 + 5]
    (
        feats_hbm, gated_hbm, inner_ref, ring_hbm,
        source, spec, table, back, held, feats, gated, rings, products, joined, ring,
        piece_sems, load_sems, feats_sems, gated_sem, ring_sems,
    ) = refs[groups // 2 + 5 :]
    _, _, rows, chans = source.shape
    for partner in range(groups):
        block = me_ref[0] ^ partner
        piece = pieces[partner // 2].at[partner % 2]
        pltpu.make_async_copy(piece, source.at[block], piece_sems.at[block]).start()
    loads = []
    for index in range(8):
        for kind, (from_ref, into) in enumerate(((table_hbm, table), (spec_hbm, spec), (back_hbm, back))):
            loads.append(pltpu.make_async_copy(from_ref.at[index], into.at[index], load_sems.at[kind, index]))
            loads[-1].start()
    held[:, :, rows:, :] = jnp.zeros((2, chans // 128, HALO, 128), F32)

    def feats_copy(block):
        return pltpu.make_async_copy(feats.at[block], feats_hbm.at[block], feats_sems.at[block])

    @pl.loop(0, groups)
    def _(step):
        pltpu.make_async_copy(pieces[0].at[0], source.at[step], piece_sems.at[step]).wait()
        for part in range(chans // 128):
            lanes = slice(part * 128, part * 128 + 128)
            for role in range(2):
                hold(held.at[role], part, source[step, role, :, lanes])
            taps = [tap_rows(taps_ref, role + 1, lanes) for role in range(2)]
            for row in range(0, rows, 16):
                span = slice(row, row + 16)
                keyed, value = [tap_sum(held.at[role], part, taps[role], row) for role in range(2)]
                feats[step, 0, span, lanes] = keyed
                feats[step, 1, span, lanes] = value
                gated[step, span, lanes] = (keyed * value).astype(BF16)
        feats_copy(step).start()

    gated_copy = pltpu.make_async_copy(gated, gated_hbm, gated_sem.at[0])
    gated_copy.start()
    split_signal(gated, rings)
    leaf = spec.shape[1] // 2

    def ring_copy(index):
        return pltpu.make_async_copy(ring.at[index], ring_hbm.at[index], ring_sems.at[index])

    @pl.loop(0, 8)
    def _(index):
        for kind, (from_ref, into) in enumerate(((table_hbm, table), (spec_hbm, spec), (back_hbm, back))):
            pltpu.make_async_copy(from_ref.at[index], into.at[index], load_sems.at[kind, index]).wait()
        ring[index] = jnp.dot(table[index], rings[index], preferred_element_type=F32)
        g_real, g_imag = ring[index, :leaf], ring[index, leaf:]
        f_real, f_imag = spec[index, :leaf], spec[index, leaf:]
        products[:leaf] = (g_real * f_real - g_imag * f_imag).astype(BF16)
        products[leaf:] = (g_real * f_imag + g_imag * f_real).astype(BF16)
        joined[index] = jnp.dot(back[index], products[...], preferred_element_type=F32)
        ring_copy(index).start()

    def place(owner, strip, inside, lanes, result):
        total = result + gain_ref[0:1, lanes] * gated[owner, inside, lanes].astype(F32)
        inner_ref[owner, inside, lanes] = total.astype(BF16)

    join_signal(joined, 0, rows, place)
    for owner in range(groups - 1):
        inner_ref[owner, rows:, :] = inner_ref[owner + 1, 0:HALO, :]
    inner_ref[groups - 1, rows:, :] = jnp.zeros((HALO, chans), BF16)

    @pl.loop(0, groups)
    def _(step):
        feats_copy(step).wait()

    gated_copy.wait()

    @pl.loop(0, 8)
    def _(index):
        ring_copy(index).wait()


def inner_work(me, pieces, spectrum, table, back, taps, gain):
    groups = 2 * len(pieces)
    _, _, rows, chans = pieces[0].shape
    length = groups * rows
    wide = length // 4
    parts = chans // 128
    return pl.pallas_call(
        functools.partial(mixed_kernel, groups),
        out_shape=(
            pltpu.HBM((groups, 2, rows, chans), F32),
            pltpu.HBM((groups, rows, chans), BF16),
            jax.ShapeDtypeStruct((groups, rows + HALO, chans), BF16),
            pltpu.HBM((8, wide, chans), F32),
        ),
        in_specs=[pl.BlockSpec(memory_space=pltpu.SMEM)]
        + [pl.BlockSpec(memory_space=pl.ANY)] * (groups // 2 + 3)
        + [pl.BlockSpec(memory_space=pltpu.VMEM)] * 2,
        out_specs=(
            pl.BlockSpec(memory_space=pl.ANY),
            pl.BlockSpec(memory_space=pl.ANY),
            pl.BlockSpec(memory_space=pltpu.VMEM),
            pl.BlockSpec(memory_space=pl.ANY),
        ),
        scratch_shapes=[
            pltpu.VMEM((groups, 2, rows, chans), BF16),
            pltpu.VMEM((8, wide, chans), F32),
            pltpu.VMEM((8, wide, wide), BF16),
            pltpu.VMEM((8, wide, wide), BF16),
            pltpu.VMEM((2, parts, HALO + rows, 128), F32),
            pltpu.VMEM((groups, 2, rows, chans), F32),
            pltpu.VMEM((groups, rows, chans), BF16),
            pltpu.VMEM((8, wide, chans), BF16),
            pltpu.VMEM((wide, chans), BF16),
            pltpu.VMEM((8, wide, chans), F32),
            pltpu.VMEM((8, wide, chans), F32),
            pltpu.SemaphoreType.DMA((groups,)),
            pltpu.SemaphoreType.DMA((3, 8)),
            pltpu.SemaphoreType.DMA((groups,)),
            pltpu.SemaphoreType.DMA((1,)),
            pltpu.SemaphoreType.DMA((8,)),
        ],
        compiler_params=pltpu.CompilerParams(vmem_limit_bytes=33 * MIB),
        cost_estimate=pl.CostEstimate(
            flops=32 * wide * wide * chans + 60 * length * chans, bytes_accessed=24 * MIB, transcendentals=0
        ),
        name="inner_values",
    )(me, *in_hbm(*pieces, spectrum, table, back), taps, gain)


def query_kernel(
    source, before, incoming, taps_ref, grad_hbm, features_hbm, mix_grad, features, held, grad_sems, features_sems
):
    groups, rows, chans = mix_grad.shape

    def write_back(owner):
        columns = pl.ds(pl.multiple_of(owner * chans, 128), chans)
        return (
            pltpu.make_async_copy(mix_grad.at[owner], grad_hbm.at[owner], grad_sems.at[owner]),
            pltpu.make_async_copy(features.at[:, columns], features_hbm.at[:, columns], features_sems.at[owner]),
        )

    @pl.loop(0, groups)
    def _(owner):
        for part in range(chans // 128):
            columns = pl.ds(pl.multiple_of(owner * chans + part * 128, 128), 128)
            lanes = slice(part * 128, part * 128 + 128)
            held[part, 0:HALO, :] = before[:, columns].astype(F32)
            held[part, HALO:, :] = source[:, columns].astype(F32)
            taps = [taps_ref[tap : tap + 1, columns] for tap in range(TAPS)]
            for row in range(0, rows, 16):
                span = slice(row, row + 16)
                total = tap_sum(held, part, taps, row)
                features[span, columns] = total
                mix_grad[owner, span, lanes] = (incoming[span, columns].astype(F32) * total).astype(BF16)
        for copy in write_back(owner):
            copy.start()

    @pl.loop(0, groups)
    def _(owner):
        for copy in write_back(owner):
            copy.wait()


def query_features(source, before, incoming, taps, groups):
    rows, width = source.shape
    chans = width // groups
    return pl.pallas_call(
        query_kernel,
        out_shape=(
            pltpu.HBM((groups, rows, chans), BF16),
            pltpu.HBM((rows, width), F32),
        ),
        in_specs=[pl.BlockSpec(memory_space=pltpu.VMEM)] * 4,
        out_specs=(pl.BlockSpec(memory_space=pl.ANY),) * 2,
        scratch_shapes=[
            pltpu.VMEM((groups, rows, chans), BF16),
            pltpu.VMEM((rows, width), F32),
            pltpu.VMEM((chans // 128, HALO + rows, 128), F32),
            pltpu.SemaphoreType.DMA((groups,)),
            pltpu.SemaphoreType.DMA((groups,)),
        ],
        compiler_params=pltpu.CompilerParams(vmem_limit_bytes=10 * MIB),
        cost_estimate=pl.CostEstimate(flops=15 * rows * width, bytes_accessed=10 * rows * width, transcendentals=0),
        name="query_features",
    )(source, before, incoming, taps)


def output_kernel(
    source, incoming, later, features, inner, taps_ref, output_hbm, grad_hbm, sums_ref, grads, sums, slots, slot_sems
):
    groups, _, chans = inner.shape
    rows = source.shape[0]

    def write_back(owner, slot):
        columns = pl.ds(pl.multiple_of(owner * chans, 128), chans)
        return [
            pltpu.make_async_copy(slots.at[slot, kind], into.at[:, columns], slot_sems.at[slot, kind])
            for kind, into in enumerate((output_hbm, grad_hbm))
        ]

    @pl.loop(0, groups)
    def _(owner):
        slot = lax.rem(owner, 2)

        @pl.when(owner >= 2)
        def _():
            for copy in write_back(owner - 2, slot):
                copy.wait()

        sums[...] = jnp.zeros_like(sums)
        for part in range(chans // 128):
            columns = pl.ds(pl.multiple_of(owner * chans + part * 128, 128), 128)
            lanes = slice(part * 128, part * 128 + 128)
            for row in range(0, rows, 16):
                span = slice(row, row + 16)
                values = inner[owner, span, lanes].astype(F32)
                grads[part, span, :] = incoming[span, columns].astype(F32) * values
                slots[slot, 0, span, lanes] = (features[span, columns] * values).astype(BF16)
            ahead = inner[owner, rows : rows + HALO, lanes].astype(F32)
            grads[part, rows:, :] = later[:, columns].astype(F32) * ahead

            def place(row, values, lanes=lanes):
                slots[slot, 1, row : row + 16, lanes] = values

            def source_block(row, columns=columns):
                return source[row : row + 16, columns]

            taps = [taps_ref[tap : tap + 1, columns] for tap in range(TAPS)]
            back_taps(grads, source_block, part, taps, place, sums, 0, lanes)
        sums_ref[owner] = jnp.concatenate(sum_rows(sums, 1), axis=0).astype(BF16)
        for copy in write_back(owner, slot):
            copy.start()

    for owner in (groups - 2, groups - 1):
        for copy in write_back(owner, owner % 2):
            copy.wait()


def query_outputs(source, incoming, later, features, inner, taps):
    rows, width = source.shape
    groups, _, chans = inner.shape
    return pl.pallas_call(
        output_kernel,
        out_shape=(
            pltpu.HBM((rows, width), BF16),
            pltpu.HBM((rows, 3 * width), BF16),
            jax.ShapeDtypeStruct((groups, HALO, chans), BF16),
        ),
        in_specs=[pl.BlockSpec(memory_space=pltpu.VMEM)] * 6,
        out_specs=(
            pl.BlockSpec(memory_space=pl.ANY),
            pl.BlockSpec(memory_space=pl.ANY),
            pl.BlockSpec(memory_space=pltpu.VMEM),
        ),
        scratch_shapes=[
            pltpu.VMEM((chans // 128, rows + HALO, 128), F32),
            pltpu.VMEM((1, TAPS, 8, chans), F32),
            pltpu.VMEM((2, 2, rows, chans), BF16),
            pltpu.SemaphoreType.DMA((2, 2)),
        ],
        compiler_params=pltpu.CompilerParams(vmem_limit_bytes=12 * MIB),
        cost_estimate=pl.CostEstimate(flops=35 * rows * width, bytes_accessed=14 * rows * width, transcendentals=0),
        name="query_outputs",
    )(source, incoming, later, features, inner, taps)


def through_kernel(groups, me_ref, *refs):
    pieces = refs[: groups // 2]
    (
        grad_hbm, feats_hbm, spec_hbm, table_hbm, back_hbm, taps_ref, gain_ref,
        ready_hbm, ring_hbm,
        source, mix_grad, feats, spec, ring, table, back, rings, products, joined, through,
        grads, sums, slots, last,
        piece_sems, signal_sem, feats_sems, load_sems, ring_sems, slot_sems, last_sems,
    ) = refs[groups // 2 :]
    _, rows, chans = through.shape
    signal = pltpu.make_async_copy(grad_hbm, mix_grad, signal_sem.at[0])
    signal.start()
    kinds = ((table_hbm, table), (spec_hbm, spec), (back_hbm, back))
    for index in range(8):
        for kind, (from_ref, into) in enumerate(kinds):
            pltpu.make_async_copy(from_ref.at[index], into.at[index], load_sems.at[kind, index]).start()
    for partner in range(groups):
        block = me_ref[0] ^ partner
        piece = pieces[partner // 2].at[partner % 2]
        pltpu.make_async_copy(piece, source.at[block], piece_sems.at[block]).start()

    def feats_copy(block):
        return pltpu.make_async_copy(feats_hbm.at[block], feats.at[block], feats_sems.at[block])

    for block in range(groups):
        feats_copy(block).start()
    grads[:, :, 0:HALO, :] = jnp.zeros((2, chans // 128, HALO, 128), F32)
    sums[...] = jnp.zeros_like(sums)
    signal.wait()
    split_signal(mix_grad, rings)
    leaf = spec.shape[1] // 2

    def ring_copy(index):
        return pltpu.make_async_copy(ring.at[index], ring_hbm.at[index], ring_sems.at[index])

    @pl.loop(0, 8)
    def _(index):
        for kind, (from_ref, into) in enumerate(kinds):
            pltpu.make_async_copy(from_ref.at[index], into.at[index], load_sems.at[kind, index]).wait()
        ring[index] = jnp.dot(table[index], rings[index], preferred_element_type=F32)
        d_real, d_imag = ring[index, :leaf], ring[index, leaf:]
        f_real, f_imag = spec[index, :leaf], spec[index, leaf:]
        products[:leaf] = (d_real * f_real + d_imag * f_imag).astype(BF16)
        products[leaf:] = (d_imag * f_real - d_real * f_imag).astype(BF16)
        joined[index] = jnp.dot(back[index], products[...], preferred_element_type=F32)
        ring_copy(index).start()

    def place_through(owner, strip, inside, lanes, result):
        grad = mix_grad[owner, inside, lanes].astype(F32)
        through[owner, inside, lanes] = (result + gain_ref[0:1, lanes] * grad).astype(BF16)

    join_signal(joined, 0, rows, place_through)

    @pl.loop(0, groups)
    def _(block):
        pltpu.make_async_copy(pieces[0].at[0], source.at[block], piece_sems.at[block]).wait()
        feats_copy(block).wait()

    def write_back(slot_at, block_at):
        return pltpu.make_async_copy(
            slots.at[slot_at], ready_hbm.at[block_at, pl.ds(0, 2 * rows)], slot_sems.at[slot_at]
        )

    @pl.loop(0, groups)
    def _(step):
        block = groups - 1 - step
        slot = lax.rem(step, 2)

        @pl.when(step >= 2)
        def _():
            write_back(slot, block + 2).wait()

        for part in range(chans // 128):
            lanes = slice(part * 128, part * 128 + 128)
            for role in range(2):
                grads[role, part, rows : rows + HALO, :] = grads[role, part, 0:HALO, :]
            for row in range(0, rows, 16):
                span = slice(row, row + 16)
                values = through[block, span, lanes].astype(F32)
                grads[0, part, span, :] = values * feats[block, 1, span, lanes]
                grads[1, part, span, :] = values * feats[block, 0, span, lanes]
            for role in range(2):

                def place(row, values, role=role, lanes=lanes):
                    slots[slot, role * rows + row : role * rows + row + 16, lanes] = values

                def source_block(row, role=role, lanes=lanes):
                    return source[block, role, row : row + 16, lanes]

                taps = tap_rows(taps_ref, role + 1, lanes)
                back_taps(grads.at[role], source_block, part, taps, place, sums, role, lanes)
        write_back(slot, block).start()

    rows_out = [jnp.zeros((HALO, chans), F32)] + sum_rows(sums, 2)
    last[...] = jnp.concatenate(rows_out, axis=0).astype(BF16)
    wait_all(
        [
            pltpu.make_async_copy(last, ready_hbm.at[owner, pl.ds(2 * rows, EXTRA)], last_sems.at[owner])
            for owner in range(groups)
        ]
    )
    write_back(groups % 2, 1).wait()
    write_back((groups + 1) % 2, 0).wait()

    @pl.loop(0, 8)
    def _(index):
        ring_copy(index).wait()


def through_work(me, pieces, mix_grad, feats, spectrum, table, back, taps, gain):
    groups, rows, chans = mix_grad.shape
    length = groups * rows
    wide = length // 4
    parts = chans // 128
    return pl.pallas_call(
        functools.partial(through_kernel, groups),
        out_shape=(
            pltpu.HBM((groups, 2 * rows + EXTRA, chans), BF16),
            pltpu.HBM((8, wide, chans), F32),
        ),
        in_specs=[pl.BlockSpec(memory_space=pltpu.SMEM)]
        + [pl.BlockSpec(memory_space=pl.ANY)] * (groups // 2 + 5)
        + [pl.BlockSpec(memory_space=pltpu.VMEM)] * 2,
        out_specs=(pl.BlockSpec(memory_space=pl.ANY),) * 2,
        scratch_shapes=[
            pltpu.VMEM((groups, 2, rows, chans), BF16),
            pltpu.VMEM((groups, rows, chans), BF16),
            pltpu.VMEM((groups, 2, rows, chans), F32),
            pltpu.VMEM((8, wide, chans), F32),
            pltpu.VMEM((8, wide, chans), F32),
            pltpu.VMEM((8, wide, wide), BF16),
            pltpu.VMEM((8, wide, wide), BF16),
            pltpu.VMEM((8, wide, chans), BF16),
            pltpu.VMEM((wide, chans), BF16),
            pltpu.VMEM((8, wide, chans), F32),
            pltpu.VMEM((groups, rows, chans), BF16),
            pltpu.VMEM((2, parts, rows + HALO, 128), F32),
            pltpu.VMEM((2, TAPS, 8, chans), F32),
            pltpu.VMEM((2, 2 * rows, chans), BF16),
            pltpu.VMEM((EXTRA, chans), BF16),
            pltpu.SemaphoreType.DMA((groups,)),
            pltpu.SemaphoreType.DMA((1,)),
            pltpu.SemaphoreType.DMA((groups,)),
            pltpu.SemaphoreType.DMA((3, 8)),
            pltpu.SemaphoreType.DMA((8,)),
            pltpu.SemaphoreType.DMA((2,)),
            pltpu.SemaphoreType.DMA((groups,)),
        ],
        compiler_params=pltpu.CompilerParams(vmem_limit_bytes=34 * MIB),
        cost_estimate=pl.CostEstimate(
            flops=32 * wide * wide * chans + 100 * length * chans, bytes_accessed=28 * MIB, transcendentals=0
        ),
        name="through_values",
    )(me, *in_hbm(*pieces), mix_grad, *in_hbm(feats, spectrum, table, back), taps, gain)


def filter_grad_kernel(
    grad_hbm, gated_hbm, d_hbm, g_hbm, back_hbm, filt_hbm, skip_ref,
    mix_grad, gated, d_ring, g_ring, back, products, joined, flat, turned_flat, signal_sems, load_sems, filt_sem,
):
    groups, rows, chans = mix_grad.shape
    signals = [
        pltpu.make_async_copy(grad_hbm, mix_grad, signal_sems.at[0]),
        pltpu.make_async_copy(gated_hbm, gated, signal_sems.at[1]),
    ]
    kinds = ((d_hbm, d_ring), (g_hbm, g_ring), (back_hbm, back))
    for index in range(8):
        for kind, (from_ref, into) in enumerate(kinds):
            pltpu.make_async_copy(from_ref.at[index], into.at[index], load_sems.at[kind, index]).start()
    for copy in signals:
        copy.start()
    leaf = d_ring.shape[1] // 2

    @pl.loop(0, 8)
    def _(index):
        for kind, (from_ref, into) in enumerate(kinds):
            pltpu.make_async_copy(from_ref.at[index], into.at[index], load_sems.at[kind, index]).wait()
        d_real, d_imag = d_ring[index, :leaf], d_ring[index, leaf:]
        g_real, g_imag = g_ring[index, :leaf], g_ring[index, leaf:]
        products[:leaf] = (d_real * g_real + d_imag * g_imag).astype(BF16)
        products[leaf:] = (d_imag * g_real - d_real * g_imag).astype(BF16)
        joined[index] = jnp.dot(back[index], products[...], preferred_element_type=F32)

    for copy in signals:
        copy.wait()
    skip_ref[...] = jnp.zeros_like(skip_ref)

    @pl.loop(0, groups)
    def _(block):
        for lane in range(0, chans, 128):
            lanes = slice(lane, lane + 128)
            total = jnp.zeros((16, 128), F32)
            for row in range(0, rows, 16):
                span = slice(row, row + 16)
                total = total + mix_grad[block, span, lanes].astype(F32) * gated[block, span, lanes].astype(F32)
            skip_ref[0:1, lanes] += jnp.sum(total, axis=0, keepdims=True)

    def place_filter(owner, strip, inside, lanes, result):
        flat[pl.ds(pl.multiple_of(owner * rows + strip * 16, 16), 16), lanes] = result

    join_signal(joined, 0, rows, place_filter)
    for block in range(groups):
        span = slice(block * rows, (block + 1) * rows)
        turned_flat[:, span] = flat[span, :].T
    wait_all([pltpu.make_async_copy(turned_flat, filt_hbm, filt_sem.at[0])])


def filter_gradient(mix_grad, gated, d_ring, g_ring, back):
    groups, rows, chans = mix_grad.shape
    length = groups * rows
    wide = length // 4
    return pl.pallas_call(
        filter_grad_kernel,
        out_shape=(pltpu.HBM((chans, length), F32), jax.ShapeDtypeStruct((1, chans), F32)),
        in_specs=[pl.BlockSpec(memory_space=pl.ANY)] * 5,
        out_specs=(pl.BlockSpec(memory_space=pl.ANY), pl.BlockSpec(memory_space=pltpu.VMEM)),
        scratch_shapes=[
            pltpu.VMEM((groups, rows, chans), BF16),
            pltpu.VMEM((groups, rows, chans), BF16),
            pltpu.VMEM((8, wide, chans), F32),
            pltpu.VMEM((8, wide, chans), F32),
            pltpu.VMEM((8, wide, wide), BF16),
            pltpu.VMEM((wide, chans), BF16),
            pltpu.VMEM((8, wide, chans), F32),
            pltpu.VMEM((length, chans), F32),
            pltpu.VMEM((chans, length), F32),
            pltpu.SemaphoreType.DMA((2,)),
            pltpu.SemaphoreType.DMA((3, 8)),
            pltpu.SemaphoreType.DMA((1,)),
        ],
        compiler_params=pltpu.CompilerParams(vmem_limit_bytes=28 * MIB),
        cost_estimate=pl.CostEstimate(
            flops=16 * wide * wide * chans + 40 * length * chans, bytes_accessed=16 * MIB, transcendentals=0
        ),
        name="filter_gradient",
    )(mix_grad, *in_hbm(gated, d_ring, g_ring, back))


def place_kernel(columns, held_ref, *refs):
    *wide_refs, sems = refs
    groups, _, chans = held_ref.shape
    rows = wide_refs[-1].shape[0]
    wide_refs = wide_refs[-1 - max(index for index, _ in columns) :]
    copies = []
    for owner in range(groups):
        for kind, (index, first) in enumerate(columns):
            copies.append(
                pltpu.make_async_copy(
                    held_ref.at[owner, pl.ds(kind * rows, rows)],
                    wide_refs[index].at[:, pl.ds(first * groups * chans + owner * chans, chans)],
                    sems.at[owner, kind],
                )
            )
    wait_all(copies)


def place_columns(held, rows, columns, earlier):
    groups, _, chans = held.shape
    width = groups * chans
    shapes = [(rows, 3 * width)]
    return pl.pallas_call(
        functools.partial(place_kernel, columns),
        input_output_aliases={1: 0} if earlier else {},
        out_shape=[pltpu.HBM(shape, BF16) for shape in shapes],
        in_specs=[pl.BlockSpec(memory_space=pltpu.VMEM)] + [pl.BlockSpec(memory_space=pl.ANY)] * len(earlier),
        out_specs=[pl.BlockSpec(memory_space=pl.ANY)] * len(shapes),
        scratch_shapes=[pltpu.SemaphoreType.DMA((groups, 2))],
        compiler_params=pltpu.CompilerParams(vmem_limit_bytes=6 * MIB),
        cost_estimate=pl.CostEstimate(flops=0, bytes_accessed=8 * rows * width, transcendentals=0),
        name="place_columns",
    )(held, *in_hbm(*earlier))


def edge_of(block, steps):
    sections, groups = lax.axis_size("section"), lax.axis_size("ctx")
    pairs = [
        (section * groups + place, (section + steps) % sections * groups + place + steps)
        for section in range(sections)
        for place in range(groups)
        if 0 <= place + steps < groups
    ]
    return lax.ppermute(block, ("section", "ctx"), pairs)


def on_device(acts, cots, kern, filt, skip):
    rows, feats_all = acts.shape[1:]
    groups = lax.axis_size("ctx")
    chans = filt.shape[1]
    width = groups * chans
    place = lax.axis_index("ctx").astype(jnp.int32)
    me = place[None]

    table, back = (jnp.asarray(one) for one in leaf_tables(rows * groups))
    spectrum = filter_spectrum(filt[0], table)
    gain = lax.dynamic_slice_in_dim(skip, place * chans, chans, axis=1)
    taps = kern[0].reshape(TAPS, 3, groups, chans)
    taps = lax.dynamic_index_in_dim(taps, place, axis=2, keepdims=False).transpose(1, 0, 2)
    taps = jnp.pad(taps, ((0, 0), (0, HALO - TAPS), (0, 0)))
    query_taps = jnp.pad(kern[0, :, :width], ((0, HALO - TAPS), (0, 0)))

    came = handed_over(leaving_pieces(me, acts[0], groups, 2), 0, 1)
    pieces = pieces_for_owners(me, acts[0], came, groups)
    pieces = [handed_over(piece, 1, 2 * chip) for chip, piece in enumerate(pieces)]
    query, incoming = acts[0, :, :width], cots[0]
    query, incoming, pieces[:LATE] = lax.optimization_barrier((query, incoming, pieces[:LATE]))
    query = passed_along(query, "section", 1)
    incoming = passed_along(incoming, "section", -1)

    feats, gated, inner, g_ring = inner_work(me, pieces, spectrum, table, back, taps, gain)
    inner = lax.all_to_all(inner, "ctx", split_axis=0, concat_axis=0, tiled=True)

    before = edge_of(acts[0, rows - HALO :, :width], 1)
    later = edge_of(cots[0, :HALO], -1)
    before, later = lax.optimization_barrier((before, later))
    mix_grad, features = query_features(query, before, incoming, query_taps, groups)
    mix_grad = lax.all_to_all(mix_grad, "ctx", split_axis=0, concat_axis=0, tiled=True)
    output, input_grad, partial = query_outputs(query, incoming, later, features, inner, query_taps)
    partial, mix_grad = lax.optimization_barrier((partial, mix_grad))
    partial = lax.all_to_all(partial, "ctx", split_axis=0, concat_axis=0, tiled=True)
    query_sums = jnp.sum(partial.astype(F32), axis=0)

    ready, d_ring = through_work(me, pieces, mix_grad, feats, spectrum, table, back, taps, gain)
    query_rows = jnp.broadcast_to(query_sums.astype(BF16), (groups, HALO, chans))
    ready = lax.dynamic_update_slice(ready, query_rows, (0, 2 * rows, 0))
    ready = lax.all_to_all(ready, "ctx", split_axis=0, concat_axis=0, tiled=True)
    filt_grad, skip_grad = filter_gradient(mix_grad, gated, d_ring, g_ring, back)
    (input_grad,) = place_columns(ready, rows, ((0, 1), (0, 2)), (input_grad,))
    sums = ready[:, 2 * rows : 2 * rows + 3 * HALO].reshape(groups, 3, HALO, chans)[:, :, :TAPS]
    kern_grad = sums.transpose(2, 1, 0, 3).reshape(TAPS, feats_all).astype(F32)
    return (output[None], input_grad[None], kern_grad[None], filt_grad[None], skip_grad)


def solution(mesh):
    return jax.shard_map(
        on_device,
        mesh=mesh,
        in_specs=(
            P("section", "ctx", None),
            P("section", "ctx", None),
            P("section", None, None),
            P("section", "ctx", None),
            P("section", None),
        ),
        out_specs=(
            P("section", "ctx", None),
            P("section", "ctx", None),
            P("section", None, None),
            P("section", "ctx", None),
            P("section", "ctx"),
        ),
        check_vma=False,
    )
```

```python
import functools
import math

import jax
import jax.numpy as jnp
import ml_dtypes
import numpy as np
from jax import lax
from jax.experimental import pallas as pl
from jax.experimental.pallas import tpu as pltpu
from jax.sharding import PartitionSpec as P

TAPS = 7
HALO = 8
EXTRA = 24
LATE = 3
ROOT = math.sqrt(0.5)
F32 = jnp.float32
BF16 = jnp.bfloat16
MIB = 1 << 20


def in_hbm(*arrays):
    return [pltpu.with_memory_space_constraint(array, pltpu.HBM) for array in arrays]


def passed_along(value, axis, steps):
    count = lax.axis_size(axis)
    pairs = [(source, (source + steps) % count) for source in range(count)]
    return lax.ppermute(value, axis, pairs)


def handed_over(value, steps, partner):
    sections, groups = lax.axis_size("section"), lax.axis_size("ctx")
    pairs = [
        (section * groups + place, (section + steps) % sections * groups + (place ^ partner))
        for section in range(sections)
        for place in range(groups)
    ]
    return lax.ppermute(value, ("section", "ctx"), pairs)


def leaf_angles():
    angles = [math.pi / 2]
    for _ in range(3):
        angles = [half for angle in angles for half in (angle / 2, angle / 2 + math.pi)]
    return angles


def leaf_tables(length):
    leaf = length // 8
    order = np.arange(leaf)
    tables = []
    for angle in leaf_angles():
        phase = (angle + 2.0 * np.pi * order[:, None]) / leaf * order[None, :]
        real, imag = np.cos(phase), np.sin(phase)
        tables.append(np.block([[real, -imag], [imag, real]]))
    table = np.stack(tables)
    back = table.transpose(0, 2, 1) / length
    return table.astype(ml_dtypes.bfloat16), back.astype(ml_dtypes.bfloat16)


def turned(pair, angle):
    real, imag = pair
    cos, sin = math.cos(angle), math.sin(angle)
    return real * cos - imag * sin, real * sin + imag * cos


def split_rings(parts):
    low, high = [], []
    for lower, upper in zip(parts[:4], parts[4:]):
        scaled = upper * ROOT
        low.append((lower + scaled, scaled))
        high.append((lower - scaled, -scaled))
    rings = [(math.pi / 4, low), (math.pi / 4 + math.pi, high)]
    while len(rings[0][1]) > 1:
        finer = []
        for angle, pieces in rings:
            half = len(pieces) // 2
            plus, minus = [], []
            for lower, upper in zip(pieces[:half], pieces[half:]):
                real, imag = turned(upper, angle / 2)
                plus.append((lower[0] + real, lower[1] + imag))
                minus.append((lower[0] - real, lower[1] - imag))
            finer += [(angle / 2, plus), (angle / 2 + math.pi, minus)]
        rings = finer
    return [pieces[0] for _, pieces in rings]


def join_rings(leaves):
    angles = [math.pi / 4, math.pi / 4 + math.pi]
    angles = [half for angle in angles for half in (angle / 2, angle / 2 + math.pi)]
    groups = [[leaf] for leaf in leaves]
    while len(groups) > 2:
        merged = []
        for index in range(0, len(groups), 2):
            angle = angles[index // 2] if len(groups) == 8 else [math.pi / 4, math.pi / 4 + math.pi][index // 2]
            lower, upper = [], []
            for plus, minus in zip(groups[index], groups[index + 1]):
                lower.append((plus[0] + minus[0], plus[1] + minus[1]))
                upper.append(turned((plus[0] - minus[0], plus[1] - minus[1]), -angle / 2))
            merged.append(lower + upper)
        groups = merged
    lower, upper = [], []
    for plus, minus in zip(groups[0], groups[1]):
        lower.append(plus[0] + minus[0])
        upper.append(((plus[0] - minus[0]) + (plus[1] - minus[1])) * ROOT)
    return lower + upper


def filter_kernel(filt_ref, table_ref, spec_ref, rings):
    chans, length = filt_ref.shape
    leaf = length // 8
    step = pl.program_id(0)

    @pl.when(step == 0)
    def _():
        @pl.loop(0, chans // 16)
        def _(strip):
            rows = pl.ds(pl.multiple_of(strip * 16, 16), 16)
            for lane in range(0, leaf, 128):
                parts = [
                    filt_ref[rows, piece * leaf + lane : piece * leaf + lane + 128].astype(F32)
                    for piece in range(8)
                ]
                for index, (real, imag) in enumerate(split_rings(parts)):
                    rings[index, rows, lane : lane + 128] = real.astype(BF16)
                    rings[index, rows, leaf + lane : leaf + lane + 128] = imag.astype(BF16)

    spec_ref[0] = lax.dot_general(
        table_ref[0], rings[step], (((1,), (1,)), ((), ())), preferred_element_type=F32
    )


def filter_spectrum(filt, table):
    chans, length = filt.shape
    wide = length // 4
    return pl.pallas_call(
        filter_kernel,
        out_shape=pltpu.HBM((8, wide, chans), F32),
        grid=(8,),
        in_specs=[
            pl.BlockSpec((chans, length), lambda j: (0, 0)),
            pl.BlockSpec((1, wide, wide), lambda j: (j, 0, 0)),
        ],
        out_specs=pl.BlockSpec((1, wide, chans), lambda j: (j, 0, 0)),
        scratch_shapes=[pltpu.VMEM((8, chans, wide), BF16)],
        compiler_params=pltpu.CompilerParams(vmem_limit_bytes=12 * MIB),
        cost_estimate=pl.CostEstimate(
            flops=16 * wide * wide * chans, bytes_accessed=10 * MIB, transcendentals=0
        ),
        name="filter_spectrum",
    )(*in_hbm(filt, table))


def wait_all(copies):
    for copy in copies:
        copy.start()
    for copy in copies:
        copy.wait()


def leave_kernel(me_ref, wide_ref, leaving_ref, sems):
    chips, roles, _, chans = leaving_ref.shape
    width = wide_ref.shape[1] // 3
    copies = []
    for chip in range(chips):
        start = (me_ref[0] ^ (2 * chip + 1)) * chans
        for role in range(roles):
            columns = pl.ds(pl.multiple_of((role + 1) * width + start, 128), chans)
            copies.append(
                pltpu.make_async_copy(wide_ref.at[:, columns], leaving_ref.at[chip, role], sems.at[chip, role])
            )
    wait_all(copies)


def piece_kernel(me_ref, wide_ref, came_ref, query_ref, *refs):
    *pieces, sems, query_sem = refs
    _, roles, _, chans = pieces[0].shape
    width = wide_ref.shape[1] // 3
    copies = [pltpu.make_async_copy(wide_ref.at[:, pl.ds(0, width)], query_ref, query_sem.at[0])]
    for chip, piece in enumerate(pieces):
        start = (me_ref[0] ^ (2 * chip)) * chans
        for role in range(roles):
            columns = pl.ds(pl.multiple_of((role + 1) * width + start, 128), chans)
            copies.append(pltpu.make_async_copy(wide_ref.at[:, columns], piece.at[0, role], sems.at[chip, role]))
        copies.append(pltpu.make_async_copy(came_ref.at[chip], piece.at[1], sems.at[chip, roles]))
    wait_all(copies)


def leaving_pieces(me, wide, groups, roles):
    rows, width = wide.shape
    chans = width // 3 // groups
    return pl.pallas_call(
        leave_kernel,
        out_shape=jax.ShapeDtypeStruct((groups // 2, roles, rows, chans), BF16),
        in_specs=[pl.BlockSpec(memory_space=pltpu.SMEM), pl.BlockSpec(memory_space=pl.ANY)],
        out_specs=pl.BlockSpec(memory_space=pltpu.VMEM),
        scratch_shapes=[pltpu.SemaphoreType.DMA((groups // 2, roles))],
        compiler_params=pltpu.CompilerParams(vmem_limit_bytes=4 * MIB),
        cost_estimate=pl.CostEstimate(flops=0, bytes_accessed=2 * rows * width, transcendentals=0),
        name="leaving_pieces",
    )(me, *in_hbm(wide))


def pieces_for_owners(me, wide, came, groups):
    chips, roles, rows, chans = came.shape
    return pl.pallas_call(
        piece_kernel,
        out_shape=[jax.ShapeDtypeStruct((rows, wide.shape[1] // 3), BF16)]
        + [jax.ShapeDtypeStruct((2, roles, rows, chans), BF16)] * chips,
        in_specs=[pl.BlockSpec(memory_space=pltpu.SMEM), pl.BlockSpec(memory_space=pl.ANY), pl.BlockSpec(memory_space=pltpu.VMEM)],
        out_specs=[pl.BlockSpec(memory_space=pltpu.VMEM)] * (chips + 1),
        scratch_shapes=[pltpu.SemaphoreType.DMA((chips, roles + 1)), pltpu.SemaphoreType.DMA((1,))],
        compiler_params=pltpu.CompilerParams(vmem_limit_bytes=8 * MIB),
        cost_estimate=pl.CostEstimate(flops=0, bytes_accessed=8 * chips * roles * rows * chans, transcendentals=0),
        name="pieces_for_owners",
    )(me, *in_hbm(wide), came)


def tap_sum(held, part, taps, row):
    total = taps[0] * held[part, HALO + row : HALO + row + 16, :]
    for tap in range(1, TAPS):
        total = total + taps[tap] * held[part, HALO + row - tap : HALO + row - tap + 16, :]
    return total


def hold(held, part, block):
    rows = block.shape[0]
    held[part, 0:HALO, :] = held[part, rows : rows + HALO, :]
    held[part, HALO:, :] = block.astype(F32)


def tap_rows(taps_ref, role, lanes):
    return [taps_ref[role, tap : tap + 1, lanes] for tap in range(TAPS)]


def split_signal(signal, rings):
    groups, rows, chans = signal.shape
    leaf = groups * rows // 8
    per_piece = leaf // rows

    @pl.loop(0, rows // 16)
    def _(strip):
        inside = pl.ds(pl.multiple_of(strip * 16, 16), 16)
        for part in range(per_piece):
            real_rows = pl.ds(pl.multiple_of(part * rows + strip * 16, 16), 16)
            imag_rows = pl.ds(pl.multiple_of(leaf + part * rows + strip * 16, 16), 16)
            for lane in range(0, chans, 128):
                lanes = slice(lane, lane + 128)
                parts = [signal[piece * per_piece + part, inside, lanes].astype(F32) for piece in range(8)]
                for index, (real, imag) in enumerate(split_rings(parts)):
                    rings[index, real_rows, lanes] = real.astype(BF16)
                    rings[index, imag_rows, lanes] = imag.astype(BF16)


def join_signal(joined, first, rows, place):
    leaf = joined.shape[1] // 2
    per_piece = leaf // rows
    chans = 256 if joined.shape[2] % 256 == 0 else 128

    @pl.loop(0, rows // 16)
    def _(strip):
        inside = pl.ds(pl.multiple_of(strip * 16, 16), 16)
        for part in range(per_piece):
            real_rows = pl.ds(pl.multiple_of(part * rows + strip * 16, 16), 16)
            imag_rows = pl.ds(pl.multiple_of(leaf + part * rows + strip * 16, 16), 16)
            for lane in range(0, chans, 128):
                column = slice(first + lane, first + lane + 128)
                leaves = [
                    (joined[index, real_rows, column], joined[index, imag_rows, column]) for index in range(8)
                ]
                for piece, result in enumerate(join_rings(leaves)):
                    place(piece * per_piece + part, strip, inside, slice(lane, lane + 128), result)


def back_taps(grads, source_block, part, taps, place, sums, role, lanes):
    rows = grads.shape[1] - HALO
    parts = [jnp.zeros((16, 128), F32) for _ in range(TAPS)]
    for row in range(0, rows, 16):
        here = source_block(row).astype(F32)
        total = jnp.zeros((16, 128), F32)
        for tap in range(TAPS):
            ahead = grads[part, row + tap : row + tap + 16, :]
            total = total + taps[tap] * ahead
            parts[tap] = parts[tap] + here * ahead
        place(row, total.astype(BF16))
    for tap in range(TAPS):
        sums[role, tap, :, lanes] += parts[tap][0:8] + parts[tap][8:16]


def sum_rows(sums, roles):
    rows_out = []
    chans = sums.shape[3]
    for role in range(roles):
        for tap in range(TAPS):
            rows_out.append(jnp.sum(sums[role, tap], axis=0, keepdims=True))
        rows_out.append(jnp.zeros((HALO - TAPS, chans), F32))
    return rows_out


def mixed_kernel(groups, me_ref, *refs):
    pieces = refs[: groups // 2]
    spec_hbm, table_hbm, back_hbm, taps_ref, gain_ref = refs[groups // 2 : groups // 2 + 5]
    (
        feats_hbm, gated_hbm, inner_ref, ring_hbm,
        source, spec, table, back, held, feats, gated, rings, products, joined, ring,
        piece_sems, load_sems, feats_sems, gated_sem, ring_sems,
    ) = refs[groups // 2 + 5 :]
    _, _, rows, chans = source.shape
    for partner in range(groups):
        block = me_ref[0] ^ partner
        piece = pieces[partner // 2].at[partner % 2]
        pltpu.make_async_copy(piece, source.at[block], piece_sems.at[block]).start()
    loads = []
    for index in range(8):
        for kind, (from_ref, into) in enumerate(((table_hbm, table), (spec_hbm, spec), (back_hbm, back))):
            loads.append(pltpu.make_async_copy(from_ref.at[index], into.at[index], load_sems.at[kind, index]))
            loads[-1].start()
    held[:, :, rows:, :] = jnp.zeros((2, chans // 128, HALO, 128), F32)

    def feats_copy(block):
        return pltpu.make_async_copy(feats.at[block], feats_hbm.at[block], feats_sems.at[block])

    @pl.loop(0, groups)
    def _(step):
        pltpu.make_async_copy(pieces[0].at[0], source.at[step], piece_sems.at[step]).wait()
        for part in range(chans // 128):
            lanes = slice(part * 128, part * 128 + 128)
            for role in range(2):
                hold(held.at[role], part, source[step, role, :, lanes])
            taps = [tap_rows(taps_ref, role + 1, lanes) for role in range(2)]
            for row in range(0, rows, 16):
                span = slice(row, row + 16)
                keyed, value = [tap_sum(held.at[role], part, taps[role], row) for role in range(2)]
                feats[step, 0, span, lanes] = keyed
                feats[step, 1, span, lanes] = value
                gated[step, span, lanes] = (keyed * value).astype(BF16)
        feats_copy(step).start()

    gated_copy = pltpu.make_async_copy(gated, gated_hbm, gated_sem.at[0])
    gated_copy.start()
    split_signal(gated, rings)
    leaf = spec.shape[1] // 2

    def ring_copy(index):
        return pltpu.make_async_copy(ring.at[index], ring_hbm.at[index], ring_sems.at[index])

    @pl.loop(0, 8)
    def _(index):
        for kind, (from_ref, into) in enumerate(((table_hbm, table), (spec_hbm, spec), (back_hbm, back))):
            pltpu.make_async_copy(from_ref.at[index], into.at[index], load_sems.at[kind, index]).wait()
        ring[index] = jnp.dot(table[index], rings[index], preferred_element_type=F32)
        g_real, g_imag = ring[index, :leaf], ring[index, leaf:]
        f_real, f_imag = spec[index, :leaf], spec[index, leaf:]
        products[:leaf] = (g_real * f_real - g_imag * f_imag).astype(BF16)
        products[leaf:] = (g_real * f_imag + g_imag * f_real).astype(BF16)
        joined[index] = jnp.dot(back[index], products[...], preferred_element_type=F32)
        ring_copy(index).start()

    def place(owner, strip, inside, lanes, result):
        total = result + gain_ref[0:1, lanes] * gated[owner, inside, lanes].astype(F32)
        inner_ref[owner, inside, lanes] = total.astype(BF16)

    join_signal(joined, 0, rows, place)
    for owner in range(groups - 1):
        inner_ref[owner, rows:, :] = inner_ref[owner + 1, 0:HALO, :]
    inner_ref[groups - 1, rows:, :] = jnp.zeros((HALO, chans), BF16)

    @pl.loop(0, groups)
    def _(step):
        feats_copy(step).wait()

    gated_copy.wait()

    @pl.loop(0, 8)
    def _(index):
        ring_copy(index).wait()


def inner_work(me, pieces, spectrum, table, back, taps, gain):
    groups = 2 * len(pieces)
    _, _, rows, chans = pieces[0].shape
    length = groups * rows
    wide = length // 4
    parts = chans // 128
    return pl.pallas_call(
        functools.partial(mixed_kernel, groups),
        out_shape=(
            pltpu.HBM((groups, 2, rows, chans), F32),
            pltpu.HBM((groups, rows, chans), BF16),
            jax.ShapeDtypeStruct((groups, rows + HALO, chans), BF16),
            pltpu.HBM((8, wide, chans), F32),
        ),
        in_specs=[pl.BlockSpec(memory_space=pltpu.SMEM)]
        + [pl.BlockSpec(memory_space=pl.ANY)] * (groups // 2 + 3)
        + [pl.BlockSpec(memory_space=pltpu.VMEM)] * 2,
        out_specs=(
            pl.BlockSpec(memory_space=pl.ANY),
            pl.BlockSpec(memory_space=pl.ANY),
            pl.BlockSpec(memory_space=pltpu.VMEM),
            pl.BlockSpec(memory_space=pl.ANY),
        ),
        scratch_shapes=[
            pltpu.VMEM((groups, 2, rows, chans), BF16),
            pltpu.VMEM((8, wide, chans), F32),
            pltpu.VMEM((8, wide, wide), BF16),
            pltpu.VMEM((8, wide, wide), BF16),
            pltpu.VMEM((2, parts, HALO + rows, 128), F32),
            pltpu.VMEM((groups, 2, rows, chans), F32),
            pltpu.VMEM((groups, rows, chans), BF16),
            pltpu.VMEM((8, wide, chans), BF16),
            pltpu.VMEM((wide, chans), BF16),
            pltpu.VMEM((8, wide, chans), F32),
            pltpu.VMEM((8, wide, chans), F32),
            pltpu.SemaphoreType.DMA((groups,)),
            pltpu.SemaphoreType.DMA((3, 8)),
            pltpu.SemaphoreType.DMA((groups,)),
            pltpu.SemaphoreType.DMA((1,)),
            pltpu.SemaphoreType.DMA((8,)),
        ],
        compiler_params=pltpu.CompilerParams(vmem_limit_bytes=33 * MIB),
        cost_estimate=pl.CostEstimate(
            flops=32 * wide * wide * chans + 60 * length * chans, bytes_accessed=24 * MIB, transcendentals=0
        ),
        name="inner_values",
    )(me, *in_hbm(*pieces, spectrum, table, back), taps, gain)


def query_kernel(
    source, before, incoming, taps_ref, grad_hbm, features_hbm, mix_grad, features, held, grad_sems, features_sems
):
    groups, rows, chans = mix_grad.shape

    def write_back(owner):
        columns = pl.ds(pl.multiple_of(owner * chans, 128), chans)
        return (
            pltpu.make_async_copy(mix_grad.at[owner], grad_hbm.at[owner], grad_sems.at[owner]),
            pltpu.make_async_copy(features.at[:, columns], features_hbm.at[:, columns], features_sems.at[owner]),
        )

    @pl.loop(0, groups)
    def _(owner):
        for part in range(chans // 128):
            columns = pl.ds(pl.multiple_of(owner * chans + part * 128, 128), 128)
            lanes = slice(part * 128, part * 128 + 128)
            held[part, 0:HALO, :] = before[:, columns].astype(F32)
            held[part, HALO:, :] = source[:, columns].astype(F32)
            taps = [taps_ref[tap : tap + 1, columns] for tap in range(TAPS)]
            for row in range(0, rows, 16):
                span = slice(row, row + 16)
                total = tap_sum(held, part, taps, row)
                features[span, columns] = total
                mix_grad[owner, span, lanes] = (incoming[span, columns].astype(F32) * total).astype(BF16)
        for copy in write_back(owner):
            copy.start()

    @pl.loop(0, groups)
    def _(owner):
        for copy in write_back(owner):
            copy.wait()


def query_features(source, before, incoming, taps, groups):
    rows, width = source.shape
    chans = width // groups
    return pl.pallas_call(
        query_kernel,
        out_shape=(
            pltpu.HBM((groups, rows, chans), BF16),
            pltpu.HBM((rows, width), F32),
        ),
        in_specs=[pl.BlockSpec(memory_space=pltpu.VMEM)] * 4,
        out_specs=(pl.BlockSpec(memory_space=pl.ANY),) * 2,
        scratch_shapes=[
            pltpu.VMEM((groups, rows, chans), BF16),
            pltpu.VMEM((rows, width), F32),
            pltpu.VMEM((chans // 128, HALO + rows, 128), F32),
            pltpu.SemaphoreType.DMA((groups,)),
            pltpu.SemaphoreType.DMA((groups,)),
        ],
        compiler_params=pltpu.CompilerParams(vmem_limit_bytes=10 * MIB),
        cost_estimate=pl.CostEstimate(flops=15 * rows * width, bytes_accessed=10 * rows * width, transcendentals=0),
        name="query_features",
    )(source, before, incoming, taps)


def output_kernel(
    source, incoming, later, features, inner, taps_ref, output_hbm, grad_hbm, sums_ref, grads, sums, slots, slot_sems
):
    groups, _, chans = inner.shape
    rows = source.shape[0]

    def write_back(owner, slot):
        columns = pl.ds(pl.multiple_of(owner * chans, 128), chans)
        return [
            pltpu.make_async_copy(slots.at[slot, kind], into.at[:, columns], slot_sems.at[slot, kind])
            for kind, into in enumerate((output_hbm, grad_hbm))
        ]

    @pl.loop(0, groups)
    def _(owner):
        slot = lax.rem(owner, 2)

        @pl.when(owner >= 2)
        def _():
            for copy in write_back(owner - 2, slot):
                copy.wait()

        sums[...] = jnp.zeros_like(sums)
        for part in range(chans // 128):
            columns = pl.ds(pl.multiple_of(owner * chans + part * 128, 128), 128)
            lanes = slice(part * 128, part * 128 + 128)
            for row in range(0, rows, 16):
                span = slice(row, row + 16)
                values = inner[owner, span, lanes].astype(F32)
                grads[part, span, :] = incoming[span, columns].astype(F32) * values
                slots[slot, 0, span, lanes] = (features[span, columns] * values).astype(BF16)
            ahead = inner[owner, rows : rows + HALO, lanes].astype(F32)
            grads[part, rows:, :] = later[:, columns].astype(F32) * ahead

            def place(row, values, lanes=lanes):
                slots[slot, 1, row : row + 16, lanes] = values

            def source_block(row, columns=columns):
                return source[row : row + 16, columns]

            taps = [taps_ref[tap : tap + 1, columns] for tap in range(TAPS)]
            back_taps(grads, source_block, part, taps, place, sums, 0, lanes)
        sums_ref[owner] = jnp.concatenate(sum_rows(sums, 1), axis=0).astype(BF16)
        for copy in write_back(owner, slot):
            copy.start()

    for owner in (groups - 2, groups - 1):
        for copy in write_back(owner, owner % 2):
            copy.wait()


def query_outputs(source, incoming, later, features, inner, taps):
    rows, width = source.shape
    groups, _, chans = inner.shape
    return pl.pallas_call(
        output_kernel,
        out_shape=(
            pltpu.HBM((rows, width), BF16),
            pltpu.HBM((rows, 3 * width), BF16),
            jax.ShapeDtypeStruct((groups, HALO, chans), BF16),
        ),
        in_specs=[pl.BlockSpec(memory_space=pltpu.VMEM)] * 6,
        out_specs=(
            pl.BlockSpec(memory_space=pl.ANY),
            pl.BlockSpec(memory_space=pl.ANY),
            pl.BlockSpec(memory_space=pltpu.VMEM),
        ),
        scratch_shapes=[
            pltpu.VMEM((chans // 128, rows + HALO, 128), F32),
            pltpu.VMEM((1, TAPS, 8, chans), F32),
            pltpu.VMEM((2, 2, rows, chans), BF16),
            pltpu.SemaphoreType.DMA((2, 2)),
        ],
        compiler_params=pltpu.CompilerParams(vmem_limit_bytes=12 * MIB),
        cost_estimate=pl.CostEstimate(flops=35 * rows * width, bytes_accessed=14 * rows * width, transcendentals=0),
        name="query_outputs",
    )(source, incoming, later, features, inner, taps)


def through_kernel(groups, me_ref, *refs):
    pieces = refs[: groups // 2]
    (
        grad_hbm, feats_hbm, spec_hbm, table_hbm, back_hbm, taps_ref, gain_ref,
        ready_hbm, ring_hbm,
        source, mix_grad, feats, spec, ring, table, back, rings, products, joined, through,
        grads, sums, slots, last,
        piece_sems, signal_sem, feats_sems, load_sems, ring_sems, slot_sems, last_sems,
    ) = refs[groups // 2 :]
    _, rows, chans = through.shape
    signal = pltpu.make_async_copy(grad_hbm, mix_grad, signal_sem.at[0])
    signal.start()
    kinds = ((table_hbm, table), (spec_hbm, spec), (back_hbm, back))
    for index in range(8):
        for kind, (from_ref, into) in enumerate(kinds):
            pltpu.make_async_copy(from_ref.at[index], into.at[index], load_sems.at[kind, index]).start()
    for partner in range(groups):
        block = me_ref[0] ^ partner
        piece = pieces[partner // 2].at[partner % 2]
        pltpu.make_async_copy(piece, source.at[block], piece_sems.at[block]).start()

    def feats_copy(block):
        return pltpu.make_async_copy(feats_hbm.at[block], feats.at[block], feats_sems.at[block])

    for block in range(groups):
        feats_copy(block).start()
    grads[:, :, 0:HALO, :] = jnp.zeros((2, chans // 128, HALO, 128), F32)
    sums[...] = jnp.zeros_like(sums)
    signal.wait()
    split_signal(mix_grad, rings)
    leaf = spec.shape[1] // 2

    def ring_copy(index):
        return pltpu.make_async_copy(ring.at[index], ring_hbm.at[index], ring_sems.at[index])

    @pl.loop(0, 8)
    def _(index):
        for kind, (from_ref, into) in enumerate(kinds):
            pltpu.make_async_copy(from_ref.at[index], into.at[index], load_sems.at[kind, index]).wait()
        ring[index] = jnp.dot(table[index], rings[index], preferred_element_type=F32)
        d_real, d_imag = ring[index, :leaf], ring[index, leaf:]
        f_real, f_imag = spec[index, :leaf], spec[index, leaf:]
        products[:leaf] = (d_real * f_real + d_imag * f_imag).astype(BF16)
        products[leaf:] = (d_imag * f_real - d_real * f_imag).astype(BF16)
        joined[index] = jnp.dot(back[index], products[...], preferred_element_type=F32)
        ring_copy(index).start()

    def place_through(owner, strip, inside, lanes, result):
        grad = mix_grad[owner, inside, lanes].astype(F32)
        through[owner, inside, lanes] = (result + gain_ref[0:1, lanes] * grad).astype(BF16)

    join_signal(joined, 0, rows, place_through)

    @pl.loop(0, groups)
    def _(block):
        pltpu.make_async_copy(pieces[0].at[0], source.at[block], piece_sems.at[block]).wait()
        feats_copy(block).wait()

    def write_back(slot_at, block_at):
        return pltpu.make_async_copy(
            slots.at[slot_at], ready_hbm.at[block_at, pl.ds(0, 2 * rows)], slot_sems.at[slot_at]
        )

    @pl.loop(0, groups)
    def _(step):
        block = groups - 1 - step
        slot = lax.rem(step, 2)

        @pl.when(step >= 2)
        def _():
            write_back(slot, block + 2).wait()

        for part in range(chans // 128):
            lanes = slice(part * 128, part * 128 + 128)
            for role in range(2):
                grads[role, part, rows : rows + HALO, :] = grads[role, part, 0:HALO, :]
            for row in range(0, rows, 16):
                span = slice(row, row + 16)
                values = through[block, span, lanes].astype(F32)
                grads[0, part, span, :] = values * feats[block, 1, span, lanes]
                grads[1, part, span, :] = values * feats[block, 0, span, lanes]
            for role in range(2):

                def place(row, values, role=role, lanes=lanes):
                    slots[slot, role * rows + row : role * rows + row + 16, lanes] = values

                def source_block(row, role=role, lanes=lanes):
                    return source[block, role, row : row + 16, lanes]

                taps = tap_rows(taps_ref, role + 1, lanes)
                back_taps(grads.at[role], source_block, part, taps, place, sums, role, lanes)
        write_back(slot, block).start()

    rows_out = [jnp.zeros((HALO, chans), F32)] + sum_rows(sums, 2)
    last[...] = jnp.concatenate(rows_out, axis=0).astype(BF16)
    wait_all(
        [
            pltpu.make_async_copy(last, ready_hbm.at[owner, pl.ds(2 * rows, EXTRA)], last_sems.at[owner])
            for owner in range(groups)
        ]
    )
    write_back(groups % 2, 1).wait()
    write_back((groups + 1) % 2, 0).wait()

    @pl.loop(0, 8)
    def _(index):
        ring_copy(index).wait()


def through_work(me, pieces, mix_grad, feats, spectrum, table, back, taps, gain):
    groups, rows, chans = mix_grad.shape
    length = groups * rows
    wide = length // 4
    parts = chans // 128
    return pl.pallas_call(
        functools.partial(through_kernel, groups),
        out_shape=(
            pltpu.HBM((groups, 2 * rows + EXTRA, chans), BF16),
            pltpu.HBM((8, wide, chans), F32),
        ),
        in_specs=[pl.BlockSpec(memory_space=pltpu.SMEM)]
        + [pl.BlockSpec(memory_space=pl.ANY)] * (groups // 2 + 5)
        + [pl.BlockSpec(memory_space=pltpu.VMEM)] * 2,
        out_specs=(pl.BlockSpec(memory_space=pl.ANY),) * 2,
        scratch_shapes=[
            pltpu.VMEM((groups, 2, rows, chans), BF16),
            pltpu.VMEM((groups, rows, chans), BF16),
            pltpu.VMEM((groups, 2, rows, chans), F32),
            pltpu.VMEM((8, wide, chans), F32),
            pltpu.VMEM((8, wide, chans), F32),
            pltpu.VMEM((8, wide, wide), BF16),
            pltpu.VMEM((8, wide, wide), BF16),
            pltpu.VMEM((8, wide, chans), BF16),
            pltpu.VMEM((wide, chans), BF16),
            pltpu.VMEM((8, wide, chans), F32),
            pltpu.VMEM((groups, rows, chans), BF16),
            pltpu.VMEM((2, parts, rows + HALO, 128), F32),
            pltpu.VMEM((2, TAPS, 8, chans), F32),
            pltpu.VMEM((2, 2 * rows, chans), BF16),
            pltpu.VMEM((EXTRA, chans), BF16),
            pltpu.SemaphoreType.DMA((groups,)),
            pltpu.SemaphoreType.DMA((1,)),
            pltpu.SemaphoreType.DMA((groups,)),
            pltpu.SemaphoreType.DMA((3, 8)),
            pltpu.SemaphoreType.DMA((8,)),
            pltpu.SemaphoreType.DMA((2,)),
            pltpu.SemaphoreType.DMA((groups,)),
        ],
        compiler_params=pltpu.CompilerParams(vmem_limit_bytes=34 * MIB),
        cost_estimate=pl.CostEstimate(
            flops=32 * wide * wide * chans + 100 * length * chans, bytes_accessed=28 * MIB, transcendentals=0
        ),
        name="through_values",
    )(me, *in_hbm(*pieces), mix_grad, *in_hbm(feats, spectrum, table, back), taps, gain)


def filter_grad_kernel(
    grad_hbm, gated_hbm, d_hbm, g_hbm, back_hbm, filt_hbm, skip_ref,
    mix_grad, gated, d_ring, g_ring, back, products, joined, flat, turned_flat, signal_sems, load_sems, filt_sem,
):
    groups, rows, chans = mix_grad.shape
    signals = [
        pltpu.make_async_copy(grad_hbm, mix_grad, signal_sems.at[0]),
        pltpu.make_async_copy(gated_hbm, gated, signal_sems.at[1]),
    ]
    kinds = ((d_hbm, d_ring), (g_hbm, g_ring), (back_hbm, back))
    for index in range(8):
        for kind, (from_ref, into) in enumerate(kinds):
            pltpu.make_async_copy(from_ref.at[index], into.at[index], load_sems.at[kind, index]).start()
    for copy in signals:
        copy.start()
    leaf = d_ring.shape[1] // 2

    @pl.loop(0, 8)
    def _(index):
        for kind, (from_ref, into) in enumerate(kinds):
            pltpu.make_async_copy(from_ref.at[index], into.at[index], load_sems.at[kind, index]).wait()
        d_real, d_imag = d_ring[index, :leaf], d_ring[index, leaf:]
        g_real, g_imag = g_ring[index, :leaf], g_ring[index, leaf:]
        products[:leaf] = (d_real * g_real + d_imag * g_imag).astype(BF16)
        products[leaf:] = (d_imag * g_real - d_real * g_imag).astype(BF16)
        joined[index] = jnp.dot(back[index], products[...], preferred_element_type=F32)

    for copy in signals:
        copy.wait()
    skip_ref[...] = jnp.zeros_like(skip_ref)

    @pl.loop(0, groups)
    def _(block):
        for lane in range(0, chans, 128):
            lanes = slice(lane, lane + 128)
            total = jnp.zeros((16, 128), F32)
            for row in range(0, rows, 16):
                span = slice(row, row + 16)
                total = total + mix_grad[block, span, lanes].astype(F32) * gated[block, span, lanes].astype(F32)
            skip_ref[0:1, lanes] += jnp.sum(total, axis=0, keepdims=True)

    def place_filter(owner, strip, inside, lanes, result):
        flat[pl.ds(pl.multiple_of(owner * rows + strip * 16, 16), 16), lanes] = result

    join_signal(joined, 0, rows, place_filter)
    for block in range(groups):
        span = slice(block * rows, (block + 1) * rows)
        turned_flat[:, span] = flat[span, :].T
    wait_all([pltpu.make_async_copy(turned_flat, filt_hbm, filt_sem.at[0])])


def filter_gradient(mix_grad, gated, d_ring, g_ring, back):
    groups, rows, chans = mix_grad.shape
    length = groups * rows
    wide = length // 4
    return pl.pallas_call(
        filter_grad_kernel,
        out_shape=(pltpu.HBM((chans, length), F32), jax.ShapeDtypeStruct((1, chans), F32)),
        in_specs=[pl.BlockSpec(memory_space=pl.ANY)] * 5,
        out_specs=(pl.BlockSpec(memory_space=pl.ANY), pl.BlockSpec(memory_space=pltpu.VMEM)),
        scratch_shapes=[
            pltpu.VMEM((groups, rows, chans), BF16),
            pltpu.VMEM((groups, rows, chans), BF16),
            pltpu.VMEM((8, wide, chans), F32),
            pltpu.VMEM((8, wide, chans), F32),
            pltpu.VMEM((8, wide, wide), BF16),
            pltpu.VMEM((wide, chans), BF16),
            pltpu.VMEM((8, wide, chans), F32),
            pltpu.VMEM((length, chans), F32),
            pltpu.VMEM((chans, length), F32),
            pltpu.SemaphoreType.DMA((2,)),
            pltpu.SemaphoreType.DMA((3, 8)),
            pltpu.SemaphoreType.DMA((1,)),
        ],
        compiler_params=pltpu.CompilerParams(vmem_limit_bytes=28 * MIB),
        cost_estimate=pl.CostEstimate(
            flops=16 * wide * wide * chans + 40 * length * chans, bytes_accessed=16 * MIB, transcendentals=0
        ),
        name="filter_gradient",
    )(mix_grad, *in_hbm(gated, d_ring, g_ring, back))


def place_kernel(columns, held_ref, *refs):
    *wide_refs, sems = refs
    groups, _, chans = held_ref.shape
    rows = wide_refs[-1].shape[0]
    wide_refs = wide_refs[-1 - max(index for index, _ in columns) :]
    copies = []
    for owner in range(groups):
        for kind, (index, first) in enumerate(columns):
            copies.append(
                pltpu.make_async_copy(
                    held_ref.at[owner, pl.ds(kind * rows, rows)],
                    wide_refs[index].at[:, pl.ds(first * groups * chans + owner * chans, chans)],
                    sems.at[owner, kind],
                )
            )
    wait_all(copies)


def place_columns(held, rows, columns, earlier):
    groups, _, chans = held.shape
    width = groups * chans
    shapes = [(rows, 3 * width)]
    return pl.pallas_call(
        functools.partial(place_kernel, columns),
        input_output_aliases={1: 0} if earlier else {},
        out_shape=[pltpu.HBM(shape, BF16) for shape in shapes],
        in_specs=[pl.BlockSpec(memory_space=pltpu.VMEM)] + [pl.BlockSpec(memory_space=pl.ANY)] * len(earlier),
        out_specs=[pl.BlockSpec(memory_space=pl.ANY)] * len(shapes),
        scratch_shapes=[pltpu.SemaphoreType.DMA((groups, 2))],
        compiler_params=pltpu.CompilerParams(vmem_limit_bytes=6 * MIB),
        cost_estimate=pl.CostEstimate(flops=0, bytes_accessed=8 * rows * width, transcendentals=0),
        name="place_columns",
    )(held, *in_hbm(*earlier))


def edge_of(block, steps):
    sections, groups = lax.axis_size("section"), lax.axis_size("ctx")
    pairs = [
        (section * groups + place, (section + steps) % sections * groups + place + steps)
        for section in range(sections)
        for place in range(groups)
        if 0 <= place + steps < groups
    ]
    return lax.ppermute(block, ("section", "ctx"), pairs)


def on_device(acts, cots, kern, filt, skip):
    rows, feats_all = acts.shape[1:]
    groups = lax.axis_size("ctx")
    chans = filt.shape[1]
    width = groups * chans
    place = lax.axis_index("ctx").astype(jnp.int32)
    me = place[None]

    table, back = (jnp.asarray(one) for one in leaf_tables(rows * groups))
    spectrum = filter_spectrum(filt[0], table)
    gain = lax.dynamic_slice_in_dim(skip, place * chans, chans, axis=1)
    came = handed_over(leaving_pieces(me, acts[0], groups, 2), 0, 1)
    query, *pieces = pieces_for_owners(me, acts[0], came, groups)
    pieces = [handed_over(piece, 1, 2 * chip) for chip, piece in enumerate(pieces)]
    incoming = cots[0]
    kern, pieces[0] = lax.optimization_barrier((kern, pieces[0]))
    taps = kern[0].reshape(TAPS, 3, groups, chans)
    taps = lax.dynamic_index_in_dim(taps, place, axis=2, keepdims=False).transpose(1, 0, 2)
    taps = jnp.pad(taps, ((0, 0), (0, HALO - TAPS), (0, 0)))
    query_taps = jnp.pad(kern[0, :, :width], ((0, HALO - TAPS), (0, 0)))
    query, incoming, pieces[:LATE] = lax.optimization_barrier((query, incoming, pieces[:LATE]))
    query = passed_along(query, "section", 1)
    incoming = passed_along(incoming, "section", -1)

    feats, gated, inner, g_ring = inner_work(me, pieces, spectrum, table, back, taps, gain)
    inner = lax.all_to_all(inner, "ctx", split_axis=0, concat_axis=0, tiled=True)

    before = edge_of(acts[0, rows - HALO :, :width], 1)
    later = edge_of(cots[0, :HALO], -1)
    before, later = lax.optimization_barrier((before, later))
    mix_grad, features = query_features(query, before, incoming, query_taps, groups)
    mix_grad = lax.all_to_all(mix_grad, "ctx", split_axis=0, concat_axis=0, tiled=True)
    output, input_grad, partial = query_outputs(query, incoming, later, features, inner, query_taps)
    partial, mix_grad = lax.optimization_barrier((partial, mix_grad))
    partial = lax.all_to_all(partial, "ctx", split_axis=0, concat_axis=0, tiled=True)
    query_sums = jnp.sum(partial.astype(F32), axis=0)

    ready, d_ring = through_work(me, pieces, mix_grad, feats, spectrum, table, back, taps, gain)
    query_rows = jnp.broadcast_to(query_sums.astype(BF16), (groups, HALO, chans))
    ready = lax.dynamic_update_slice(ready, query_rows, (0, 2 * rows, 0))
    ready = lax.all_to_all(ready, "ctx", split_axis=0, concat_axis=0, tiled=True)
    filt_grad, skip_grad = filter_gradient(mix_grad, gated, d_ring, g_ring, back)
    (input_grad,) = place_columns(ready, rows, ((0, 1), (0, 2)), (input_grad,))
    sums = ready[:, 2 * rows : 2 * rows + 3 * HALO].reshape(groups, 3, HALO, chans)[:, :, :TAPS]
    kern_grad = sums.transpose(2, 1, 0, 3).reshape(TAPS, feats_all).astype(F32)
    return (output[None], input_grad[None], kern_grad[None], filt_grad[None], skip_grad)


def solution(mesh):
    return jax.shard_map(
        on_device,
        mesh=mesh,
        in_specs=(
            P("section", "ctx", None),
            P("section", "ctx", None),
            P("section", None, None),
            P("section", "ctx", None),
            P("section", None),
        ),
        out_specs=(
            P("section", "ctx", None),
            P("section", "ctx", None),
            P("section", None, None),
            P("section", "ctx", None),
            P("section", "ctx"),
        ),
        check_vma=False,
    )
```

```python
import functools
import math

import jax
import jax.numpy as jnp
import ml_dtypes
import numpy as np
from jax import lax
from jax.experimental import pallas as pl
from jax.experimental.pallas import tpu as pltpu
from jax.sharding import PartitionSpec as P

TAPS = 7
HALO = 8
EXTRA = 24
LATE = 3
ROOT = math.sqrt(0.5)
F32 = jnp.float32
BF16 = jnp.bfloat16
MIB = 1 << 20


def in_hbm(*arrays):
    return [pltpu.with_memory_space_constraint(array, pltpu.HBM) for array in arrays]


def passed_along(value, axis, steps):
    count = lax.axis_size(axis)
    pairs = [(source, (source + steps) % count) for source in range(count)]
    return lax.ppermute(value, axis, pairs)


def handed_over(value, steps, partner):
    sections, groups = lax.axis_size("section"), lax.axis_size("ctx")
    pairs = [
        (section * groups + place, (section + steps) % sections * groups + (place ^ partner))
        for section in range(sections)
        for place in range(groups)
    ]
    return lax.ppermute(value, ("section", "ctx"), pairs)


def leaf_angles():
    angles = [math.pi / 2]
    for _ in range(3):
        angles = [half for angle in angles for half in (angle / 2, angle / 2 + math.pi)]
    return angles


def leaf_tables(length):
    leaf = length // 8
    order = np.arange(leaf)
    tables = []
    for angle in leaf_angles():
        phase = (angle + 2.0 * np.pi * order[:, None]) / leaf * order[None, :]
        real, imag = np.cos(phase), np.sin(phase)
        tables.append(np.block([[real, -imag], [imag, real]]))
    table = np.stack(tables)
    back = table.transpose(0, 2, 1) / length
    return table.astype(ml_dtypes.bfloat16), back.astype(ml_dtypes.bfloat16)


def turned(pair, angle):
    real, imag = pair
    cos, sin = math.cos(angle), math.sin(angle)
    return real * cos - imag * sin, real * sin + imag * cos


def split_rings(parts):
    low, high = [], []
    for lower, upper in zip(parts[:4], parts[4:]):
        scaled = upper * ROOT
        low.append((lower + scaled, scaled))
        high.append((lower - scaled, -scaled))
    rings = [(math.pi / 4, low), (math.pi / 4 + math.pi, high)]
    while len(rings[0][1]) > 1:
        finer = []
        for angle, pieces in rings:
            half = len(pieces) // 2
            plus, minus = [], []
            for lower, upper in zip(pieces[:half], pieces[half:]):
                real, imag = turned(upper, angle / 2)
                plus.append((lower[0] + real, lower[1] + imag))
                minus.append((lower[0] - real, lower[1] - imag))
            finer += [(angle / 2, plus), (angle / 2 + math.pi, minus)]
        rings = finer
    return [pieces[0] for _, pieces in rings]


def join_rings(leaves):
    angles = [math.pi / 4, math.pi / 4 + math.pi]
    angles = [half for angle in angles for half in (angle / 2, angle / 2 + math.pi)]
    groups = [[leaf] for leaf in leaves]
    while len(groups) > 2:
        merged = []
        for index in range(0, len(groups), 2):
            angle = angles[index // 2] if len(groups) == 8 else [math.pi / 4, math.pi / 4 + math.pi][index // 2]
            lower, upper = [], []
            for plus, minus in zip(groups[index], groups[index + 1]):
                lower.append((plus[0] + minus[0], plus[1] + minus[1]))
                upper.append(turned((plus[0] - minus[0], plus[1] - minus[1]), -angle / 2))
            merged.append(lower + upper)
        groups = merged
    lower, upper = [], []
    for plus, minus in zip(groups[0], groups[1]):
        lower.append(plus[0] + minus[0])
        upper.append(((plus[0] - minus[0]) + (plus[1] - minus[1])) * ROOT)
    return lower + upper


def filter_kernel(filt_ref, table_ref, spec_ref, rings):
    chans, length = filt_ref.shape
    leaf = length // 8
    step = pl.program_id(0)

    @pl.when(step == 0)
    def _():
        @pl.loop(0, chans // 16)
        def _(strip):
            rows = pl.ds(pl.multiple_of(strip * 16, 16), 16)
            for lane in range(0, leaf, 128):
                parts = [
                    filt_ref[rows, piece * leaf + lane : piece * leaf + lane + 128].astype(F32)
                    for piece in range(8)
                ]
                for index, (real, imag) in enumerate(split_rings(parts)):
                    rings[index, rows, lane : lane + 128] = real.astype(BF16)
                    rings[index, rows, leaf + lane : leaf + lane + 128] = imag.astype(BF16)

    spec_ref[0] = lax.dot_general(
        table_ref[0], rings[step], (((1,), (1,)), ((), ())), preferred_element_type=F32
    )


def filter_spectrum(filt, table):
    chans, length = filt.shape
    wide = length // 4
    return pl.pallas_call(
        filter_kernel,
        out_shape=pltpu.HBM((8, wide, chans), F32),
        grid=(8,),
        in_specs=[
            pl.BlockSpec((chans, length), lambda j: (0, 0)),
            pl.BlockSpec((1, wide, wide), lambda j: (j, 0, 0)),
        ],
        out_specs=pl.BlockSpec((1, wide, chans), lambda j: (j, 0, 0)),
        scratch_shapes=[pltpu.VMEM((8, chans, wide), BF16)],
        compiler_params=pltpu.CompilerParams(vmem_limit_bytes=12 * MIB),
        cost_estimate=pl.CostEstimate(
            flops=16 * wide * wide * chans, bytes_accessed=10 * MIB, transcendentals=0
        ),
        name="filter_spectrum",
    )(*in_hbm(filt, table))


def wait_all(copies):
    for copy in copies:
        copy.start()
    for copy in copies:
        copy.wait()


def leave_kernel(me_ref, wide_ref, leaving_ref, sems):
    chips, roles, _, chans = leaving_ref.shape
    width = wide_ref.shape[1] // 3
    copies = []
    for chip in range(chips):
        start = (me_ref[0] ^ (2 * chip + 1)) * chans
        for role in range(roles):
            columns = pl.ds(pl.multiple_of((role + 1) * width + start, 128), chans)
            copies.append(
                pltpu.make_async_copy(wide_ref.at[:, columns], leaving_ref.at[chip, role], sems.at[chip, role])
            )
    wait_all(copies)


def piece_kernel(me_ref, wide_ref, came_ref, query_ref, *refs):
    *pieces, sems, query_sem = refs
    _, roles, _, chans = pieces[0].shape
    width = wide_ref.shape[1] // 3
    copies = [pltpu.make_async_copy(wide_ref.at[:, pl.ds(0, width)], query_ref, query_sem.at[0])]
    for chip, piece in enumerate(pieces):
        start = (me_ref[0] ^ (2 * chip)) * chans
        for role in range(roles):
            columns = pl.ds(pl.multiple_of((role + 1) * width + start, 128), chans)
            copies.append(pltpu.make_async_copy(wide_ref.at[:, columns], piece.at[0, role], sems.at[chip, role]))
        copies.append(pltpu.make_async_copy(came_ref.at[chip], piece.at[1], sems.at[chip, roles]))
    wait_all(copies)


def leaving_pieces(me, wide, groups, roles):
    rows, width = wide.shape
    chans = width // 3 // groups
    return pl.pallas_call(
        leave_kernel,
        out_shape=jax.ShapeDtypeStruct((groups // 2, roles, rows, chans), BF16),
        in_specs=[pl.BlockSpec(memory_space=pltpu.SMEM), pl.BlockSpec(memory_space=pl.ANY)],
        out_specs=pl.BlockSpec(memory_space=pltpu.VMEM),
        scratch_shapes=[pltpu.SemaphoreType.DMA((groups // 2, roles))],
        compiler_params=pltpu.CompilerParams(vmem_limit_bytes=4 * MIB),
        cost_estimate=pl.CostEstimate(flops=0, bytes_accessed=2 * rows * width, transcendentals=0),
        name="leaving_pieces",
    )(me, *in_hbm(wide))


def pieces_for_owners(me, wide, came, groups):
    chips, roles, rows, chans = came.shape
    return pl.pallas_call(
        piece_kernel,
        out_shape=[jax.ShapeDtypeStruct((rows, wide.shape[1] // 3), BF16)]
        + [jax.ShapeDtypeStruct((2, roles, rows, chans), BF16)] * chips,
        in_specs=[pl.BlockSpec(memory_space=pltpu.SMEM), pl.BlockSpec(memory_space=pl.ANY), pl.BlockSpec(memory_space=pltpu.VMEM)],
        out_specs=[pl.BlockSpec(memory_space=pltpu.VMEM)] * (chips + 1),
        scratch_shapes=[pltpu.SemaphoreType.DMA((chips, roles + 1)), pltpu.SemaphoreType.DMA((1,))],
        compiler_params=pltpu.CompilerParams(vmem_limit_bytes=8 * MIB),
        cost_estimate=pl.CostEstimate(flops=0, bytes_accessed=8 * chips * roles * rows * chans, transcendentals=0),
        name="pieces_for_owners",
    )(me, *in_hbm(wide), came)


def tap_sum(held, part, taps, row):
    total = taps[0] * held[part, HALO + row : HALO + row + 16, :]
    for tap in range(1, TAPS):
        total = total + taps[tap] * held[part, HALO + row - tap : HALO + row - tap + 16, :]
    return total


def hold(held, part, block):
    rows = block.shape[0]
    held[part, 0:HALO, :] = held[part, rows : rows + HALO, :]
    held[part, HALO:, :] = block.astype(F32)


def tap_rows(taps_ref, role, lanes):
    return [taps_ref[role, tap : tap + 1, lanes] for tap in range(TAPS)]


def split_signal(signal, rings):
    groups, rows, chans = signal.shape
    leaf = groups * rows // 8
    per_piece = leaf // rows

    @pl.loop(0, rows // 16)
    def _(strip):
        inside = pl.ds(pl.multiple_of(strip * 16, 16), 16)
        for part in range(per_piece):
            real_rows = pl.ds(pl.multiple_of(part * rows + strip * 16, 16), 16)
            imag_rows = pl.ds(pl.multiple_of(leaf + part * rows + strip * 16, 16), 16)
            for lane in range(0, chans, 128):
                lanes = slice(lane, lane + 128)
                parts = [signal[piece * per_piece + part, inside, lanes].astype(F32) for piece in range(8)]
                for index, (real, imag) in enumerate(split_rings(parts)):
                    rings[index, real_rows, lanes] = real.astype(BF16)
                    rings[index, imag_rows, lanes] = imag.astype(BF16)


def join_signal(joined, first, rows, place):
    leaf = joined.shape[1] // 2
    per_piece = leaf // rows
    chans = 256 if joined.shape[2] % 256 == 0 else 128

    @pl.loop(0, rows // 16)
    def _(strip):
        inside = pl.ds(pl.multiple_of(strip * 16, 16), 16)
        for part in range(per_piece):
            real_rows = pl.ds(pl.multiple_of(part * rows + strip * 16, 16), 16)
            imag_rows = pl.ds(pl.multiple_of(leaf + part * rows + strip * 16, 16), 16)
            for lane in range(0, chans, 128):
                column = slice(first + lane, first + lane + 128)
                leaves = [
                    (joined[index, real_rows, column], joined[index, imag_rows, column]) for index in range(8)
                ]
                for piece, result in enumerate(join_rings(leaves)):
                    place(piece * per_piece + part, strip, inside, slice(lane, lane + 128), result)


def back_taps(grads, source_block, part, taps, place, sums, role, lanes):
    rows = grads.shape[1] - HALO
    parts = [jnp.zeros((16, 128), F32) for _ in range(TAPS)]
    for row in range(0, rows, 16):
        here = source_block(row).astype(F32)
        total = jnp.zeros((16, 128), F32)
        for tap in range(TAPS):
            ahead = grads[part, row + tap : row + tap + 16, :]
            total = total + taps[tap] * ahead
            parts[tap] = parts[tap] + here * ahead
        place(row, total.astype(BF16))
    for tap in range(TAPS):
        sums[role, tap, :, lanes] += parts[tap][0:8] + parts[tap][8:16]


def sum_rows(sums, roles):
    rows_out = []
    chans = sums.shape[3]
    for role in range(roles):
        for tap in range(TAPS):
            rows_out.append(jnp.sum(sums[role, tap], axis=0, keepdims=True))
        rows_out.append(jnp.zeros((HALO - TAPS, chans), F32))
    return rows_out


def mixed_kernel(groups, me_ref, *refs):
    pieces = refs[: groups // 2]
    spec_hbm, table_hbm, back_hbm, taps_ref, gain_ref = refs[groups // 2 : groups // 2 + 5]
    (
        feats_hbm, gated_hbm, inner_ref, ring_hbm,
        source, spec, table, back, held, feats, gated, rings, products, joined, ring,
        piece_sems, load_sems, feats_sems, gated_sem, ring_sems,
    ) = refs[groups // 2 + 5 :]
    _, _, rows, chans = source.shape
    for partner in range(groups):
        block = me_ref[0] ^ partner
        piece = pieces[partner // 2].at[partner % 2]
        pltpu.make_async_copy(piece, source.at[block], piece_sems.at[block]).start()
    loads = []
    for index in range(8):
        for kind, (from_ref, into) in enumerate(((table_hbm, table), (spec_hbm, spec), (back_hbm, back))):
            loads.append(pltpu.make_async_copy(from_ref.at[index], into.at[index], load_sems.at[kind, index]))
            loads[-1].start()
    held[:, :, rows:, :] = jnp.zeros((2, chans // 128, HALO, 128), F32)

    def feats_copy(block):
        return pltpu.make_async_copy(feats.at[block], feats_hbm.at[block], feats_sems.at[block])

    @pl.loop(0, groups)
    def _(step):
        pltpu.make_async_copy(pieces[0].at[0], source.at[step], piece_sems.at[step]).wait()
        for part in range(chans // 128):
            lanes = slice(part * 128, part * 128 + 128)
            for role in range(2):
                hold(held.at[role], part, source[step, role, :, lanes])
            taps = [tap_rows(taps_ref, role + 1, lanes) for role in range(2)]
            for row in range(0, rows, 16):
                span = slice(row, row + 16)
                keyed, value = [tap_sum(held.at[role], part, taps[role], row) for role in range(2)]
                feats[step, 0, span, lanes] = keyed
                feats[step, 1, span, lanes] = value
                gated[step, span, lanes] = (keyed * value).astype(BF16)
        feats_copy(step).start()

    gated_copy = pltpu.make_async_copy(gated, gated_hbm, gated_sem.at[0])
    gated_copy.start()
    split_signal(gated, rings)
    leaf = spec.shape[1] // 2

    def ring_copy(index):
        return pltpu.make_async_copy(ring.at[index], ring_hbm.at[index], ring_sems.at[index])

    @pl.loop(0, 8)
    def _(index):
        for kind, (from_ref, into) in enumerate(((table_hbm, table), (spec_hbm, spec), (back_hbm, back))):
            pltpu.make_async_copy(from_ref.at[index], into.at[index], load_sems.at[kind, index]).wait()
        ring[index] = jnp.dot(table[index], rings[index], preferred_element_type=F32)
        g_real, g_imag = ring[index, :leaf], ring[index, leaf:]
        f_real, f_imag = spec[index, :leaf], spec[index, leaf:]
        products[:leaf] = (g_real * f_real - g_imag * f_imag).astype(BF16)
        products[leaf:] = (g_real * f_imag + g_imag * f_real).astype(BF16)
        joined[index] = jnp.dot(back[index], products[...], preferred_element_type=F32)
        ring_copy(index).start()

    def place(owner, strip, inside, lanes, result):
        total = result + gain_ref[0:1, lanes] * gated[owner, inside, lanes].astype(F32)
        inner_ref[owner, inside, lanes] = total.astype(BF16)

    join_signal(joined, 0, rows, place)
    for owner in range(groups - 1):
        inner_ref[owner, rows:, :] = inner_ref[owner + 1, 0:HALO, :]
    inner_ref[groups - 1, rows:, :] = jnp.zeros((HALO, chans), BF16)

    @pl.loop(0, groups)
    def _(step):
        feats_copy(step).wait()

    gated_copy.wait()

    @pl.loop(0, 8)
    def _(index):
        ring_copy(index).wait()


def inner_work(me, pieces, spectrum, table, back, taps, gain):
    groups = 2 * len(pieces)
    _, _, rows, chans = pieces[0].shape
    length = groups * rows
    wide = length // 4
    parts = chans // 128
    return pl.pallas_call(
        functools.partial(mixed_kernel, groups),
        out_shape=(
            pltpu.HBM((groups, 2, rows, chans), F32),
            pltpu.HBM((groups, rows, chans), BF16),
            jax.ShapeDtypeStruct((groups, rows + HALO, chans), BF16),
            pltpu.HBM((8, wide, chans), F32),
        ),
        in_specs=[pl.BlockSpec(memory_space=pltpu.SMEM)]
        + [pl.BlockSpec(memory_space=pl.ANY)] * (groups // 2 + 3)
        + [pl.BlockSpec(memory_space=pltpu.VMEM)] * 2,
        out_specs=(
            pl.BlockSpec(memory_space=pl.ANY),
            pl.BlockSpec(memory_space=pl.ANY),
            pl.BlockSpec(memory_space=pltpu.VMEM),
            pl.BlockSpec(memory_space=pl.ANY),
        ),
        scratch_shapes=[
            pltpu.VMEM((groups, 2, rows, chans), BF16),
            pltpu.VMEM((8, wide, chans), F32),
            pltpu.VMEM((8, wide, wide), BF16),
            pltpu.VMEM((8, wide, wide), BF16),
            pltpu.VMEM((2, parts, HALO + rows, 128), F32),
            pltpu.VMEM((groups, 2, rows, chans), F32),
            pltpu.VMEM((groups, rows, chans), BF16),
            pltpu.VMEM((8, wide, chans), BF16),
            pltpu.VMEM((wide, chans), BF16),
            pltpu.VMEM((8, wide, chans), F32),
            pltpu.VMEM((8, wide, chans), F32),
            pltpu.SemaphoreType.DMA((groups,)),
            pltpu.SemaphoreType.DMA((3, 8)),
            pltpu.SemaphoreType.DMA((groups,)),
            pltpu.SemaphoreType.DMA((1,)),
            pltpu.SemaphoreType.DMA((8,)),
        ],
        compiler_params=pltpu.CompilerParams(vmem_limit_bytes=33 * MIB),
        cost_estimate=pl.CostEstimate(
            flops=32 * wide * wide * chans + 60 * length * chans, bytes_accessed=24 * MIB, transcendentals=0
        ),
        name="inner_values",
    )(me, *in_hbm(*pieces, spectrum, table, back), taps, gain)


def query_kernel(
    source, before, incoming, taps_ref, grad_hbm, features_hbm, mix_grad, features, held, grad_sems, features_sems
):
    groups, rows, chans = mix_grad.shape

    def write_back(owner):
        columns = pl.ds(pl.multiple_of(owner * chans, 128), chans)
        return (
            pltpu.make_async_copy(mix_grad.at[owner], grad_hbm.at[owner], grad_sems.at[owner]),
            pltpu.make_async_copy(features.at[:, columns], features_hbm.at[:, columns], features_sems.at[owner]),
        )

    @pl.loop(0, groups)
    def _(owner):
        for part in range(chans // 128):
            columns = pl.ds(pl.multiple_of(owner * chans + part * 128, 128), 128)
            lanes = slice(part * 128, part * 128 + 128)
            held[part, 0:HALO, :] = before[:, columns].astype(F32)
            held[part, HALO:, :] = source[:, columns].astype(F32)
            taps = [taps_ref[tap : tap + 1, columns] for tap in range(TAPS)]
            for row in range(0, rows, 16):
                span = slice(row, row + 16)
                total = tap_sum(held, part, taps, row)
                features[span, columns] = total
                mix_grad[owner, span, lanes] = (incoming[span, columns].astype(F32) * total).astype(BF16)
        for copy in write_back(owner):
            copy.start()

    @pl.loop(0, groups)
    def _(owner):
        for copy in write_back(owner):
            copy.wait()


def query_features(source, before, incoming, taps, groups):
    rows, width = source.shape
    chans = width // groups
    return pl.pallas_call(
        query_kernel,
        out_shape=(
            pltpu.HBM((groups, rows, chans), BF16),
            pltpu.HBM((rows, width), F32),
        ),
        in_specs=[pl.BlockSpec(memory_space=pltpu.VMEM)] * 4,
        out_specs=(pl.BlockSpec(memory_space=pl.ANY),) * 2,
        scratch_shapes=[
            pltpu.VMEM((groups, rows, chans), BF16),
            pltpu.VMEM((rows, width), F32),
            pltpu.VMEM((chans // 128, HALO + rows, 128), F32),
            pltpu.SemaphoreType.DMA((groups,)),
            pltpu.SemaphoreType.DMA((groups,)),
        ],
        compiler_params=pltpu.CompilerParams(vmem_limit_bytes=10 * MIB),
        cost_estimate=pl.CostEstimate(flops=15 * rows * width, bytes_accessed=10 * rows * width, transcendentals=0),
        name="query_features",
    )(source, before, incoming, taps)


def output_kernel(
    source, incoming, later, features, inner, taps_ref, output_hbm, grad_hbm, sums_ref, grads, sums, slots, slot_sems
):
    groups, _, chans = inner.shape
    rows = source.shape[0]

    def write_back(owner, slot):
        columns = pl.ds(pl.multiple_of(owner * chans, 128), chans)
        return [
            pltpu.make_async_copy(slots.at[slot, kind], into.at[:, columns], slot_sems.at[slot, kind])
            for kind, into in enumerate((output_hbm, grad_hbm))
        ]

    @pl.loop(0, groups)
    def _(owner):
        slot = lax.rem(owner, 2)

        @pl.when(owner >= 2)
        def _():
            for copy in write_back(owner - 2, slot):
                copy.wait()

        sums[...] = jnp.zeros_like(sums)
        for part in range(chans // 128):
            columns = pl.ds(pl.multiple_of(owner * chans + part * 128, 128), 128)
            lanes = slice(part * 128, part * 128 + 128)
            for row in range(0, rows, 16):
                span = slice(row, row + 16)
                values = inner[owner, span, lanes].astype(F32)
                grads[part, span, :] = incoming[span, columns].astype(F32) * values
                slots[slot, 0, span, lanes] = (features[span, columns] * values).astype(BF16)
            ahead = inner[owner, rows : rows + HALO, lanes].astype(F32)
            grads[part, rows:, :] = later[:, columns].astype(F32) * ahead

            def place(row, values, lanes=lanes):
                slots[slot, 1, row : row + 16, lanes] = values

            def source_block(row, columns=columns):
                return source[row : row + 16, columns]

            taps = [taps_ref[tap : tap + 1, columns] for tap in range(TAPS)]
            back_taps(grads, source_block, part, taps, place, sums, 0, lanes)
        sums_ref[owner] = jnp.concatenate(sum_rows(sums, 1), axis=0).astype(BF16)
        for copy in write_back(owner, slot):
            copy.start()

    for owner in (groups - 2, groups - 1):
        for copy in write_back(owner, owner % 2):
            copy.wait()


def query_outputs(source, incoming, later, features, inner, taps):
    rows, width = source.shape
    groups, _, chans = inner.shape
    return pl.pallas_call(
        output_kernel,
        out_shape=(
            pltpu.HBM((rows, width), BF16),
            pltpu.HBM((rows, 3 * width), BF16),
            jax.ShapeDtypeStruct((groups, HALO, chans), BF16),
        ),
        in_specs=[pl.BlockSpec(memory_space=pltpu.VMEM)] * 6,
        out_specs=(
            pl.BlockSpec(memory_space=pl.ANY),
            pl.BlockSpec(memory_space=pl.ANY),
            pl.BlockSpec(memory_space=pltpu.VMEM),
        ),
        scratch_shapes=[
            pltpu.VMEM((chans // 128, rows + HALO, 128), F32),
            pltpu.VMEM((1, TAPS, 8, chans), F32),
            pltpu.VMEM((2, 2, rows, chans), BF16),
            pltpu.SemaphoreType.DMA((2, 2)),
        ],
        compiler_params=pltpu.CompilerParams(vmem_limit_bytes=12 * MIB),
        cost_estimate=pl.CostEstimate(flops=35 * rows * width, bytes_accessed=14 * rows * width, transcendentals=0),
        name="query_outputs",
    )(source, incoming, later, features, inner, taps)


def through_kernel(groups, me_ref, *refs):
    pieces = refs[: groups // 2]
    (
        grad_hbm, feats_hbm, spec_hbm, table_hbm, back_hbm, taps_ref, gain_ref,
        ready_hbm, ring_hbm, sums_ref,
        source, mix_grad, feats, spec, ring, table, back, rings, products, joined, through,
        grads, sums, slots,
        piece_sems, signal_sem, feats_sems, load_sems, ring_sems, slot_sems,
    ) = refs[groups // 2 :]
    _, rows, chans = through.shape
    signal = pltpu.make_async_copy(grad_hbm, mix_grad, signal_sem.at[0])
    signal.start()
    kinds = ((table_hbm, table), (spec_hbm, spec), (back_hbm, back))
    for index in range(8):
        for kind, (from_ref, into) in enumerate(kinds):
            pltpu.make_async_copy(from_ref.at[index], into.at[index], load_sems.at[kind, index]).start()
    for partner in range(groups):
        block = me_ref[0] ^ partner
        piece = pieces[partner // 2].at[partner % 2]
        pltpu.make_async_copy(piece, source.at[block], piece_sems.at[block]).start()

    def feats_copy(block):
        return pltpu.make_async_copy(feats_hbm.at[block], feats.at[block], feats_sems.at[block])

    for block in range(groups):
        feats_copy(block).start()
    grads[:, :, 0:HALO, :] = jnp.zeros((2, chans // 128, HALO, 128), F32)
    sums[...] = jnp.zeros_like(sums)
    signal.wait()
    split_signal(mix_grad, rings)
    leaf = spec.shape[1] // 2

    def ring_copy(index):
        return pltpu.make_async_copy(ring.at[index], ring_hbm.at[index], ring_sems.at[index])

    @pl.loop(0, 8)
    def _(index):
        for kind, (from_ref, into) in enumerate(kinds):
            pltpu.make_async_copy(from_ref.at[index], into.at[index], load_sems.at[kind, index]).wait()
        ring[index] = jnp.dot(table[index], rings[index], preferred_element_type=F32)
        d_real, d_imag = ring[index, :leaf], ring[index, leaf:]
        f_real, f_imag = spec[index, :leaf], spec[index, leaf:]
        products[:leaf] = (d_real * f_real + d_imag * f_imag).astype(BF16)
        products[leaf:] = (d_imag * f_real - d_real * f_imag).astype(BF16)
        joined[index] = jnp.dot(back[index], products[...], preferred_element_type=F32)
        ring_copy(index).start()

    def place_through(owner, strip, inside, lanes, result):
        grad = mix_grad[owner, inside, lanes].astype(F32)
        through[owner, inside, lanes] = (result + gain_ref[0:1, lanes] * grad).astype(BF16)

    join_signal(joined, 0, rows, place_through)

    @pl.loop(0, groups)
    def _(block):
        pltpu.make_async_copy(pieces[0].at[0], source.at[block], piece_sems.at[block]).wait()
        feats_copy(block).wait()

    def write_back(slot_at, block_at):
        return pltpu.make_async_copy(
            slots.at[slot_at], ready_hbm.at[block_at, pl.ds(0, 2 * rows)], slot_sems.at[slot_at]
        )

    @pl.loop(0, groups)
    def _(step):
        block = groups - 1 - step
        slot = lax.rem(step, 2)

        @pl.when(step >= 2)
        def _():
            write_back(slot, block + 2).wait()

        for part in range(chans // 128):
            lanes = slice(part * 128, part * 128 + 128)
            for role in range(2):
                grads[role, part, rows : rows + HALO, :] = grads[role, part, 0:HALO, :]
            for row in range(0, rows, 16):
                span = slice(row, row + 16)
                values = through[block, span, lanes].astype(F32)
                grads[0, part, span, :] = values * feats[block, 1, span, lanes]
                grads[1, part, span, :] = values * feats[block, 0, span, lanes]
            for role in range(2):

                def place(row, values, role=role, lanes=lanes):
                    slots[slot, role * rows + row : role * rows + row + 16, lanes] = values

                def source_block(row, role=role, lanes=lanes):
                    return source[block, role, row : row + 16, lanes]

                taps = tap_rows(taps_ref, role + 1, lanes)
                back_taps(grads.at[role], source_block, part, taps, place, sums, role, lanes)
        write_back(slot, block).start()

    sums_ref[...] = jnp.concatenate(sum_rows(sums, 2), axis=0)
    write_back(groups % 2, 1).wait()
    write_back((groups + 1) % 2, 0).wait()

    @pl.loop(0, 8)
    def _(index):
        ring_copy(index).wait()


def through_work(me, pieces, mix_grad, feats, spectrum, table, back, taps, gain):
    groups, rows, chans = mix_grad.shape
    length = groups * rows
    wide = length // 4
    parts = chans // 128
    return pl.pallas_call(
        functools.partial(through_kernel, groups),
        out_shape=(
            pltpu.HBM((groups, 2 * rows + EXTRA, chans), BF16),
            pltpu.HBM((8, wide, chans), F32),
            jax.ShapeDtypeStruct((2 * HALO, chans), F32),
        ),
        in_specs=[pl.BlockSpec(memory_space=pltpu.SMEM)]
        + [pl.BlockSpec(memory_space=pl.ANY)] * (groups // 2 + 5)
        + [pl.BlockSpec(memory_space=pltpu.VMEM)] * 2,
        out_specs=(pl.BlockSpec(memory_space=pl.ANY),) * 2 + (pl.BlockSpec(memory_space=pltpu.VMEM),),
        scratch_shapes=[
            pltpu.VMEM((groups, 2, rows, chans), BF16),
            pltpu.VMEM((groups, rows, chans), BF16),
            pltpu.VMEM((groups, 2, rows, chans), F32),
            pltpu.VMEM((8, wide, chans), F32),
            pltpu.VMEM((8, wide, chans), F32),
            pltpu.VMEM((8, wide, wide), BF16),
            pltpu.VMEM((8, wide, wide), BF16),
            pltpu.VMEM((8, wide, chans), BF16),
            pltpu.VMEM((wide, chans), BF16),
            pltpu.VMEM((8, wide, chans), F32),
            pltpu.VMEM((groups, rows, chans), BF16),
            pltpu.VMEM((2, parts, rows + HALO, 128), F32),
            pltpu.VMEM((2, TAPS, 8, chans), F32),
            pltpu.VMEM((2, 2 * rows, chans), BF16),
            pltpu.SemaphoreType.DMA((groups,)),
            pltpu.SemaphoreType.DMA((1,)),
            pltpu.SemaphoreType.DMA((groups,)),
            pltpu.SemaphoreType.DMA((3, 8)),
            pltpu.SemaphoreType.DMA((8,)),
            pltpu.SemaphoreType.DMA((2,)),
        ],
        compiler_params=pltpu.CompilerParams(vmem_limit_bytes=34 * MIB),
        cost_estimate=pl.CostEstimate(
            flops=32 * wide * wide * chans + 100 * length * chans, bytes_accessed=28 * MIB, transcendentals=0
        ),
        name="through_values",
    )(me, *in_hbm(*pieces), mix_grad, *in_hbm(feats, spectrum, table, back), taps, gain)


def filter_grad_kernel(
    grad_hbm, gated_hbm, d_hbm, g_hbm, back_hbm, filt_hbm, skip_ref,
    mix_grad, gated, d_ring, g_ring, back, products, joined, flat, turned_flat, signal_sems, load_sems, filt_sem,
):
    groups, rows, chans = mix_grad.shape
    signals = [
        pltpu.make_async_copy(grad_hbm, mix_grad, signal_sems.at[0]),
        pltpu.make_async_copy(gated_hbm, gated, signal_sems.at[1]),
    ]
    kinds = ((d_hbm, d_ring), (g_hbm, g_ring), (back_hbm, back))
    for index in range(8):
        for kind, (from_ref, into) in enumerate(kinds):
            pltpu.make_async_copy(from_ref.at[index], into.at[index], load_sems.at[kind, index]).start()
    for copy in signals:
        copy.start()
    leaf = d_ring.shape[1] // 2

    @pl.loop(0, 8)
    def _(index):
        for kind, (from_ref, into) in enumerate(kinds):
            pltpu.make_async_copy(from_ref.at[index], into.at[index], load_sems.at[kind, index]).wait()
        d_real, d_imag = d_ring[index, :leaf], d_ring[index, leaf:]
        g_real, g_imag = g_ring[index, :leaf], g_ring[index, leaf:]
        products[:leaf] = (d_real * g_real + d_imag * g_imag).astype(BF16)
        products[leaf:] = (d_imag * g_real - d_real * g_imag).astype(BF16)
        joined[index] = jnp.dot(back[index], products[...], preferred_element_type=F32)

    for copy in signals:
        copy.wait()
    skip_ref[...] = jnp.zeros_like(skip_ref)

    @pl.loop(0, groups)
    def _(block):
        for lane in range(0, chans, 128):
            lanes = slice(lane, lane + 128)
            total = jnp.zeros((16, 128), F32)
            for row in range(0, rows, 16):
                span = slice(row, row + 16)
                total = total + mix_grad[block, span, lanes].astype(F32) * gated[block, span, lanes].astype(F32)
            skip_ref[0:1, lanes] += jnp.sum(total, axis=0, keepdims=True)

    def place_filter(owner, strip, inside, lanes, result):
        flat[pl.ds(pl.multiple_of(owner * rows + strip * 16, 16), 16), lanes] = result

    join_signal(joined, 0, rows, place_filter)
    for block in range(groups):
        span = slice(block * rows, (block + 1) * rows)
        turned_flat[:, span] = flat[span, :].T
    wait_all([pltpu.make_async_copy(turned_flat, filt_hbm, filt_sem.at[0])])


def filter_gradient(mix_grad, gated, d_ring, g_ring, back):
    groups, rows, chans = mix_grad.shape
    length = groups * rows
    wide = length // 4
    return pl.pallas_call(
        filter_grad_kernel,
        out_shape=(pltpu.HBM((chans, length), F32), jax.ShapeDtypeStruct((1, chans), F32)),
        in_specs=[pl.BlockSpec(memory_space=pl.ANY)] * 5,
        out_specs=(pl.BlockSpec(memory_space=pl.ANY), pl.BlockSpec(memory_space=pltpu.VMEM)),
        scratch_shapes=[
            pltpu.VMEM((groups, rows, chans), BF16),
            pltpu.VMEM((groups, rows, chans), BF16),
            pltpu.VMEM((8, wide, chans), F32),
            pltpu.VMEM((8, wide, chans), F32),
            pltpu.VMEM((8, wide, wide), BF16),
            pltpu.VMEM((wide, chans), BF16),
            pltpu.VMEM((8, wide, chans), F32),
            pltpu.VMEM((length, chans), F32),
            pltpu.VMEM((chans, length), F32),
            pltpu.SemaphoreType.DMA((2,)),
            pltpu.SemaphoreType.DMA((3, 8)),
            pltpu.SemaphoreType.DMA((1,)),
        ],
        compiler_params=pltpu.CompilerParams(vmem_limit_bytes=28 * MIB),
        cost_estimate=pl.CostEstimate(
            flops=16 * wide * wide * chans + 40 * length * chans, bytes_accessed=16 * MIB, transcendentals=0
        ),
        name="filter_gradient",
    )(mix_grad, *in_hbm(gated, d_ring, g_ring, back))


def place_kernel(columns, held_ref, *refs):
    *wide_refs, sems = refs
    groups, _, chans = held_ref.shape
    rows = wide_refs[-1].shape[0]
    wide_refs = wide_refs[-1 - max(index for index, _ in columns) :]
    copies = []
    for owner in range(groups):
        for kind, (index, first) in enumerate(columns):
            copies.append(
                pltpu.make_async_copy(
                    held_ref.at[owner, pl.ds(kind * rows, rows)],
                    wide_refs[index].at[:, pl.ds(first * groups * chans + owner * chans, chans)],
                    sems.at[owner, kind],
                )
            )
    wait_all(copies)


def place_columns(held, rows, columns, earlier):
    groups, _, chans = held.shape
    width = groups * chans
    shapes = [(rows, 3 * width)]
    return pl.pallas_call(
        functools.partial(place_kernel, columns),
        input_output_aliases={1: 0} if earlier else {},
        out_shape=[pltpu.HBM(shape, BF16) for shape in shapes],
        in_specs=[pl.BlockSpec(memory_space=pltpu.VMEM)] + [pl.BlockSpec(memory_space=pl.ANY)] * len(earlier),
        out_specs=[pl.BlockSpec(memory_space=pl.ANY)] * len(shapes),
        scratch_shapes=[pltpu.SemaphoreType.DMA((groups, 2))],
        compiler_params=pltpu.CompilerParams(vmem_limit_bytes=6 * MIB),
        cost_estimate=pl.CostEstimate(flops=0, bytes_accessed=8 * rows * width, transcendentals=0),
        name="place_columns",
    )(held, *in_hbm(*earlier))


def edge_of(block, steps):
    sections, groups = lax.axis_size("section"), lax.axis_size("ctx")
    pairs = [
        (section * groups + place, (section + steps) % sections * groups + place + steps)
        for section in range(sections)
        for place in range(groups)
        if 0 <= place + steps < groups
    ]
    return lax.ppermute(block, ("section", "ctx"), pairs)


def on_device(acts, cots, kern, filt, skip):
    rows, feats_all = acts.shape[1:]
    groups = lax.axis_size("ctx")
    chans = filt.shape[1]
    width = groups * chans
    place = lax.axis_index("ctx").astype(jnp.int32)
    me = place[None]

    table, back = (jnp.asarray(one) for one in leaf_tables(rows * groups))
    spectrum = filter_spectrum(filt[0], table)
    gain = lax.dynamic_slice_in_dim(skip, place * chans, chans, axis=1)
    came = handed_over(leaving_pieces(me, acts[0], groups, 2), 0, 1)
    query, *pieces = pieces_for_owners(me, acts[0], came, groups)
    pieces = [handed_over(piece, 1, 2 * chip) for chip, piece in enumerate(pieces)]
    incoming = cots[0]
    kern, pieces[0] = lax.optimization_barrier((kern, pieces[0]))
    taps = kern[0].reshape(TAPS, 3, groups, chans)
    taps = lax.dynamic_index_in_dim(taps, place, axis=2, keepdims=False).transpose(1, 0, 2)
    taps = jnp.pad(taps, ((0, 0), (0, HALO - TAPS), (0, 0)))
    query_taps = jnp.pad(kern[0, :, :width], ((0, HALO - TAPS), (0, 0)))
    query, incoming, pieces[:LATE] = lax.optimization_barrier((query, incoming, pieces[:LATE]))
    query = passed_along(query, "section", 1)
    incoming = passed_along(incoming, "section", -1)

    feats, gated, inner, g_ring = inner_work(me, pieces, spectrum, table, back, taps, gain)
    inner = lax.all_to_all(inner, "ctx", split_axis=0, concat_axis=0, tiled=True)

    before = edge_of(acts[0, rows - HALO :, :width], 1)
    later = edge_of(cots[0, :HALO], -1)
    before, later = lax.optimization_barrier((before, later))
    mix_grad, features = query_features(query, before, incoming, query_taps, groups)
    mix_grad = lax.all_to_all(mix_grad, "ctx", split_axis=0, concat_axis=0, tiled=True)
    output, input_grad, partial = query_outputs(query, incoming, later, features, inner, query_taps)
    partial, mix_grad = lax.optimization_barrier((partial, mix_grad))
    partial = lax.all_to_all(partial, "ctx", split_axis=0, concat_axis=0, tiled=True)
    query_sums = jnp.sum(partial.astype(F32), axis=0)

    ready, d_ring, value_sums = through_work(me, pieces, mix_grad, feats, spectrum, table, back, taps, gain)
    tap_sums = jnp.concatenate([query_sums, value_sums], axis=0).astype(BF16)
    tap_sums = jnp.broadcast_to(tap_sums, (groups, EXTRA, chans))
    ready = lax.dynamic_update_slice(ready, tap_sums, (0, 2 * rows, 0))
    ready = lax.all_to_all(ready, "ctx", split_axis=0, concat_axis=0, tiled=True)
    filt_grad, skip_grad = filter_gradient(mix_grad, gated, d_ring, g_ring, back)
    (input_grad,) = place_columns(ready, rows, ((0, 1), (0, 2)), (input_grad,))
    sums = ready[:, 2 * rows : 2 * rows + 3 * HALO].reshape(groups, 3, HALO, chans)[:, :, :TAPS]
    kern_grad = sums.transpose(2, 1, 0, 3).reshape(TAPS, feats_all).astype(F32)
    return (output[None], input_grad[None], kern_grad[None], filt_grad[None], skip_grad)


def solution(mesh):
    return jax.shard_map(
        on_device,
        mesh=mesh,
        in_specs=(
            P("section", "ctx", None),
            P("section", "ctx", None),
            P("section", None, None),
            P("section", "ctx", None),
            P("section", None),
        ),
        out_specs=(
            P("section", "ctx", None),
            P("section", "ctx", None),
            P("section", None, None),
            P("section", "ctx", None),
            P("section", "ctx"),
        ),
        check_vma=False,
    )
```
